32 devices in a mesh: groups: 2 (over y), section: 8 (over z, x), sub: 2 (over core).
Axes of the slice: x: 2, y: 2, z: 4, core: 2. Of those that a mesh axis runs over, the one named last changes fastest.
Arguments:
- echoes: float32 [4, 384, 32, 256], P('groups', None, 'section', 'sub'), parts along dimension 0, may hold values from -6 to 6
- range_taps: float32 [2, 5], replicated, may hold values from -3 to 3
- pulse_taper: float32 [256], replicated, may hold values from 0.3 to 1
- channel_phase: float32 [256], replicated, may hold values from -3.140625 to 3.140625
- loading: float32 [1], replicated, may hold values from 0.5 to 2
- beam_index: int32 [256], replicated, may hold values from 0 to 1023
Outputs:
- normalized_beams: float32 [2, 256, 32, 256], P('groups', ('section', 'sub')), parts along dimension 0
The draws below stay inside these ranges and needn't reach their ends.
There are 2 independent parts, one for each index of `groups`. The reference program is written for one: setup_inputs(seed, part) draws one part's arguments, and reference() takes and returns one part's arrays. A program takes and returns all parts, laid end to end along the dimension named above; an argument that names none is the same for every part. Nothing has to cross between parts.
All inputs are finite; a program needn't handle non-finite values. Where the reference program divides by a largest or mean magnitude, that divisor is 1e-20 or more.
Results may differ from the reference program's by a relative error of at most 0.0003.
Values sent between devices are 32-bit elements; how exact they have to be, the bound alone decides.
No kernel may reach another device: no remote copies, remote signals or barrier semaphores. Data moves between devices by JAX's collectives and lax.ppermute only.
A program may use at most 64 MiB of HBM per device.

```python
import math
import jax
import jax.numpy as jnp
from jax import lax

CHANNELS = 256
PULSES = 256
BEAMS = 256
INTERVALS = 2
ITERS = 2
LOOKS = 1024
HALF = 2
GATES = 32
HOP = 128
TRAIN = 384


def plant(entries, rng, least, high):
    shape = entries.shape
    place = [jax.random.randint(jax.random.fold_in(rng, axis), (), 0, shape[axis]) for axis in range(len(shape))]
    entries = entries.at[tuple(place)].set(least)
    longest = shape.index(max(shape))
    place[longest] = (place[longest] + 1) % shape[longest]
    return entries.at[tuple(place)].set(high)


def block_levels(stream_key, shape, split, low, largest):
    loudness, own = 1.0, jax.random.fold_in(stream_key, 6)
    for position, parts in split:
        steps = jnp.exp(jax.random.uniform(jax.random.fold_in(own, position), (parts,), jnp.float32, low / len(split), largest / len(split)))
        loudness = loudness * jnp.repeat(steps, shape[position] // parts).reshape([-1 if axis == position else 1 for axis in range(len(shape))])
    return loudness


def noise(stream_key, dims, width, reach, shards=(), kind=jnp.bfloat16):
    drawn = jax.random.normal(stream_key, dims, jnp.float32) * width
    if len(shards) > 0:
        drawn = block_levels(stream_key, dims, shards, -0.22, 0.18) * drawn
    return jnp.clip(drawn, min=-reach, max=reach).astype(kind)


def setup_inputs(seed: int = 0, part: int = 0) -> dict:
    keys = jax.random.split(jax.random.key(seed), 7)
    own_keys = jax.random.split(jax.random.fold_in(keys[6], part), 7)
    return {
        "echoes": noise(own_keys[0], (2, TRAIN, GATES, CHANNELS), 1.0, 6.0, ((2, 8), (3, 2)), jnp.float32),
        "range_taps": noise(keys[1], (2, 2 * HALF + 1), 0.5, 3.0, (), jnp.float32),
        "pulse_taper": jnp.clip(jnp.exp(jax.random.uniform(keys[2], (PULSES,), jnp.float32, math.log(0.3), math.log(1.0))), 0.3, 1.0),
        "channel_phase": jnp.clip(jax.random.uniform(keys[3], (CHANNELS,), jnp.float32, -3.140625, 3.140625), -3.140625, 3.140625),
        "loading": jnp.clip(jnp.exp(jax.random.uniform(keys[4], (1,), jnp.float32, math.log(0.5), math.log(2.0))), 0.5, 2.0),
        "beam_index": plant(jax.random.randint(keys[5], (BEAMS,), 0, LOOKS), jax.random.fold_in(keys[5], 1), 0, LOOKS - 1).astype(jnp.int32),
    }


precise = lax.Precision.HIGHEST
epsilon = 1e-6


def apply_taps(pad_real, pad_imag, range_taps, gate_count):
    axis_gates = pad_real.ndim - 2
    shape_out = pad_real.shape[:axis_gates] + (gate_count,) + pad_real.shape[axis_gates + 1:]
    out_real = jnp.zeros(shape_out, jnp.float32)
    out_imag = jnp.zeros(shape_out, jnp.float32)
    for offset in range(range_taps.shape[1]):
        part_real = lax.slice_in_dim(pad_real, offset, offset + gate_count, axis=axis_gates)
        part_imag = lax.slice_in_dim(pad_imag, offset, offset + gate_count, axis=axis_gates)
        out_real = out_real + range_taps[0, offset] * part_real - range_taps[1, offset] * part_imag
        out_imag = out_imag + range_taps[0, offset] * part_imag + range_taps[1, offset] * part_real
    return out_real, out_imag


def doppler_table(pulse_taper):
    pulse_count = pulse_taper.shape[0]
    pulse_index = jnp.arange(pulse_count, dtype=jnp.int32)
    product = (pulse_index[:, None] * pulse_index[None, :]) % pulse_count
    phase_angle = (2.0 * math.pi / pulse_count) * product.astype(jnp.float32)
    cosine = jnp.cos(phase_angle) * pulse_taper[None, :]
    sine_part = jnp.sin(phase_angle) * pulse_taper[None, :]
    upper_rows = jnp.concatenate([cosine, sine_part], axis=1)
    lower_rows = jnp.concatenate([-sine_part, cosine], axis=1)
    return jnp.concatenate([upper_rows, lower_rows], axis=0)


def transform(doppler, segment):
    shape_in = segment.shape
    flattened = segment.reshape(shape_in[0] * shape_in[1], -1)
    result = jnp.dot(doppler, flattened, precision=precise, preferred_element_type=jnp.float32)
    return result.reshape(shape_in)


def batched(first, second):
    return jnp.einsum('dij,djk->dik', first, second, precision=precise)


def complex_product(left_real, left_imag, right_real, right_imag):
    out_real = batched(left_real, right_real) - batched(left_imag, right_imag)
    out_imag = batched(left_real, right_imag) + batched(left_imag, right_real)
    return out_real, out_imag


def gram_product(first, second):
    return jnp.einsum('dgi,dgj->dij', first, second, precision=precise)


def loaded_inverse(real_part, imag_part, loading):
    gate_count = real_part.shape[1]
    channels = real_part.shape[2]
    cov_real = (gram_product(real_part, real_part) + gram_product(imag_part, imag_part)) / gate_count
    cov_imag = (gram_product(real_part, imag_part) - gram_product(imag_part, real_part)) / gate_count
    identity = jnp.eye(channels, dtype=jnp.float32)
    trace_sum = jnp.sum(cov_real * identity[None], axis=(1, 2))
    cov_real = cov_real + (loading[0] * trace_sum / channels)[:, None, None] * identity[None]
    row_bound = jnp.max(jnp.sum(jnp.abs(cov_real) + jnp.abs(cov_imag), axis=2), axis=1)
    inv_real = identity[None] / row_bound[:, None, None]
    inv_imag = jnp.zeros_like(inv_real)
    for newton_step in range(ITERS):
        prod_real, prod_imag = complex_product(cov_real, cov_imag, inv_real, inv_imag)
        inv_real, inv_imag = complex_product(inv_real, inv_imag, 2.0 * identity[None] - prod_real, -prod_imag)
    return inv_real, inv_imag


def steering(beam_index, channel_phase):
    channels = channel_phase.shape[0]
    direction = -1.0 + (2.0 * beam_index.astype(jnp.float32) + 1.0) / LOOKS
    phase_angle = math.pi * jnp.arange(channels, dtype=jnp.float32)[:, None] * direction[None, :] + channel_phase[:, None]
    return jnp.cos(phase_angle), jnp.sin(phase_angle)


def beam_weights(inv_real, inv_imag, steer_real, steer_imag):
    weight_real = jnp.einsum('dij,jb->dib', inv_real, steer_real, precision=precise) - jnp.einsum('dij,jb->dib', inv_imag, steer_imag, precision=precise)
    weight_imag = jnp.einsum('dij,jb->dib', inv_real, steer_imag, precision=precise) + jnp.einsum('dij,jb->dib', inv_imag, steer_real, precision=precise)
    gain_norm = jnp.sum(steer_real[None] * weight_real + steer_imag[None] * weight_imag, axis=1)
    return weight_real / gain_norm[:, None, :], weight_imag / gain_norm[:, None, :]


def form_beams(data_real, data_imag, weight_real, weight_imag):
    out_real = jnp.einsum('dgc,dcb->dgb', data_real, weight_real, precision=precise) + jnp.einsum('dgc,dcb->dgb', data_imag, weight_imag, precision=precise)
    out_imag = jnp.einsum('dgc,dcb->dgb', data_imag, weight_real, precision=precise) - jnp.einsum('dgc,dcb->dgb', data_real, weight_imag, precision=precise)
    return out_real * out_real + out_imag * out_imag


def reference(echoes, range_taps, pulse_taper, channel_phase, loading, beam_index):
    rim_width = range_taps.shape[1] // 2
    padded = jnp.pad(echoes, ((0, 0), (0, 0), (rim_width, rim_width), (0, 0)))
    filt_real, filt_imag = apply_taps(padded[0], padded[1], range_taps, echoes.shape[2])
    filtered = jnp.stack([filt_real, filt_imag])
    doppler = doppler_table(pulse_taper)
    spectra = [transform(doppler, lax.slice_in_dim(filtered, interval * HOP, interval * HOP + PULSES, axis=1)) for interval in range(INTERVALS)]
    steer_real, steer_imag = steering(beam_index, channel_phase)
    outputs = []
    for interval in range(INTERVALS - 1):
        inv_real, inv_imag = loaded_inverse(spectra[interval][0], spectra[interval][1], loading)
        weight_real, weight_imag = beam_weights(inv_real, inv_imag, steer_real, steer_imag)
        beam_power = form_beams(spectra[interval + 1][0], spectra[interval + 1][1], weight_real, weight_imag)
        noise_level = jnp.sum(beam_power, axis=(0, 1)) / (PULSES * GATES)
        outputs.append(beam_power / (noise_level + epsilon))
    return jnp.stack(outputs)
```

```python
import math

import jax
import jax.numpy as jnp
import numpy as np
from jax import lax
from jax.experimental import pallas as pl
from jax.experimental.pallas import tpu as pltpu
from jax.sharding import PartitionSpec as P

PULSES = 256
INTERVALS = 2
ITERS = 2
LOOKS = 1024
HOP = 128


precise = lax.Precision.HIGHEST
epsilon = 1e-06
F32 = jnp.float32
BF16 = jnp.bfloat16
LANES = 128
VMEM = pl.BlockSpec(memory_space=pltpu.VMEM)
SMEM = pl.BlockSpec(memory_space=pltpu.SMEM)
LIMIT = 56 << 20


def split(value):
    high = value.astype(BF16)
    return high, (value - high.astype(F32)).astype(BF16)


def dot(left, right):
    return jnp.dot(left, right, preferred_element_type=F32)


def dot_nt(left, right):
    return lax.dot_general(left, right, (((1,), (1,)), ((), ())), preferred_element_type=F32)


def dot_tn(left, right):
    return lax.dot_general(left, right, (((0,), (0,)), ((), ())), preferred_element_type=F32)


def triple(product, left, right):
    return product(left[0], right[0]) + (product(left[0], right[1]) + product(left[1], right[0]))


def doppler_tables(pulses):
    half = pulses // 2
    bins = np.arange(half)[:, None]
    tables = []
    for parity in (0, 1):
        phase = 2.0 * np.pi * ((bins * np.arange(parity, pulses, 2)[None, :]) % pulses) / pulses
        cosine, sine = np.cos(phase), np.sin(phase)
        table = np.concatenate(
            [np.concatenate([cosine, sine], 1), np.concatenate([-sine, cosine], 1)], 0
        ).astype(np.float32)
        high = table.astype(jnp.bfloat16)
        tables += [high, (table - high.astype(np.float32)).astype(jnp.bfloat16)]
    return np.stack(tables)


def doppler_body(gates, hop, first_ref, second_ref, taper_ref, table_ref, result, tapers):
    half = hop
    for segment in (0, 1):
        row = taper_ref[segment : segment + 1, :]
        tapers[segment * hop : (segment + 1) * hop, :] = jnp.broadcast_to(row, (hop, hop)).T
    for gate in range(gates):
        for parity in (0, 1):
            rows = []
            for part in (0, 1):
                for ref, segment in ((first_ref, 0), (second_ref, 1)):
                    block = ref[part, 0, pl.ds(parity * gates + gate, hop // 2, stride=2 * gates), :]
                    taper = tapers[pl.ds(segment * hop + parity, hop // 2, stride=2), :]
                    rows.append(block * taper)
            data = split(jnp.concatenate(rows, axis=0))
            table = (table_ref[2 * parity], table_ref[2 * parity + 1])
            value = triple(dot, table, data)
            if parity == 0:
                even = value
            else:
                for part in (0, 1):
                    own = slice(part * half, (part + 1) * half)
                    result[part, gate, :half] = even[own] + value[own]
                    result[part, gate, half:] = even[own] - value[own]


def doppler(view, taper, sections, interval, split_sub):
    gates = view.shape[2] // HOP
    per = PULSES // sections
    own = per // 2

    def body(first_ref, second_ref, taper_ref, table_ref, *rest):
        out_refs, result, tapers = rest[:-2], rest[-2], rest[-1]
        doppler_body(gates, HOP, first_ref, second_ref, taper_ref, table_ref, result, tapers)
        section = lax.axis_index("section")
        if not split_sub:
            for step in range(sections):
                start = pl.multiple_of(jnp.bitwise_xor(section, step) * per, per)
                out_refs[step][...] = result[:, :, pl.ds(start, per), :]
        else:
            sub = lax.axis_index("sub")
            for step in range(sections):
                start = jnp.bitwise_xor(section, step) * per
                mine = pl.multiple_of(start + sub * own, own)
                theirs = pl.multiple_of(start + (1 - sub) * own, own)
                out_refs[0][step] = result[:, :, pl.ds(mine, own), :]
                out_refs[1][step] = result[:, :, pl.ds(theirs, own), :]

    block = lambda place: pl.BlockSpec((2, 1, HOP * gates, LANES), lambda i: (0, place, 0, 0))
    whole = lambda shape: pl.BlockSpec(shape, lambda i: (0,) * len(shape))
    tables = jnp.asarray(doppler_tables(PULSES))
    if split_sub:
        shape = (sections, 2, gates, own, LANES)
        outs = [jax.ShapeDtypeStruct(shape, F32)] * 2
    else:
        shape = (2, gates, per, LANES)
        outs = [jax.ShapeDtypeStruct(shape, F32)] * sections
    return pl.pallas_call(
        body,
        grid=(1,),
        in_specs=[block(interval), block(interval + 1), whole(taper.shape), whole(tables.shape)],
        out_specs=[whole(shape)] * len(outs),
        out_shape=outs,
        scratch_shapes=[
            pltpu.VMEM((2, gates, PULSES, LANES), F32),
            pltpu.VMEM((PULSES, LANES), F32),
        ],
        compiler_params=pltpu.CompilerParams(vmem_limit_bytes=LIMIT),
        name=f"doppler{interval}",
    )(view, view, taper, tables)


def gather_sub(blocks):
    sections = len(blocks)
    _, gates, per, _ = blocks[0].shape
    own = per // 2

    def body(*refs):
        section, sub = lax.axis_index("section"), lax.axis_index("sub")
        mine = pl.multiple_of(sub * own, own)
        theirs = pl.multiple_of((1 - sub) * own, own)
        for step in range(sections):
            source = jnp.bitwise_xor(section, step)
            refs[sections][source] = refs[step][:, :, pl.ds(mine, own), :]
            refs[sections + 1][source] = refs[step][:, :, pl.ds(theirs, own), :]

    shape = jax.ShapeDtypeStruct((sections, 2, gates, own, LANES), F32)
    return pl.pallas_call(
        body,
        in_specs=[VMEM] * sections,
        out_specs=[VMEM] * 2,
        out_shape=[shape] * 2,
        compiler_params=pltpu.CompilerParams(vmem_limit_bytes=LIMIT),
        name="gather_sub",
    )(*blocks)


def pair_up(mine, other):
    sections = mine.shape[0]

    def body(mine_ref, other_ref, *out_refs):
        for step in range(sections):
            out_refs[step][0] = mine_ref[step]
            out_refs[step][1] = other_ref[step]

    shape = jax.ShapeDtypeStruct((2,) + mine.shape[1:], F32)
    return pl.pallas_call(
        body,
        in_specs=[VMEM] * 2,
        out_specs=[VMEM] * sections,
        out_shape=[shape] * sections,
        compiler_params=pltpu.CompilerParams(vmem_limit_bytes=LIMIT),
        name="pair_up",
    )(mine, other)


def shifted(value, amount):
    sections = value.shape[0]
    rolled = pltpu.roll(value, amount % sections, 0)
    row = lax.broadcasted_iota(jnp.int32, value.shape, 0)
    keep = row >= amount if amount > 0 else row < sections + amount
    return jnp.where(keep, rolled, 0.0)


def filtered_bin(load, gates, taps_ref):
    taps = taps_ref.shape[1]
    rim = taps // 2
    data = {}
    for part in (0, 1):
        for gate in range(gates):
            data[part, gate] = load(part, gate)
    for part in (0, 1):
        for gate in range(-rim, 0):
            data[part, gate] = shifted(data[part, gate + gates], 1)
        for gate in range(gates, gates + rim):
            data[part, gate] = shifted(data[part, gate - gates], -1)
    real, imag = [], []
    for gate in range(gates):
        sum_real, sum_imag = None, None
        for tap in range(taps):
            tap_real, tap_imag = taps_ref[0, tap], taps_ref[1, tap]
            in_real, in_imag = data[0, gate + tap - rim], data[1, gate + tap - rim]
            add_real = tap_real * in_real - tap_imag * in_imag
            add_imag = tap_real * in_imag + tap_imag * in_real
            sum_real = add_real if sum_real is None else sum_real + add_real
            sum_imag = add_imag if sum_imag is None else sum_imag + add_imag
        real.append(sum_real)
        imag.append(sum_imag)
    return jnp.concatenate(real, axis=0), jnp.concatenate(imag, axis=0)


def stacked_rows(high_low, rows, channels):
    real, imag = high_low[:, :channels], high_low[:, channels:]
    return jnp.concatenate(
        [jnp.concatenate([real, -imag], axis=1), jnp.concatenate([imag, real], axis=1)], axis=0
    )


def weights_kernel(mine, other, steer_high, steer_low, range_taps, loading):
    sections, _, gates, own, _ = mine.shape
    count = sections * gates
    channels = 2 * LANES
    beams = steer_high.shape[1] // 2
    stride = 2 * gates * own
    mine = mine.reshape(sections * stride, LANES)
    other = other.reshape(sections * stride, LANES)

    def body(mine_ref, other_ref, sh_ref, sl_ref, taps_ref, load_ref,
             yh_ref, yl_ref, th_ref, tl_ref, scale_ref, gain_ref,
             quad_ref, u_ref):
        def one_bin(index, carry):
            def load(part, gate):
                at = pl.ds((part * gates + gate) * own + index, sections, stride=stride)
                return jnp.concatenate([mine_ref[at, :], other_ref[at, :]], axis=1)

            real, imag = filtered_bin(load, gates, taps_ref)
            both = jnp.concatenate([real, imag], axis=1)
            high, low = split(both)
            base = pl.multiple_of(index * count, count)
            yh_ref[pl.ds(base, count), :] = high
            yl_ref[pl.ds(base, count), :] = low
            up = lambda v: jnp.concatenate([v[:, :channels], v[:, channels:]], axis=0)
            turn = lambda v: jnp.concatenate(
                [up(v), jnp.concatenate([v[:, channels:], -v[:, :channels]], axis=0)], axis=1
            )
            lh, ll = up(high), up(low)
            rh, rl = turn(high), turn(low)
            left = jnp.concatenate([lh, lh, ll], axis=0)
            right = jnp.concatenate([rh, rl, rh], axis=0)
            cov = jnp.abs(dot_tn(left, right))
            sums = jnp.sum(cov[:, :channels] + cov[:, channels:], axis=0, keepdims=True)
            bound = jnp.max(sums, axis=1, keepdims=True) / count
            trace = jnp.sum(jnp.sum(both * both, axis=0, keepdims=True), axis=1, keepdims=True) / count
            delta = load_ref[0] * trace / channels
            bound = bound + delta
            ratio = 1.0 - delta / bound
            first = 1.0 + ratio * (1.0 + ratio * (1.0 + ratio))
            second = 1.0 + ratio * (2.0 + 3.0 * ratio)
            third = 1.0 + 3.0 * ratio
            norm = 1.0 / (count * bound)
            ah, al = stacked_rows(high, count, channels), stacked_rows(low, count, channels)
            gram = triple(dot_nt, (ah, al), (ah, al)) * norm
            side = 2 * count
            eye = (
                lax.broadcasted_iota(jnp.int32, (side, side), 0)
                == lax.broadcasted_iota(jnp.int32, (side, side), 1)
            )
            square = jnp.dot(gram, gram, precision=precise, preferred_element_type=F32)
            quad = (jnp.where(eye, second, 0.0) - third * gram + square) * norm
            quad_ref[index] = quad
            scale_ref[index] = jnp.broadcast_to(first, (1, beams))
            return carry

        lax.fori_loop(0, own, one_bin, 0)
        sh, sl = sh_ref[...], sl_ref[...]
        yh, yl = yh_ref[...], yl_ref[...]
        u_ref[...] = triple(dot, (yh, yl), (sh, sl))
        steer = sh[:channels].astype(F32) + sl[:channels].astype(F32)
        power = jnp.sum(steer * steer, axis=0, keepdims=True)
        power = power[:, :beams] + power[:, beams:]

        def second_pass(index, carry):
            base = pl.multiple_of(index * count, count)
            u = u_ref[pl.ds(base, count), :]
            up = jnp.concatenate([u[:, :beams], u[:, beams:]], axis=0)
            value = triple(dot, split(quad_ref[index]), split(up))
            high, low = split(value)
            th_ref[index] = high
            tl_ref[index] = low
            gain = scale_ref[index] * power - jnp.sum(up * value, axis=0, keepdims=True)
            gain_ref[index] = 1.0 / (gain * gain)
            return carry

        lax.fori_loop(0, own, second_pass, 0)

    out_shape = [
        jax.ShapeDtypeStruct((own * count, 2 * channels), BF16),
        jax.ShapeDtypeStruct((own * count, 2 * channels), BF16),
        jax.ShapeDtypeStruct((own, 2 * count, beams), BF16),
        jax.ShapeDtypeStruct((own, 2 * count, beams), BF16),
        jax.ShapeDtypeStruct((own, 1, beams), F32),
        jax.ShapeDtypeStruct((own, 1, beams), F32),
    ]
    return pl.pallas_call(
        body,
        in_specs=[VMEM] * 4 + [SMEM] * 2,
        out_specs=[VMEM] * 6,
        out_shape=out_shape,
        scratch_shapes=[
            pltpu.VMEM((own, 2 * count, 2 * count), F32),
            pltpu.VMEM((own * count, 2 * beams), F32),
        ],
        compiler_params=pltpu.CompilerParams(vmem_limit_bytes=LIMIT),
        name="weights",
    )(mine, other, steer_high, steer_low, range_taps, loading)


def beams_kernel(blocks, weights, steer_high, steer_low, range_taps):
    sections = len(blocks)
    _, _, gates, own, _ = blocks[0].shape
    size = 4 * gates * own
    count = sections * gates
    channels = 2 * LANES
    beams = steer_high.shape[1] // 2
    blocks = [block.reshape(size, LANES) for block in blocks]

    def body(*refs):
        block_refs = refs[:sections]
        (yh_ref, yl_ref, th_ref, tl_ref, scale_ref, gain_ref, sh_ref, sl_ref, taps_ref,
         power_ref, total_ref, held, z_ref, zh_ref, zl_ref, v_ref) = refs[sections:]
        section = lax.axis_index("section")
        for step in range(sections):
            start = pl.multiple_of(jnp.bitwise_xor(section, step) * size, size)
            held[pl.ds(start, size), :] = block_refs[step][...]

        for index in range(own):
            def load(part, gate):
                at = lambda side: pl.ds(
                    ((side * 2 + part) * gates + gate) * own + index, sections, stride=size
                )
                return jnp.concatenate([held[at(0), :], held[at(1), :]], axis=1)

            real, imag = filtered_bin(load, gates, taps_ref)
            base = index * count
            for gate in range(gates):
                here = slice(gate * sections, (gate + 1) * sections)
                at = pl.ds(base + gate, sections, stride=gates)
                for side in (0, 1):
                    lanes = slice(side * LANES, (side + 1) * LANES)
                    z_ref[side, at, :] = real[here, lanes]
                    z_ref[2 + side, at, :] = -imag[here, lanes]
            rows = pl.ds(base, count)
            high, low = split(jnp.concatenate([z_ref[q, rows, :] for q in range(4)], axis=1))
            zh_ref[rows, :] = high
            zl_ref[rows, :] = low
        v_ref[...] = triple(dot, (zh_ref[...], zl_ref[...]), (sh_ref[...], sl_ref[...]))
        total = jnp.zeros((1, beams), F32)
        for index in range(own):
            rows = pl.ds(index * count, count)
            stack = lambda ref: stacked_rows(ref[rows, :], count, channels)
            cross = triple(dot_nt, (stack(zh_ref), stack(zl_ref)), (stack(yh_ref), stack(yl_ref)))
            v = v_ref[rows, :]
            up = jnp.concatenate([v[:, :beams], v[:, beams:]], axis=0)
            out = scale_ref[index] * up - triple(dot, split(cross), (th_ref[index], tl_ref[index]))
            power = (out[:count] * out[:count] + out[count:] * out[count:]) * gain_ref[index]
            total = total + jnp.sum(power, axis=0, keepdims=True)
            power_ref[index] = power
        total_ref[...] = jnp.broadcast_to(total, total_ref.shape)

    return pl.pallas_call(
        body,
        in_specs=[VMEM] * (sections + 8) + [SMEM],
        out_specs=[VMEM] * 2,
        out_shape=[
            jax.ShapeDtypeStruct((own, count, beams), F32),
            jax.ShapeDtypeStruct((2 * sections, beams), F32),
        ],
        scratch_shapes=[
            pltpu.VMEM((sections * size, LANES), F32),
            pltpu.VMEM((4, own * count, LANES), F32),
            pltpu.VMEM((own * count, 2 * channels), BF16),
            pltpu.VMEM((own * count, 2 * channels), BF16),
            pltpu.VMEM((own * count, 2 * beams), F32),
        ],
        compiler_params=pltpu.CompilerParams(vmem_limit_bytes=LIMIT),
        name="beams",
    )(*blocks, *weights, steer_high, steer_low, range_taps)


def steering_tables(beam_index, channel_phase):
    channels = channel_phase.shape[0]
    own = channels // 2
    sub = lax.axis_index("sub")
    place = jnp.arange(channels, dtype=jnp.int32)
    place = jnp.where(place + sub * own >= channels, place + sub * own - channels, place + sub * own)
    turned = jnp.concatenate([channel_phase[own:], channel_phase[:own]])
    phase = jnp.where(sub == 0, channel_phase, turned)
    direction = -1.0 + (2.0 * beam_index.astype(F32) + 1.0) / LOOKS
    angle = math.pi * place.astype(F32)[:, None] * direction[None, :] + phase[:, None]
    cosine, sine = jnp.cos(angle), jnp.sin(angle)
    table = jnp.concatenate(
        [jnp.concatenate([cosine, sine], 1), jnp.concatenate([-sine, cosine], 1)], 0
    )
    high = lax.reduce_precision(table, 8, 7)
    return high.astype(BF16), lax.reduce_precision(table - high, 8, 7).astype(BF16)


def permuted(block, sections, step):
    return lax.ppermute(block, "section", [(place, place ^ step) for place in range(sections)])


def factored(echoes, range_taps, pulse_taper, channel_phase, loading, beam_index):
    parts, pulses, gates, lanes = echoes.shape
    sections = lax.axis_size("section")
    order = sorted(range(1, sections), reverse=True)
    swap = [(0, 1), (1, 0)]
    view = echoes.reshape(parts, pulses // HOP, HOP * gates, lanes)
    taper = pulse_taper.reshape(2, HOP)

    sent = doppler(view, taper, sections, 0, False)
    got = {0: sent[0]}
    for step in order:
        got[step] = permuted(sent[step], sections, step)
    mine, theirs = doppler(view, taper, sections, 1, True)
    other = lax.ppermute(theirs, "sub", swap)
    sent = pair_up(mine, other)
    later = {0: sent[0]}
    for step in order:
        later[step] = permuted(sent[step], sections, step)

    steer_high, steer_low = steering_tables(beam_index, channel_phase)
    keep, pass_on = gather_sub([got[step] for step in range(sections)])
    other = lax.ppermute(pass_on, "sub", swap)
    weights = weights_kernel(keep, other, steer_high, steer_low, range_taps, loading)
    power, total = beams_kernel(
        [later[step] for step in range(sections)], weights, steer_high, steer_low, range_taps
    )
    totals = lax.all_to_all(total, ("section", "sub"), 0, 0, tiled=True)
    noise_level = jnp.sum(totals, axis=0) / (PULSES * gates * sections)
    return (power / (noise_level + epsilon))[None]


def apply_taps(pad_real, pad_imag, range_taps, gate_count):
    axis_gates = pad_real.ndim - 2
    shape_out = pad_real.shape[:axis_gates] + (gate_count,) + pad_real.shape[axis_gates + 1 :]
    out_real = jnp.zeros(shape_out, jnp.float32)
    out_imag = jnp.zeros(shape_out, jnp.float32)
    for offset in range(range_taps.shape[1]):
        part_real = lax.slice_in_dim(pad_real, offset, offset + gate_count, axis=axis_gates)
        part_imag = lax.slice_in_dim(pad_imag, offset, offset + gate_count, axis=axis_gates)
        out_real = out_real + range_taps[0, offset] * part_real - range_taps[1, offset] * part_imag
        out_imag = out_imag + range_taps[0, offset] * part_imag + range_taps[1, offset] * part_real
    return (out_real, out_imag)


def doppler_table(pulse_taper):
    pulse_count = pulse_taper.shape[0]
    pulse_index = jnp.arange(pulse_count, dtype=jnp.int32)
    product = pulse_index[:, None] * pulse_index[None, :] % pulse_count
    phase_angle = 2.0 * math.pi / pulse_count * product.astype(jnp.float32)
    cosine = jnp.cos(phase_angle) * pulse_taper[None, :]
    sine_part = jnp.sin(phase_angle) * pulse_taper[None, :]
    upper_rows = jnp.concatenate([cosine, sine_part], axis=1)
    lower_rows = jnp.concatenate([-sine_part, cosine], axis=1)
    return jnp.concatenate([upper_rows, lower_rows], axis=0)


def transform(doppler, segment):
    shape_in = segment.shape
    flattened = segment.reshape(shape_in[0] * shape_in[1], -1)
    result = jnp.dot(doppler, flattened, precision=precise, preferred_element_type=jnp.float32)
    return result.reshape(shape_in)


def batched(first, second):
    return jnp.einsum("dij,djk->dik", first, second, precision=precise)


def complex_product(left_real, left_imag, right_real, right_imag):
    out_real = batched(left_real, right_real) - batched(left_imag, right_imag)
    out_imag = batched(left_real, right_imag) + batched(left_imag, right_real)
    return (out_real, out_imag)


def gram_product(first, second):
    return jnp.einsum("dgi,dgj->dij", first, second, precision=precise)


def loaded_inverse(real_part, imag_part, loading):
    gate_count = real_part.shape[1]
    channels = real_part.shape[2]
    cov_real = (
        gram_product(real_part, real_part) + gram_product(imag_part, imag_part)
    ) / gate_count
    cov_imag = (
        gram_product(real_part, imag_part) - gram_product(imag_part, real_part)
    ) / gate_count
    identity = jnp.eye(channels, dtype=jnp.float32)
    trace_sum = jnp.sum(cov_real * identity[None], axis=(1, 2))
    cov_real = cov_real + (loading[0] * trace_sum / channels)[:, None, None] * identity[None]
    row_bound = jnp.max(jnp.sum(jnp.abs(cov_real) + jnp.abs(cov_imag), axis=2), axis=1)
    inv_real = identity[None] / row_bound[:, None, None]
    inv_imag = jnp.zeros_like(inv_real)
    for newton_step in range(ITERS):
        prod_real, prod_imag = complex_product(cov_real, cov_imag, inv_real, inv_imag)
        inv_real, inv_imag = complex_product(
            inv_real, inv_imag, 2.0 * identity[None] - prod_real, -prod_imag
        )
    return (inv_real, inv_imag)


def steering(beam_index, channel_phase):
    channels = channel_phase.shape[0]
    direction = -1.0 + (2.0 * beam_index.astype(jnp.float32) + 1.0) / LOOKS
    phase_angle = (
        math.pi * jnp.arange(channels, dtype=jnp.float32)[:, None] * direction[None, :]
        + channel_phase[:, None]
    )
    return (jnp.cos(phase_angle), jnp.sin(phase_angle))


def beam_weights(inv_real, inv_imag, steer_real, steer_imag):
    weight_real = jnp.einsum("dij,jb->dib", inv_real, steer_real, precision=precise) - jnp.einsum(
        "dij,jb->dib", inv_imag, steer_imag, precision=precise
    )
    weight_imag = jnp.einsum("dij,jb->dib", inv_real, steer_imag, precision=precise) + jnp.einsum(
        "dij,jb->dib", inv_imag, steer_real, precision=precise
    )
    gain_norm = jnp.sum(steer_real[None] * weight_real + steer_imag[None] * weight_imag, axis=1)
    return (weight_real / gain_norm[:, None, :], weight_imag / gain_norm[:, None, :])


def form_beams(data_real, data_imag, weight_real, weight_imag):
    out_real = jnp.einsum("dgc,dcb->dgb", data_real, weight_real, precision=precise) + jnp.einsum(
        "dgc,dcb->dgb", data_imag, weight_imag, precision=precise
    )
    out_imag = jnp.einsum("dgc,dcb->dgb", data_imag, weight_real, precision=precise) - jnp.einsum(
        "dgc,dcb->dgb", data_real, weight_imag, precision=precise
    )
    return out_real * out_real + out_imag * out_imag


def on_device(echoes, range_taps, pulse_taper, channel_phase, loading, beam_index):
    rim_width = range_taps.shape[1] // 2
    doppler = doppler_table(pulse_taper)
    spectra = [
        transform(
            doppler, lax.slice_in_dim(echoes, interval * HOP, interval * HOP + PULSES, axis=1)
        )
        for interval in range(INTERVALS)
    ]
    turned = [
        lax.all_to_all(
            lax.all_to_all(spectrum, "section", split_axis=1, concat_axis=2, tiled=True),
            "sub",
            split_axis=1,
            concat_axis=3,
            tiled=True,
        )
        for spectrum in spectra
    ]
    refined = []
    for spectrum in turned:
        padded_bins = jnp.pad(spectrum, ((0, 0), (0, 0), (rim_width, rim_width), (0, 0)))
        part_real, part_imag = apply_taps(
            padded_bins[0], padded_bins[1], range_taps, spectrum.shape[2]
        )
        refined.append(jnp.stack([part_real, part_imag]))
    turned = refined
    steer_real, steer_imag = steering(beam_index, channel_phase)
    interval = 0
    inv_real, inv_imag = loaded_inverse(turned[interval][0], turned[interval][1], loading)
    weight_real, weight_imag = beam_weights(inv_real, inv_imag, steer_real, steer_imag)
    beam_power = form_beams(
        turned[interval + 1][0], turned[interval + 1][1], weight_real, weight_imag
    )
    partials = [jnp.sum(beam_power, axis=(0, 1))]
    totals = lax.psum(jnp.stack(partials), ("section", "sub"))
    noise_level = totals / (PULSES * turned[0].shape[2])
    return jnp.stack([beam_power / (noise_level[0] + epsilon)])


def solution(mesh):
    in_specs = (P("groups", None, "section", "sub"), P(), P(), P(), P(), P())
    out_specs = P("groups", ("section", "sub"), None, None)
    small = mesh.shape["section"] == 8 and mesh.shape["sub"] == 2

    def run(echoes, range_taps, pulse_taper, channel_phase, loading, beam_index):
        args = (echoes, range_taps, pulse_taper, channel_phase, loading, beam_index)
        fits = small and echoes.shape[2] == 4 and echoes.shape[3] == LANES
        return factored(*args) if fits else on_device(*args)

    return jax.shard_map(run, mesh=mesh, in_specs=in_specs, out_specs=out_specs, check_vma=False)
```

```python
import math

import jax
import jax.numpy as jnp
import numpy as np
from jax import lax
from jax.experimental import pallas as pl
from jax.experimental.pallas import tpu as pltpu
from jax.sharding import PartitionSpec as P


PULSES = 256
INTERVALS = 2
ITERS = 2
LOOKS = 1024
HOP = 128


precise = lax.Precision.HIGHEST
epsilon = 1e-06
F32 = jnp.float32
BF16 = jnp.bfloat16
LANES = 128
VMEM = pl.BlockSpec(memory_space=pltpu.VMEM)
SMEM = pl.BlockSpec(memory_space=pltpu.SMEM)
LIMIT = 16 << 20


def split(value):
    high = value.astype(BF16)
    return high, (value - high.astype(F32)).astype(BF16)


def dot(left, right):
    return jnp.dot(left, right, preferred_element_type=F32)


def dot_nt(left, right):
    return lax.dot_general(left, right, (((1,), (1,)), ((), ())), preferred_element_type=F32)


def dot_tn(left, right):
    return lax.dot_general(left, right, (((0,), (0,)), ((), ())), preferred_element_type=F32)


def triple(product, left, right):
    return product(left[0], right[0]) + (product(left[0], right[1]) + product(left[1], right[0]))


def doppler_tables(pulses):
    half = pulses // 2
    bins = np.arange(half)[:, None]
    tables = []
    for parity in (0, 1):
        phase = 2.0 * np.pi * ((bins * np.arange(parity, pulses, 2)[None, :]) % pulses) / pulses
        cosine, sine = np.cos(phase), np.sin(phase)
        table = np.concatenate(
            [np.concatenate([cosine, sine], 1), np.concatenate([-sine, cosine], 1)], 0
        ).astype(np.float32)
        high = table.astype(jnp.bfloat16)
        tables += [high, (table - high.astype(np.float32)).astype(jnp.bfloat16)]
    return np.stack(tables)


def doppler_body(gates, hop, interval, view_ref, taper_ref, table_ref, result, tapers):
    half = hop
    for segment in (0, 1):
        row = taper_ref[segment : segment + 1, :]
        tapers[segment * hop : (segment + 1) * hop, :] = jnp.broadcast_to(row, (hop, hop)).T
    for gate in range(gates):
        for parity in (0, 1):
            rows = []
            for part in (0, 1):
                for segment in (0, 1):
                    at = pl.ds(parity * gates + gate, hop // 2, stride=2 * gates)
                    block = view_ref[part, interval + segment, at, :]
                    taper = tapers[pl.ds(segment * hop + parity, hop // 2, stride=2), :]
                    rows.append(block * taper)
            data = split(jnp.concatenate(rows, axis=0))
            table = (table_ref[2 * parity], table_ref[2 * parity + 1])
            value = triple(dot, table, data)
            if parity == 0:
                even = value
            else:
                for part in (0, 1):
                    own = slice(part * half, (part + 1) * half)
                    result[part, gate, :half] = even[own] + value[own]
                    result[part, gate, half:] = even[own] - value[own]


def doppler(view, taper, sections, interval, split_sub):
    gates = view.shape[2] // HOP
    per = PULSES // sections
    own = per // 2

    def body(view_ref, taper_ref, table_ref, *rest):
        out_refs, result, tapers = rest[:-2], rest[-2], rest[-1]
        doppler_body(gates, HOP, interval, view_ref, taper_ref, table_ref, result, tapers)
        section = lax.axis_index("section")
        if not split_sub:
            for step in range(sections):
                start = pl.multiple_of(jnp.bitwise_xor(section, step) * per, per)
                out_refs[step][...] = result[:, :, pl.ds(start, per), :]
        else:
            sub = lax.axis_index("sub")
            for step in range(sections):
                start = jnp.bitwise_xor(section, step) * per
                mine = pl.multiple_of(start + sub * own, own)
                theirs = pl.multiple_of(start + (1 - sub) * own, own)
                out_refs[0][step] = result[:, :, pl.ds(mine, own), :]
                out_refs[1][step] = result[:, :, pl.ds(theirs, own), :]

    tables = jnp.asarray(doppler_tables(PULSES))
    if split_sub:
        shape = (sections, 2, gates, own, LANES)
        outs = [jax.ShapeDtypeStruct(shape, F32)] * 2
    else:
        shape = (2, gates, per, LANES)
        outs = [jax.ShapeDtypeStruct(shape, F32)] * sections
    return pl.pallas_call(
        body,
        in_specs=[VMEM] * 3,
        out_specs=[VMEM] * len(outs),
        out_shape=outs,
        scratch_shapes=[
            pltpu.VMEM((2, gates, PULSES, LANES), F32),
            pltpu.VMEM((PULSES, LANES), F32),
        ],
        compiler_params=pltpu.CompilerParams(vmem_limit_bytes=LIMIT),
    )(view, taper, tables)


def gather_sub(blocks):
    sections = len(blocks)
    _, gates, per, _ = blocks[0].shape
    own = per // 2

    def body(*refs):
        section, sub = lax.axis_index("section"), lax.axis_index("sub")
        mine = pl.multiple_of(sub * own, own)
        theirs = pl.multiple_of((1 - sub) * own, own)
        for step in range(sections):
            source = jnp.bitwise_xor(section, step)
            refs[sections][source] = refs[step][:, :, pl.ds(mine, own), :]
            refs[sections + 1][source] = refs[step][:, :, pl.ds(theirs, own), :]

    shape = jax.ShapeDtypeStruct((sections, 2, gates, own, LANES), F32)
    return pl.pallas_call(
        body,
        in_specs=[VMEM] * sections,
        out_specs=[VMEM] * 2,
        out_shape=[shape] * 2,
        compiler_params=pltpu.CompilerParams(vmem_limit_bytes=LIMIT),
        name="gather_sub",
    )(*blocks)


def pair_up(mine, other):
    sections = mine.shape[0]

    def body(mine_ref, other_ref, *out_refs):
        for step in range(sections):
            out_refs[step][0] = mine_ref[step]
            out_refs[step][1] = other_ref[step]

    shape = jax.ShapeDtypeStruct((2,) + mine.shape[1:], F32)
    return pl.pallas_call(
        body,
        in_specs=[VMEM] * 2,
        out_specs=[VMEM] * sections,
        out_shape=[shape] * sections,
        compiler_params=pltpu.CompilerParams(vmem_limit_bytes=LIMIT),
        name="pair_up",
    )(mine, other)


def filter_matrix(taps_ref, gates, sections, conjugate):
    count = gates * sections
    side = 2 * count
    taps = taps_ref.shape[1]
    row = lax.broadcasted_iota(jnp.int32, (side, side), 0)
    column = lax.broadcasted_iota(jnp.int32, (side, side), 1)
    row_imag, column_imag = row >= count, column >= count
    row_gate = jnp.where(row_imag, row - count, row)
    place = jnp.where(column_imag, column - count, column)
    inner = sum(jnp.where(place >= gate * sections, 1, 0) for gate in range(1, gates))
    column_gate = (place - inner * sections) * gates + inner
    tap = column_gate - row_gate + taps // 2
    real = sum(jnp.where(tap == j, taps_ref[0, j], 0.0) for j in range(taps))
    imag = sum(jnp.where(tap == j, taps_ref[1, j], 0.0) for j in range(taps))
    straight, crossed = row_imag == column_imag, jnp.where(row_imag, imag, -imag)
    matrix = jnp.where(straight, real, crossed)
    if conjugate:
        matrix = jnp.where(row_imag, -matrix, matrix)
    return split(matrix)


def stacked(product, left, right):
    rows = left[0].shape[0]
    both = product(jnp.concatenate(left, axis=0), right[0])
    return both[:rows] + (both[rows:] + product(left[0], right[1]))


def beside(value, negate_first):
    count = value.shape[0] // 2
    real, imag = value[:count], value[count:]
    if negate_first:
        return jnp.concatenate(
            [jnp.concatenate([real, -imag], axis=1), jnp.concatenate([imag, real], axis=1)], axis=0
        )
    return jnp.concatenate(
        [jnp.concatenate([real, imag], axis=1), jnp.concatenate([-imag, real], axis=1)], axis=0
    )


def weights_kernel(mine, other, steer, range_taps, loading):
    sections, _, gates, own, _ = mine.shape
    count = sections * gates
    side = 2 * count
    channels = 2 * LANES
    beams = steer.shape[1] // 2
    stride = 2 * gates * own
    mine = mine.reshape(sections * stride, LANES)
    other = other.reshape(sections * stride, LANES)

    def body(mine_ref, other_ref, steer_ref, taps_ref, load_ref,
             bh_ref, bl_ref, th_ref, tl_ref, gain_ref,
             ah_ref, al_ref, rows_ref, sums_ref, squares_ref, u_ref):
        matrix = filter_matrix(taps_ref, gates, sections, True)
        for index in range(own):
            def load(ref):
                return jnp.concatenate(
                    [ref[pl.ds((part * gates + gate) * own + index, sections, stride=stride), :]
                     for part in (0, 1) for gate in range(gates)], axis=0)

            data = jnp.concatenate([load(mine_ref), load(other_ref)], axis=1)
            value = stacked(dot, matrix, split(data))
            squares_ref[index : index + 1, :] = jnp.sum(value * value, axis=0, keepdims=True)
            high, low = split(value)
            ah_ref[index] = high
            al_ref[index] = low
            bh_ref[index] = beside(high, False)
            bl_ref[index] = beside(low, False)
            here = slice(index * count, (index + 1) * count)
            for place, part in enumerate((high, low, high)):
                lanes = slice(place * 2 * channels, (place + 1) * 2 * channels)
                rows_ref[here, lanes] = jnp.concatenate([part[:count], part[count:]], axis=1)
        for index in range(own):
            high, low = ah_ref[index], al_ref[index]
            turn = lambda v: jnp.concatenate(
                [v, jnp.concatenate([v[count:], -v[:count]], axis=0)], axis=1
            )
            rh, rl = turn(high), turn(low)
            left = jnp.concatenate([high, high, low], axis=0)
            right = jnp.concatenate([rh, rl, rh], axis=0)
            cov = jnp.abs(dot_tn(left, right))
            sums_ref[index : index + 1, :] = jnp.sum(
                cov[:, :channels] + cov[:, channels:], axis=0, keepdims=True
            )
        bound = jnp.max(sums_ref[...], axis=1, keepdims=True) / count
        trace = jnp.sum(squares_ref[...], axis=1, keepdims=True) / count
        delta = load_ref[0] * trace / channels
        bound = bound + delta
        ratio = 1.0 - delta / bound
        first = 1.0 + ratio * (1.0 + ratio * (1.0 + ratio))
        second = 1.0 + ratio * (2.0 + 3.0 * ratio)
        third = 1.0 + 3.0 * ratio
        norm = 1.0 / (count * bound)
        u_ref[...] = dot(rows_ref[...], steer_ref[...])
        low_at = 2 * 2 * channels
        table = steer_ref[:channels, :].astype(F32) + steer_ref[low_at : low_at + channels, :].astype(F32)
        power = jnp.sum(table * table, axis=0, keepdims=True)
        power = power[:, :beams] + power[:, beams:]
        eye = (
            lax.broadcasted_iota(jnp.int32, (side, side), 0)
            == lax.broadcasted_iota(jnp.int32, (side, side), 1)
        )
        for index in range(own):
            at = slice(index, index + 1)
            halves = beside(ah_ref[index], True), beside(al_ref[index], True)
            gram = stacked(dot_nt, halves, halves) * norm[at]
            parts = split(gram)
            square = stacked(dot, parts, parts)
            quad = (jnp.where(eye, second[at], 0.0) - third[at] * gram + square) * (norm[at] / first[at])
            u = u_ref[index * count : (index + 1) * count, :]
            up = jnp.concatenate([u[:, :beams], u[:, beams:]], axis=0)
            value = stacked(dot, split(quad), split(up))
            high, low = split(value)
            th_ref[index] = beside(high, False)
            tl_ref[index] = beside(low, False)
            gain = power - jnp.sum(up * value, axis=0, keepdims=True)
            gain_ref[at, :] = 1.0 / (gain * gain)

    wide = jax.ShapeDtypeStruct((own, side, 2 * channels), BF16)
    turned = jax.ShapeDtypeStruct((own, side, 2 * beams), BF16)
    return pl.pallas_call(
        body,
        in_specs=[VMEM] * 3 + [SMEM] * 2,
        out_specs=[VMEM] * 5,
        out_shape=[wide, wide, turned, turned, jax.ShapeDtypeStruct((own, beams), F32)],
        scratch_shapes=[
            pltpu.VMEM((own, side, channels), BF16),
            pltpu.VMEM((own, side, channels), BF16),
            pltpu.VMEM((own * count, 6 * channels), BF16),
            pltpu.VMEM((own, channels), F32),
            pltpu.VMEM((own, channels), F32),
            pltpu.VMEM((own * count, 2 * beams), F32),
        ],
        compiler_params=pltpu.CompilerParams(vmem_limit_bytes=LIMIT),
        name="weights",
    )(mine, other, steer, range_taps, loading)


def beams_kernel(blocks, weights, steer, range_taps):
    sections = len(blocks)
    _, _, gates, own, _ = blocks[0].shape
    size = 4 * gates * own
    count = sections * gates
    side = 2 * count
    channels = 2 * LANES
    beams = steer.shape[1] // 2
    blocks = [block.reshape(size, LANES) for block in blocks]

    def body(*refs):
        block_refs = refs[:sections]
        (bh_ref, bl_ref, th_ref, tl_ref, gain_ref, steer_ref, taps_ref,
         power_ref, total_ref, held, rows_ref, v_ref, cross_ref) = refs[sections:]
        section = lax.axis_index("section")
        for step in range(sections):
            start = pl.multiple_of(jnp.bitwise_xor(section, step) * size, size)
            held[pl.ds(start, size), :] = block_refs[step][...]
        matrix = filter_matrix(taps_ref, gates, sections, False)
        wide = 2 * channels
        for index in range(own):
            def load(half, part):
                return jnp.concatenate(
                    [held[pl.ds(((half * 2 + part) * gates + gate) * own + index, sections, stride=size), :]
                     for gate in range(gates)], axis=0)

            data = jnp.concatenate([load(half, part) for part in (0, 1) for half in (0, 1)], axis=1)
            high, low = split(data)
            here = slice(index * count, (index + 1) * count)
            for place, part in enumerate((high, low, high)):
                rows_ref[here, place * wide : (place + 1) * wide] = part
        for index in range(own):
            here = slice(index * count, (index + 1) * count)
            parts = rows_ref[here, :wide], rows_ref[here, wide : 2 * wide]
            cross_ref[index] = stacked(dot_nt, parts, (bh_ref[index], bl_ref[index]))
        v_ref[...] = dot(rows_ref[...], steer_ref[...])
        for index in range(own):
            here = slice(index * count, (index + 1) * count)
            low_rank = stacked(dot, split(cross_ref[index]), (th_ref[index], tl_ref[index]))
            v_ref[here, :] = v_ref[here, :] - low_rank
        total = jnp.zeros((1, beams), F32)
        for index in range(own):
            v = v_ref[index * count : (index + 1) * count, :]
            up = jnp.concatenate([v[:, :beams], v[:, beams:]], axis=0)
            out = stacked(dot, matrix, split(up))
            power = (out[:count] * out[:count] + out[count:] * out[count:]) * gain_ref[index : index + 1, :]
            total = total + jnp.sum(power, axis=0, keepdims=True)
            power_ref[index] = power
        total_ref[...] = jnp.broadcast_to(total, total_ref.shape)

    return pl.pallas_call(
        body,
        in_specs=[VMEM] * (sections + 6) + [SMEM],
        out_specs=[VMEM] * 2,
        out_shape=[
            jax.ShapeDtypeStruct((own, count, beams), F32),
            jax.ShapeDtypeStruct((2 * sections, beams), F32),
        ],
        scratch_shapes=[
            pltpu.VMEM((sections * size, LANES), F32),
            pltpu.VMEM((own * count, 6 * channels), BF16),
            pltpu.VMEM((own * count, 2 * beams), F32),
            pltpu.VMEM((own, count, side), F32),
        ],
        compiler_params=pltpu.CompilerParams(vmem_limit_bytes=LIMIT),
        name="beams",
    )(*blocks, *weights, steer, range_taps)


def steering_tables(beam_index, channel_phase):
    channels = channel_phase.shape[0]
    own = channels // 2
    sub = lax.axis_index("sub")
    place = jnp.arange(channels, dtype=jnp.int32)
    place = jnp.where(place + sub * own >= channels, place + sub * own - channels, place + sub * own)
    turned = jnp.concatenate([channel_phase[own:], channel_phase[:own]])
    phase = jnp.where(sub == 0, channel_phase, turned)
    direction = -1.0 + (2.0 * beam_index.astype(F32) + 1.0) / LOOKS
    angle = math.pi * place.astype(F32)[:, None] * direction[None, :] + phase[:, None]
    cosine, sine = jnp.cos(angle), jnp.sin(angle)
    table = jnp.concatenate(
        [jnp.concatenate([cosine, -sine], 1), jnp.concatenate([sine, cosine], 1)], 0
    )
    high = lax.reduce_precision(table, 8, 7)
    low = lax.reduce_precision(table - high, 8, 7).astype(BF16)
    high = high.astype(BF16)
    return jnp.concatenate([high, high, low], 0)


def permuted(block, sections, step):
    return lax.ppermute(block, "section", [(place, place ^ step) for place in range(sections)])


def swapped(block):
    return lax.ppermute(block, "sub", [(0, 1), (1, 0)])


def factored_steps(echoes, range_taps, pulse_taper, channel_phase, loading, beam_index):
    parts, pulses, gates, lanes = echoes.shape
    sections = lax.axis_size("section")
    order = sorted(range(1, sections), reverse=True)
    view = echoes.reshape(parts, pulses // HOP, HOP * gates, lanes)
    taper = pulse_taper.reshape(2, HOP)

    sent = doppler(view, taper, sections, 0, False)
    got = {0: sent[0]}
    for step in order:
        got[step] = permuted(sent[step], sections, step)
    mine, theirs = doppler(view, taper, sections, 1, True)
    other = swapped(theirs)
    sent = pair_up(mine, other)
    later = {0: sent[0]}
    for step in order:
        later[step] = permuted(sent[step], sections, step)

    steer = steering_tables(beam_index, channel_phase)
    keep, pass_on = gather_sub([got[step] for step in range(sections)])
    other = swapped(pass_on)
    weights = weights_kernel(keep, other, steer, range_taps, loading)
    power, total = beams_kernel(
        [later[step] for step in range(sections)], weights, steer, range_taps
    )
    totals = lax.all_to_all(total, ("section", "sub"), 0, 0, tiled=True)
    noise_level = jnp.sum(totals, axis=0) / (PULSES * gates * sections)
    return (power / (noise_level + epsilon))[None]


def apply_taps(pad_real, pad_imag, range_taps, gate_count):
    axis_gates = pad_real.ndim - 2
    shape_out = pad_real.shape[:axis_gates] + (gate_count,) + pad_real.shape[axis_gates + 1 :]
    out_real = jnp.zeros(shape_out, jnp.float32)
    out_imag = jnp.zeros(shape_out, jnp.float32)
    for offset in range(range_taps.shape[1]):
        part_real = lax.slice_in_dim(pad_real, offset, offset + gate_count, axis=axis_gates)
        part_imag = lax.slice_in_dim(pad_imag, offset, offset + gate_count, axis=axis_gates)
        out_real = out_real + range_taps[0, offset] * part_real - range_taps[1, offset] * part_imag
        out_imag = out_imag + range_taps[0, offset] * part_imag + range_taps[1, offset] * part_real
    return (out_real, out_imag)


def doppler_table(pulse_taper):
    pulse_count = pulse_taper.shape[0]
    pulse_index = jnp.arange(pulse_count, dtype=jnp.int32)
    product = pulse_index[:, None] * pulse_index[None, :] % pulse_count
    phase_angle = 2.0 * math.pi / pulse_count * product.astype(jnp.float32)
    cosine = jnp.cos(phase_angle) * pulse_taper[None, :]
    sine_part = jnp.sin(phase_angle) * pulse_taper[None, :]
    upper_rows = jnp.concatenate([cosine, sine_part], axis=1)
    lower_rows = jnp.concatenate([-sine_part, cosine], axis=1)
    return jnp.concatenate([upper_rows, lower_rows], axis=0)


def transform(doppler, segment):
    shape_in = segment.shape
    flattened = segment.reshape(shape_in[0] * shape_in[1], -1)
    result = jnp.dot(doppler, flattened, precision=precise, preferred_element_type=jnp.float32)
    return result.reshape(shape_in)


def batched(first, second):
    return jnp.einsum("dij,djk->dik", first, second, precision=precise)


def complex_product(left_real, left_imag, right_real, right_imag):
    out_real = batched(left_real, right_real) - batched(left_imag, right_imag)
    out_imag = batched(left_real, right_imag) + batched(left_imag, right_real)
    return (out_real, out_imag)


def gram_product(first, second):
    return jnp.einsum("dgi,dgj->dij", first, second, precision=precise)


def loaded_inverse(real_part, imag_part, loading):
    gate_count = real_part.shape[1]
    channels = real_part.shape[2]
    cov_real = (
        gram_product(real_part, real_part) + gram_product(imag_part, imag_part)
    ) / gate_count
    cov_imag = (
        gram_product(real_part, imag_part) - gram_product(imag_part, real_part)
    ) / gate_count
    identity = jnp.eye(channels, dtype=jnp.float32)
    trace_sum = jnp.sum(cov_real * identity[None], axis=(1, 2))
    cov_real = cov_real + (loading[0] * trace_sum / channels)[:, None, None] * identity[None]
    row_bound = jnp.max(jnp.sum(jnp.abs(cov_real) + jnp.abs(cov_imag), axis=2), axis=1)
    inv_real = identity[None] / row_bound[:, None, None]
    inv_imag = jnp.zeros_like(inv_real)
    for _ in range(ITERS):
        prod_real, prod_imag = complex_product(cov_real, cov_imag, inv_real, inv_imag)
        inv_real, inv_imag = complex_product(
            inv_real, inv_imag, 2.0 * identity[None] - prod_real, -prod_imag
        )
    return (inv_real, inv_imag)


def steering(beam_index, channel_phase):
    channels = channel_phase.shape[0]
    direction = -1.0 + (2.0 * beam_index.astype(jnp.float32) + 1.0) / LOOKS
    phase_angle = (
        math.pi * jnp.arange(channels, dtype=jnp.float32)[:, None] * direction[None, :]
        + channel_phase[:, None]
    )
    return (jnp.cos(phase_angle), jnp.sin(phase_angle))


def beam_weights(inv_real, inv_imag, steer_real, steer_imag):
    weight_real = jnp.einsum("dij,jb->dib", inv_real, steer_real, precision=precise) - jnp.einsum(
        "dij,jb->dib", inv_imag, steer_imag, precision=precise
    )
    weight_imag = jnp.einsum("dij,jb->dib", inv_real, steer_imag, precision=precise) + jnp.einsum(
        "dij,jb->dib", inv_imag, steer_real, precision=precise
    )
    gain_norm = jnp.sum(steer_real[None] * weight_real + steer_imag[None] * weight_imag, axis=1)
    return (weight_real / gain_norm[:, None, :], weight_imag / gain_norm[:, None, :])


def form_beams(data_real, data_imag, weight_real, weight_imag):
    out_real = jnp.einsum("dgc,dcb->dgb", data_real, weight_real, precision=precise) + jnp.einsum(
        "dgc,dcb->dgb", data_imag, weight_imag, precision=precise
    )
    out_imag = jnp.einsum("dgc,dcb->dgb", data_imag, weight_real, precision=precise) - jnp.einsum(
        "dgc,dcb->dgb", data_real, weight_imag, precision=precise
    )
    return out_real * out_real + out_imag * out_imag


def on_device(echoes, range_taps, pulse_taper, channel_phase, loading, beam_index):
    rim_width = range_taps.shape[1] // 2
    doppler = doppler_table(pulse_taper)
    spectra = [
        transform(
            doppler, lax.slice_in_dim(echoes, interval * HOP, interval * HOP + PULSES, axis=1)
        )
        for interval in range(INTERVALS)
    ]
    turned = [
        lax.all_to_all(
            lax.all_to_all(spectrum, "section", split_axis=1, concat_axis=2, tiled=True),
            "sub",
            split_axis=1,
            concat_axis=3,
            tiled=True,
        )
        for spectrum in spectra
    ]
    refined = []
    for spectrum in turned:
        padded_bins = jnp.pad(spectrum, ((0, 0), (0, 0), (rim_width, rim_width), (0, 0)))
        part_real, part_imag = apply_taps(
            padded_bins[0], padded_bins[1], range_taps, spectrum.shape[2]
        )
        refined.append(jnp.stack([part_real, part_imag]))
    turned = refined
    steer_real, steer_imag = steering(beam_index, channel_phase)
    interval = 0
    inv_real, inv_imag = loaded_inverse(turned[interval][0], turned[interval][1], loading)
    weight_real, weight_imag = beam_weights(inv_real, inv_imag, steer_real, steer_imag)
    beam_power = form_beams(
        turned[interval + 1][0], turned[interval + 1][1], weight_real, weight_imag
    )
    partials = [jnp.sum(beam_power, axis=(0, 1))]
    totals = lax.psum(jnp.stack(partials), ("section", "sub"))
    noise_level = totals / (PULSES * turned[0].shape[2])
    return jnp.stack([beam_power / (noise_level[0] + epsilon)])


def solution(mesh):
    in_specs = (P("groups", None, "section", "sub"), P(), P(), P(), P(), P())
    out_specs = P("groups", ("section", "sub"), None, None)
    sections = mesh.shape["section"]
    small = sections == 8 and mesh.shape["sub"] == 2

    def run(echoes, range_taps, pulse_taper, channel_phase, loading, beam_index):
        args = (echoes, range_taps, pulse_taper, channel_phase, loading, beam_index)
        fits = small and echoes.shape[2] == 4 and echoes.shape[3] == LANES
        return factored_steps(*args) if fits else on_device(*args)

    return jax.shard_map(run, mesh=mesh, in_specs=in_specs, out_specs=out_specs, check_vma=False)
```

```python
import math

import jax
import jax.numpy as jnp
import numpy as np
from jax import lax
from jax.experimental import pallas as pl
from jax.experimental.pallas import tpu as pltpu
from jax.sharding import PartitionSpec as P


PULSES = 256
INTERVALS = 2
ITERS = 2
LOOKS = 1024
HOP = 128


precise = lax.Precision.HIGHEST
epsilon = 1e-06
F32 = jnp.float32
BF16 = jnp.bfloat16
LANES = 128
VMEM = pl.BlockSpec(memory_space=pltpu.VMEM)
SMEM = pl.BlockSpec(memory_space=pltpu.SMEM)
HBM = pl.BlockSpec(memory_space=pltpu.HBM)
LIMIT = 16 << 20
PAD = 8


def split(value):
    high = value.astype(BF16)
    return high, (value - high.astype(F32)).astype(BF16)


def dot(left, right):
    return jnp.dot(left, right, preferred_element_type=F32)


def dot_nt(left, right):
    return lax.dot_general(left, right, (((1,), (1,)), ((), ())), preferred_element_type=F32)


def dot_tn(left, right):
    return lax.dot_general(left, right, (((0,), (0,)), ((), ())), preferred_element_type=F32)


def triple(product, left, right):
    return product(left[0], right[0]) + (product(left[0], right[1]) + product(left[1], right[0]))


def doppler_tables(pulses):
    half = pulses // 2
    bins = np.arange(half)[:, None]
    tables = []
    for parity in (0, 1):
        phase = 2.0 * np.pi * ((bins * np.arange(parity, pulses, 2)[None, :]) % pulses) / pulses
        cosine, sine = np.cos(phase), np.sin(phase)
        table = np.concatenate([cosine, sine], 1).astype(np.float32)
        high = table.astype(jnp.bfloat16)
        tables += [high, (table - high.astype(np.float32)).astype(jnp.bfloat16)]
    return np.stack(tables)


def full_table(rows):
    half = rows.shape[1] // 2
    turned = jnp.concatenate([-rows[:, half:], rows[:, :half]], axis=1)
    return jnp.concatenate([rows, turned], axis=0)


def doppler_body(gates, hop, view_ref, taper_ref, table_ref, result, tapers):
    half = hop
    for segment in (0, 1):
        row = taper_ref[segment : segment + 1, :]
        tapers[segment * hop : (segment + 1) * hop, :] = jnp.broadcast_to(row, (hop, hop)).T
    for gate in range(gates):
        for parity in (0, 1):
            rows = []
            for part in (0, 1):
                for segment in (0, 1):
                    at = pl.ds(parity * gates + gate, hop // 2, stride=2 * gates)
                    block = view_ref[part, segment, at, :]
                    taper = tapers[pl.ds(segment * hop + parity, hop // 2, stride=2), :]
                    rows.append(block * taper)
            data = split(jnp.concatenate(rows, axis=0))
            table = full_table(table_ref[2 * parity]), full_table(table_ref[2 * parity + 1])
            value = triple(dot, table, data)
            if parity == 0:
                even = value
            else:
                for part in (0, 1):
                    own = slice(part * half, (part + 1) * half)
                    result[part, gate, :half] = even[own] + value[own]
                    result[part, gate, half:] = even[own] - value[own]


def doppler(view, taper, sections, interval, split_sub):
    gates = view.shape[2] // HOP
    per = PULSES // sections
    own = per // 2

    def body(view_ref, taper_ref, table_ref, *rest):
        outs = 2 if split_sub else sections
        out_refs, scratch = rest[:outs], rest[outs:]
        result, tapers, own_view, own_taper, own_table, sems = scratch
        copies = [pltpu.make_async_copy(taper_ref, own_taper, sems.at[0])]
        copies.append(pltpu.make_async_copy(table_ref, own_table, sems.at[1]))
        for part in (0, 1):
            blocks = view_ref.at[part, pl.ds(interval, 2)]
            copies.append(pltpu.make_async_copy(blocks, own_view.at[part], sems.at[2 + part]))
        for copy in copies:
            copy.start()
        for copy in copies:
            copy.wait()
        doppler_body(gates, HOP, own_view, own_taper, own_table, result, tapers)
        section = lax.axis_index("section")
        if not split_sub:
            for step in range(sections):
                start = pl.multiple_of(jnp.bitwise_xor(section, step) * per, per)
                out_refs[step][...] = result[:, :, pl.ds(start, per), :]
        else:
            sub = lax.axis_index("sub")
            for step in range(sections):
                start = jnp.bitwise_xor(section, step) * per
                mine = pl.multiple_of(start + sub * own, own)
                theirs = pl.multiple_of(start + (1 - sub) * own, own)
                out_refs[0][step] = result[:, :, pl.ds(mine, own), :]
                out_refs[1][step] = result[:, :, pl.ds(theirs, own), :]

    tables = jnp.asarray(doppler_tables(PULSES))
    if split_sub:
        shape = (sections, 2, gates, own, LANES)
        outs = [jax.ShapeDtypeStruct(shape, F32)] * 2
    else:
        shape = (2, gates, per, LANES)
        outs = [jax.ShapeDtypeStruct(shape, F32)] * sections
    return pl.pallas_call(
        body,
        in_specs=[HBM] * 3,
        out_specs=[VMEM] * len(outs),
        out_shape=outs,
        scratch_shapes=[
            pltpu.VMEM((2, gates, PULSES, LANES), F32),
            pltpu.VMEM((PULSES, LANES), F32),
            pltpu.VMEM((view.shape[0], 2) + view.shape[2:], F32),
            pltpu.VMEM(taper.shape, F32),
            pltpu.VMEM(tables.shape, BF16),
            pltpu.SemaphoreType.DMA((4,)),
        ],
        compiler_params=pltpu.CompilerParams(vmem_limit_bytes=LIMIT),
    )(*[pltpu.with_memory_space_constraint(v, pltpu.HBM) for v in (view, taper, tables)])


def gather_sub(blocks):
    sections = len(blocks)
    _, gates, per, _ = blocks[0].shape
    own = per // 2

    def body(*refs):
        section, sub = lax.axis_index("section"), lax.axis_index("sub")
        mine = pl.multiple_of(sub * own, own)
        theirs = pl.multiple_of((1 - sub) * own, own)
        for step in range(sections):
            source = jnp.bitwise_xor(section, step)
            refs[sections][source] = refs[step][:, :, pl.ds(mine, own), :]
            refs[sections + 1][source] = refs[step][:, :, pl.ds(theirs, own), :]

    shape = jax.ShapeDtypeStruct((sections, 2, gates, own, LANES), F32)
    return pl.pallas_call(
        body,
        in_specs=[VMEM] * sections,
        out_specs=[VMEM] * 2,
        out_shape=[shape] * 2,
        compiler_params=pltpu.CompilerParams(vmem_limit_bytes=LIMIT),
        name="gather_sub",
    )(*blocks)


def pair_up(mine, other):
    sections = mine.shape[0]

    def body(mine_ref, other_ref, *out_refs):
        for step in range(sections):
            out_refs[step][0] = mine_ref[step]
            out_refs[step][1] = other_ref[step]

    shape = jax.ShapeDtypeStruct((2,) + mine.shape[1:], F32)
    return pl.pallas_call(
        body,
        in_specs=[VMEM] * 2,
        out_specs=[VMEM] * sections,
        out_shape=[shape] * sections,
        compiler_params=pltpu.CompilerParams(vmem_limit_bytes=LIMIT),
        name="pair_up",
    )(mine, other)


def filter_matrix(taps_ref, gates, sections, conjugate):
    count = gates * sections
    side = 2 * count
    taps = taps_ref.shape[1]
    row = lax.broadcasted_iota(jnp.int32, (side, side), 0)
    column = lax.broadcasted_iota(jnp.int32, (side, side), 1)
    row_imag, column_imag = row >= count, column >= count
    row_gate = jnp.where(row_imag, row - count, row)
    place = jnp.where(column_imag, column - count, column)
    inner = sum(jnp.where(place >= gate * sections, 1, 0) for gate in range(1, gates))
    column_gate = (place - inner * sections) * gates + inner
    tap = column_gate - row_gate + taps // 2
    real = sum(jnp.where(tap == j, taps_ref[0, j], 0.0) for j in range(taps))
    imag = sum(jnp.where(tap == j, taps_ref[1, j], 0.0) for j in range(taps))
    straight, crossed = row_imag == column_imag, jnp.where(row_imag, imag, -imag)
    matrix = jnp.where(straight, real, crossed)
    if conjugate:
        matrix = jnp.where(row_imag, -matrix, matrix)
    return split(matrix)


def stacked(product, left, right):
    rows = left[0].shape[0]
    both = product(jnp.concatenate(left, axis=0), right[0])
    return both[:rows] + (both[rows:] + product(left[0], right[1]))


def beside(value, negate_first):
    count = value.shape[0] // 2
    real, imag = value[:count], value[count:]
    if negate_first:
        return jnp.concatenate(
            [jnp.concatenate([real, -imag], axis=1), jnp.concatenate([imag, real], axis=1)], axis=0
        )
    return jnp.concatenate(
        [jnp.concatenate([real, imag], axis=1), jnp.concatenate([-imag, real], axis=1)], axis=0
    )


def weights_kernel(mine, other, steer, range_taps, loading):
    sections, _, gates, own, _ = mine.shape
    count = sections * gates
    side = 2 * count
    channels = 2 * LANES
    beams = steer.shape[1] // 2
    stride = 2 * gates * own
    mine = mine.reshape(sections * stride, LANES)
    other = other.reshape(sections * stride, LANES)

    def body(mine_ref, other_ref, steer_ref, taps_ref, load_ref,
             bh_ref, bl_ref, th_ref, tl_ref, gain_ref,
             ah_ref, al_ref, rows_ref, sums_ref, squares_ref, u_ref, gram_ref):
        matrix = filter_matrix(taps_ref, gates, sections, True)
        for index in range(own):
            def load(ref):
                return jnp.concatenate(
                    [ref[pl.ds((part * gates + gate) * own + index, sections, stride=stride), :]
                     for part in (0, 1) for gate in range(gates)], axis=0)

            data = jnp.concatenate([load(mine_ref), load(other_ref)], axis=1)
            value = stacked(dot, matrix, split(data))
            squares_ref[index : index + 1, :] = jnp.sum(value * value, axis=0, keepdims=True)
            high, low = split(value)
            ah_ref[index] = high
            al_ref[index] = low
            bh_ref[index] = beside(high, False)
            bl_ref[index] = beside(low, False)
            here = slice(index * count, (index + 1) * count)
            for place, part in enumerate((high, low, high)):
                lanes = slice(place * 2 * channels, (place + 1) * 2 * channels)
                rows_ref[here, lanes] = jnp.concatenate([part[:count], part[count:]], axis=1)
        for index in range(own):
            high, low = ah_ref[index], al_ref[index]
            turn = lambda v: jnp.concatenate(
                [v, jnp.concatenate([v[count:], -v[:count]], axis=0)], axis=1
            )
            rh, rl = turn(high), turn(low)
            left = jnp.concatenate([high, high, low], axis=0)
            right = jnp.concatenate([rh, rl, rh], axis=0)
            cov = jnp.abs(dot_tn(left, right))
            sums_ref[index : index + 1, :] = jnp.sum(
                cov[:, :channels] + cov[:, channels:], axis=0, keepdims=True
            )
        bound = jnp.max(sums_ref[...], axis=1, keepdims=True) / count
        trace = jnp.sum(squares_ref[...], axis=1, keepdims=True) / count
        delta = load_ref[0] * trace / channels
        bound = bound + delta
        ratio = 1.0 - delta / bound
        first = 1.0 + ratio * (1.0 + ratio * (1.0 + ratio))
        second = 1.0 + ratio * (2.0 + 3.0 * ratio)
        third = 1.0 + 3.0 * ratio
        norm = 1.0 / (count * bound)
        u_ref[...] = dot(rows_ref[...], steer_ref[...])
        low_at = 2 * 2 * channels
        table = steer_ref[:channels, :].astype(F32) + steer_ref[low_at : low_at + channels, :].astype(F32)
        power = jnp.sum(table * table, axis=0, keepdims=True)
        power = power[:, :beams] + power[:, beams:]
        eye = (
            lax.broadcasted_iota(jnp.int32, (side, side), 0)
            == lax.broadcasted_iota(jnp.int32, (side, side), 1)
        )
        for index in range(own):
            at = slice(index, index + 1)
            halves = beside(ah_ref[index], True), beside(al_ref[index], True)
            gram_ref[index] = stacked(dot_nt, halves, halves) * norm[at]
        for index in range(own):
            at = slice(index, index + 1)
            gram = gram_ref[index]
            parts = split(gram)
            square = stacked(dot, parts, parts)
            quad = jnp.where(eye, second[at], 0.0) - third[at] * gram + square
            gram_ref[index] = quad * (norm[at] / first[at])
        for index in range(own):
            u = u_ref[index * count : (index + 1) * count, :]
            up = jnp.concatenate([u[:, :beams], u[:, beams:]], axis=0)
            value = stacked(dot, split(gram_ref[index]), split(up))
            high, low = split(value)
            th_ref[index] = beside(high, False)
            tl_ref[index] = beside(low, False)
            sums_ref[index : index + 1, :] = jnp.sum(up * value, axis=0, keepdims=True)
        gain = power - sums_ref[...]
        gain_ref[...] = 1.0 / (gain * gain)

    wide = jax.ShapeDtypeStruct((own, side, 2 * channels), BF16)
    turned = jax.ShapeDtypeStruct((own, side, 2 * beams), BF16)
    return pl.pallas_call(
        body,
        in_specs=[VMEM] * 3 + [SMEM] * 2,
        out_specs=[VMEM] * 5,
        out_shape=[wide, wide, turned, turned, jax.ShapeDtypeStruct((own, beams), F32)],
        scratch_shapes=[
            pltpu.VMEM((own, side, channels), BF16),
            pltpu.VMEM((own, side, channels), BF16),
            pltpu.VMEM((own * count, 6 * channels), BF16),
            pltpu.VMEM((own, channels), F32),
            pltpu.VMEM((own, channels), F32),
            pltpu.VMEM((own * count, 2 * beams), F32),
            pltpu.VMEM((own, side, side), F32),
        ],
        compiler_params=pltpu.CompilerParams(vmem_limit_bytes=LIMIT),
        name="weights",
    )(mine, other, steer, range_taps, loading)


def beams_kernel(blocks, weights, steer, range_taps):
    sections = len(blocks)
    _, _, gates, own, _ = blocks[0].shape
    size = 4 * gates * own
    pitch = size + PAD
    count = sections * gates
    side = 2 * count
    channels = 2 * LANES
    beams = steer.shape[1] // 2
    blocks = [block.reshape(size, LANES) for block in blocks]

    def body(*refs):
        block_refs = refs[:sections]
        (bh_ref, bl_ref, th_ref, tl_ref, gain_ref, steer_ref, taps_ref,
         power_ref, total_ref, held, rows_ref, v_ref, cross_ref) = refs[sections:]
        section = lax.axis_index("section")
        for step in range(sections):
            start = pl.multiple_of(jnp.bitwise_xor(section, step) * pitch, 8)
            held[pl.ds(start, size), :] = block_refs[step][...]
        matrix = filter_matrix(taps_ref, gates, sections, False)
        wide = 2 * channels
        for index in range(own):
            def load(half, part):
                return jnp.concatenate(
                    [held[pl.ds(((half * 2 + part) * gates + gate) * own + index, sections, stride=pitch), :]
                     for gate in range(gates)], axis=0)

            data = jnp.concatenate([load(half, part) for part in (0, 1) for half in (0, 1)], axis=1)
            high, low = split(data)
            here = slice(index * count, (index + 1) * count)
            for place, part in enumerate((high, low, high)):
                rows_ref[here, place * wide : (place + 1) * wide] = part
        for index in range(own):
            here = slice(index * count, (index + 1) * count)
            parts = rows_ref[here, :wide], rows_ref[here, wide : 2 * wide]
            cross_ref[index] = stacked(dot_nt, parts, (bh_ref[index], bl_ref[index]))
        v_ref[...] = dot(rows_ref[...], steer_ref[...])
        for index in range(own):
            here = slice(index * count, (index + 1) * count)
            low_rank = stacked(dot, split(cross_ref[index]), (th_ref[index], tl_ref[index]))
            v_ref[here, :] = v_ref[here, :] - low_rank
        total = jnp.zeros((1, beams), F32)
        for index in range(own):
            v = v_ref[index * count : (index + 1) * count, :]
            up = jnp.concatenate([v[:, :beams], v[:, beams:]], axis=0)
            out = stacked(dot, matrix, split(up))
            power = (out[:count] * out[:count] + out[count:] * out[count:]) * gain_ref[index : index + 1, :]
            total = total + jnp.sum(power, axis=0, keepdims=True)
            power_ref[index] = power
        total_ref[...] = jnp.broadcast_to(total, total_ref.shape)

    return pl.pallas_call(
        body,
        in_specs=[VMEM] * (sections + 6) + [SMEM],
        out_specs=[VMEM] * 2,
        out_shape=[
            jax.ShapeDtypeStruct((own, count, beams), F32),
            jax.ShapeDtypeStruct((2 * sections, beams), F32),
        ],
        scratch_shapes=[
            pltpu.VMEM((sections * pitch, LANES), F32),
            pltpu.VMEM((own * count, 6 * channels), BF16),
            pltpu.VMEM((own * count, 2 * beams), F32),
            pltpu.VMEM((own, count, side), F32),
        ],
        compiler_params=pltpu.CompilerParams(vmem_limit_bytes=LIMIT),
        name="beams",
    )(*blocks, *weights, steer, range_taps)


def steering_tables(beam_index, channel_phase):
    channels = channel_phase.shape[0]
    own = channels // 2
    sub = lax.axis_index("sub")
    place = jnp.arange(channels, dtype=jnp.int32)
    place = jnp.where(place + sub * own >= channels, place + sub * own - channels, place + sub * own)
    turned = jnp.concatenate([channel_phase[own:], channel_phase[:own]])
    phase = jnp.where(sub == 0, channel_phase, turned)
    direction = -1.0 + (2.0 * beam_index.astype(F32) + 1.0) / LOOKS
    angle = math.pi * place.astype(F32)[:, None] * direction[None, :] + phase[:, None]
    cosine, sine = jnp.cos(angle), jnp.sin(angle)
    table = jnp.concatenate(
        [jnp.concatenate([cosine, -sine], 1), jnp.concatenate([sine, cosine], 1)], 0
    )
    high = lax.reduce_precision(table, 8, 7)
    low = lax.reduce_precision(table - high, 8, 7).astype(BF16)
    high = high.astype(BF16)
    return jnp.concatenate([high, high, low], 0)


def permuted(block, sections, step):
    return lax.ppermute(block, "section", [(place, place ^ step) for place in range(sections)])


def swapped(block):
    return lax.ppermute(block, "sub", [(0, 1), (1, 0)])


def factored_steps(echoes, range_taps, pulse_taper, channel_phase, loading, beam_index):
    parts, pulses, gates, lanes = echoes.shape
    sections = lax.axis_size("section")
    order = sorted(range(1, sections), reverse=True)
    view = echoes.reshape(parts, pulses // HOP, HOP * gates, lanes)
    taper = pulse_taper.reshape(2, HOP)

    sent = doppler(view, taper, sections, 0, False)
    got = {0: sent[0]}
    for step in order:
        got[step] = permuted(sent[step], sections, step)
    mine, theirs = doppler(view, taper, sections, 1, True)
    other = swapped(theirs)
    sent = pair_up(mine, other)
    later = {0: sent[0]}
    for step in order:
        later[step] = permuted(sent[step], sections, step)

    steer = steering_tables(beam_index, channel_phase)
    keep, pass_on = gather_sub([got[step] for step in range(sections)])
    other = swapped(pass_on)
    weights = weights_kernel(keep, other, steer, range_taps, loading)
    power, total = beams_kernel(
        [later[step] for step in range(sections)], weights, steer, range_taps
    )
    totals = lax.all_to_all(total, ("section", "sub"), 0, 0, tiled=True)
    noise_level = jnp.sum(totals, axis=0) / (PULSES * gates * sections)
    return (power / (noise_level + epsilon))[None]


def apply_taps(pad_real, pad_imag, range_taps, gate_count):
    axis_gates = pad_real.ndim - 2
    shape_out = pad_real.shape[:axis_gates] + (gate_count,) + pad_real.shape[axis_gates + 1 :]
    out_real = jnp.zeros(shape_out, jnp.float32)
    out_imag = jnp.zeros(shape_out, jnp.float32)
    for offset in range(range_taps.shape[1]):
        part_real = lax.slice_in_dim(pad_real, offset, offset + gate_count, axis=axis_gates)
        part_imag = lax.slice_in_dim(pad_imag, offset, offset + gate_count, axis=axis_gates)
        out_real = out_real + range_taps[0, offset] * part_real - range_taps[1, offset] * part_imag
        out_imag = out_imag + range_taps[0, offset] * part_imag + range_taps[1, offset] * part_real
    return (out_real, out_imag)


def doppler_table(pulse_taper):
    pulse_count = pulse_taper.shape[0]
    pulse_index = jnp.arange(pulse_count, dtype=jnp.int32)
    product = pulse_index[:, None] * pulse_index[None, :] % pulse_count
    phase_angle = 2.0 * math.pi / pulse_count * product.astype(jnp.float32)
    cosine = jnp.cos(phase_angle) * pulse_taper[None, :]
    sine_part = jnp.sin(phase_angle) * pulse_taper[None, :]
    upper_rows = jnp.concatenate([cosine, sine_part], axis=1)
    lower_rows = jnp.concatenate([-sine_part, cosine], axis=1)
    return jnp.concatenate([upper_rows, lower_rows], axis=0)


def transform(doppler, segment):
    shape_in = segment.shape
    flattened = segment.reshape(shape_in[0] * shape_in[1], -1)
    result = jnp.dot(doppler, flattened, precision=precise, preferred_element_type=jnp.float32)
    return result.reshape(shape_in)


def batched(first, second):
    return jnp.einsum("dij,djk->dik", first, second, precision=precise)


def complex_product(left_real, left_imag, right_real, right_imag):
    out_real = batched(left_real, right_real) - batched(left_imag, right_imag)
    out_imag = batched(left_real, right_imag) + batched(left_imag, right_real)
    return (out_real, out_imag)


def gram_product(first, second):
    return jnp.einsum("dgi,dgj->dij", first, second, precision=precise)


def loaded_inverse(real_part, imag_part, loading):
    gate_count = real_part.shape[1]
    channels = real_part.shape[2]
    cov_real = (
        gram_product(real_part, real_part) + gram_product(imag_part, imag_part)
    ) / gate_count
    cov_imag = (
        gram_product(real_part, imag_part) - gram_product(imag_part, real_part)
    ) / gate_count
    identity = jnp.eye(channels, dtype=jnp.float32)
    trace_sum = jnp.sum(cov_real * identity[None], axis=(1, 2))
    cov_real = cov_real + (loading[0] * trace_sum / channels)[:, None, None] * identity[None]
    row_bound = jnp.max(jnp.sum(jnp.abs(cov_real) + jnp.abs(cov_imag), axis=2), axis=1)
    inv_real = identity[None] / row_bound[:, None, None]
    inv_imag = jnp.zeros_like(inv_real)
    for _ in range(ITERS):
        prod_real, prod_imag = complex_product(cov_real, cov_imag, inv_real, inv_imag)
        inv_real, inv_imag = complex_product(
            inv_real, inv_imag, 2.0 * identity[None] - prod_real, -prod_imag
        )
    return (inv_real, inv_imag)


def steering(beam_index, channel_phase):
    channels = channel_phase.shape[0]
    direction = -1.0 + (2.0 * beam_index.astype(jnp.float32) + 1.0) / LOOKS
    phase_angle = (
        math.pi * jnp.arange(channels, dtype=jnp.float32)[:, None] * direction[None, :]
        + channel_phase[:, None]
    )
    return (jnp.cos(phase_angle), jnp.sin(phase_angle))


def beam_weights(inv_real, inv_imag, steer_real, steer_imag):
    weight_real = jnp.einsum("dij,jb->dib", inv_real, steer_real, precision=precise) - jnp.einsum(
        "dij,jb->dib", inv_imag, steer_imag, precision=precise
    )
    weight_imag = jnp.einsum("dij,jb->dib", inv_real, steer_imag, precision=precise) + jnp.einsum(
        "dij,jb->dib", inv_imag, steer_real, precision=precise
    )
    gain_norm = jnp.sum(steer_real[None] * weight_real + steer_imag[None] * weight_imag, axis=1)
    return (weight_real / gain_norm[:, None, :], weight_imag / gain_norm[:, None, :])


def form_beams(data_real, data_imag, weight_real, weight_imag):
    out_real = jnp.einsum("dgc,dcb->dgb", data_real, weight_real, precision=precise) + jnp.einsum(
        "dgc,dcb->dgb", data_imag, weight_imag, precision=precise
    )
    out_imag = jnp.einsum("dgc,dcb->dgb", data_imag, weight_real, precision=precise) - jnp.einsum(
        "dgc,dcb->dgb", data_real, weight_imag, precision=precise
    )
    return out_real * out_real + out_imag * out_imag


def on_device(echoes, range_taps, pulse_taper, channel_phase, loading, beam_index):
    rim_width = range_taps.shape[1] // 2
    doppler = doppler_table(pulse_taper)
    spectra = [
        transform(
            doppler, lax.slice_in_dim(echoes, interval * HOP, interval * HOP + PULSES, axis=1)
        )
        for interval in range(INTERVALS)
    ]
    turned = [
        lax.all_to_all(
            lax.all_to_all(spectrum, "section", split_axis=1, concat_axis=2, tiled=True),
            "sub",
            split_axis=1,
            concat_axis=3,
            tiled=True,
        )
        for spectrum in spectra
    ]
    refined = []
    for spectrum in turned:
        padded_bins = jnp.pad(spectrum, ((0, 0), (0, 0), (rim_width, rim_width), (0, 0)))
        part_real, part_imag = apply_taps(
            padded_bins[0], padded_bins[1], range_taps, spectrum.shape[2]
        )
        refined.append(jnp.stack([part_real, part_imag]))
    turned = refined
    steer_real, steer_imag = steering(beam_index, channel_phase)
    interval = 0
    inv_real, inv_imag = loaded_inverse(turned[interval][0], turned[interval][1], loading)
    weight_real, weight_imag = beam_weights(inv_real, inv_imag, steer_real, steer_imag)
    beam_power = form_beams(
        turned[interval + 1][0], turned[interval + 1][1], weight_real, weight_imag
    )
    partials = [jnp.sum(beam_power, axis=(0, 1))]
    totals = lax.psum(jnp.stack(partials), ("section", "sub"))
    noise_level = totals / (PULSES * turned[0].shape[2])
    return jnp.stack([beam_power / (noise_level[0] + epsilon)])


def solution(mesh):
    in_specs = (P("groups", None, "section", "sub"), P(), P(), P(), P(), P())
    out_specs = P("groups", ("section", "sub"), None, None)
    sections = mesh.shape["section"]
    small = sections == 8 and mesh.shape["sub"] == 2

    def run(echoes, range_taps, pulse_taper, channel_phase, loading, beam_index):
        args = (echoes, range_taps, pulse_taper, channel_phase, loading, beam_index)
        fits = small and echoes.shape[2] == 4 and echoes.shape[3] == LANES
        return factored_steps(*args) if fits else on_device(*args)

    return jax.shard_map(run, mesh=mesh, in_specs=in_specs, out_specs=out_specs, check_vma=False)
```

```python
import math

import jax
import jax.numpy as jnp
import numpy as np
from jax import lax
from jax.experimental import pallas as pl
from jax.experimental.pallas import tpu as pltpu
from jax.sharding import PartitionSpec as P


PULSES = 256
INTERVALS = 2
ITERS = 2
LOOKS = 1024
HOP = 128


precise = lax.Precision.HIGHEST
epsilon = 1e-06
F32 = jnp.float32
BF16 = jnp.bfloat16
LANES = 128
VMEM = pl.BlockSpec(memory_space=pltpu.VMEM)
SMEM = pl.BlockSpec(memory_space=pltpu.SMEM)
HBM = pl.BlockSpec(memory_space=pltpu.HBM)
LIMIT = 16 << 20
PAD = 8


def split(value):
    high = value.astype(BF16)
    return high, (value - high.astype(F32)).astype(BF16)


def dot(left, right):
    return jnp.dot(left, right, preferred_element_type=F32)


def dot_nt(left, right):
    return lax.dot_general(left, right, (((1,), (1,)), ((), ())), preferred_element_type=F32)


def dot_tn(left, right):
    return lax.dot_general(left, right, (((0,), (0,)), ((), ())), preferred_element_type=F32)


def triple(product, left, right):
    return product(left[0], right[0]) + (product(left[0], right[1]) + product(left[1], right[0]))


def doppler_tables(pulses):
    half = pulses // 2
    bins = np.arange(half)[:, None]
    tables = []
    for parity in (0, 1):
        phase = 2.0 * np.pi * ((bins * np.arange(parity, pulses, 2)[None, :]) % pulses) / pulses
        cosine, sine = np.cos(phase), np.sin(phase)
        table = np.concatenate([cosine, sine], 1).astype(np.float32)
        high = table.astype(jnp.bfloat16)
        tables += [high, (table - high.astype(np.float32)).astype(jnp.bfloat16)]
    return np.stack(tables)


def full_table(rows):
    half = rows.shape[1] // 2
    turned = jnp.concatenate([-rows[:, half:], rows[:, :half]], axis=1)
    return jnp.concatenate([rows, turned], axis=0)


def doppler_body(gates, hop, view_ref, taper_ref, table_ref, result, tapers):
    half = hop
    for segment in (0, 1):
        row = taper_ref[segment : segment + 1, :]
        tapers[segment * hop : (segment + 1) * hop, :] = jnp.broadcast_to(row, (hop, hop)).T
    for group in range(0, gates, 2):
        members = range(group, min(group + 2, gates))
        for parity in (0, 1):
            rows = []
            for part in (0, 1):
                for segment in (0, 1):
                    taper = tapers[pl.ds(segment * hop + parity, hop // 2, stride=2), :]
                    blocks = []
                    for gate in members:
                        at = pl.ds(parity * gates + gate, hop // 2, stride=2 * gates)
                        blocks.append(view_ref[part, segment, at, :] * taper)
                    rows.append(jnp.concatenate(blocks, axis=1))
            data = split(jnp.concatenate(rows, axis=0))
            table = full_table(table_ref[2 * parity]), full_table(table_ref[2 * parity + 1])
            value = triple(dot, table, data)
            if parity == 0:
                even = value
        for place, gate in enumerate(members):
            lanes = slice(place * LANES, (place + 1) * LANES)
            for part in (0, 1):
                own = slice(part * half, (part + 1) * half)
                result[part, gate, :half] = even[own, lanes] + value[own, lanes]
                result[part, gate, half:] = even[own, lanes] - value[own, lanes]


def doppler(view, taper, sections, interval, split_sub):
    gates = view.shape[2] // HOP
    per = PULSES // sections
    own = per // 2

    def body(view_ref, taper_ref, table_ref, *rest):
        outs = 2 if split_sub else sections
        out_refs, scratch = rest[:outs], rest[outs:]
        result, tapers, own_view, own_taper, own_table, sems = scratch
        copies = [pltpu.make_async_copy(taper_ref, own_taper, sems.at[0])]
        copies.append(pltpu.make_async_copy(table_ref, own_table, sems.at[1]))
        for part in (0, 1):
            blocks = view_ref.at[part, pl.ds(interval, 2)]
            copies.append(pltpu.make_async_copy(blocks, own_view.at[part], sems.at[2 + part]))
        for copy in copies:
            copy.start()
        for copy in copies:
            copy.wait()
        doppler_body(gates, HOP, own_view, own_taper, own_table, result, tapers)
        section = lax.axis_index("section")
        if not split_sub:
            for step in range(sections):
                start = pl.multiple_of(jnp.bitwise_xor(section, step) * per, per)
                out_refs[step][...] = result[:, :, pl.ds(start, per), :]
        else:
            sub = lax.axis_index("sub")
            for step in range(sections):
                start = jnp.bitwise_xor(section, step) * per
                mine = pl.multiple_of(start + sub * own, own)
                theirs = pl.multiple_of(start + (1 - sub) * own, own)
                out_refs[0][step] = result[:, :, pl.ds(mine, own), :]
                out_refs[1][step] = result[:, :, pl.ds(theirs, own), :]

    tables = jnp.asarray(doppler_tables(PULSES))
    if split_sub:
        shape = (sections, 2, gates, own, LANES)
        outs = [jax.ShapeDtypeStruct(shape, F32)] * 2
    else:
        shape = (2, gates, per, LANES)
        outs = [jax.ShapeDtypeStruct(shape, F32)] * sections
    return pl.pallas_call(
        body,
        in_specs=[HBM] * 3,
        out_specs=[VMEM] * len(outs),
        out_shape=outs,
        scratch_shapes=[
            pltpu.VMEM((2, gates, PULSES, LANES), F32),
            pltpu.VMEM((PULSES, LANES), F32),
            pltpu.VMEM((view.shape[0], 2) + view.shape[2:], F32),
            pltpu.VMEM(taper.shape, F32),
            pltpu.VMEM(tables.shape, BF16),
            pltpu.SemaphoreType.DMA((4,)),
        ],
        compiler_params=pltpu.CompilerParams(vmem_limit_bytes=LIMIT),
    )(*[pltpu.with_memory_space_constraint(v, pltpu.HBM) for v in (view, taper, tables)])


def gather_sub(blocks):
    sections = len(blocks)
    _, gates, per, _ = blocks[0].shape
    own = per // 2

    def body(*refs):
        section, sub = lax.axis_index("section"), lax.axis_index("sub")
        mine = pl.multiple_of(sub * own, own)
        theirs = pl.multiple_of((1 - sub) * own, own)
        for step in range(sections):
            source = jnp.bitwise_xor(section, step)
            refs[sections][source] = refs[step][:, :, pl.ds(mine, own), :]
            refs[sections + 1][source] = refs[step][:, :, pl.ds(theirs, own), :]

    shape = jax.ShapeDtypeStruct((sections, 2, gates, own, LANES), F32)
    return pl.pallas_call(
        body,
        in_specs=[VMEM] * sections,
        out_specs=[VMEM] * 2,
        out_shape=[shape] * 2,
        compiler_params=pltpu.CompilerParams(vmem_limit_bytes=LIMIT),
        name="gather_sub",
    )(*blocks)


def pair_up(mine, other):
    sections = mine.shape[0]

    def body(mine_ref, other_ref, *out_refs):
        for step in range(sections):
            out_refs[step][0] = mine_ref[step]
            out_refs[step][1] = other_ref[step]

    shape = jax.ShapeDtypeStruct((2,) + mine.shape[1:], F32)
    return pl.pallas_call(
        body,
        in_specs=[VMEM] * 2,
        out_specs=[VMEM] * sections,
        out_shape=[shape] * sections,
        compiler_params=pltpu.CompilerParams(vmem_limit_bytes=LIMIT),
        name="pair_up",
    )(mine, other)


def filter_matrix(taps_ref, gates, sections, conjugate):
    count = gates * sections
    side = 2 * count
    taps = taps_ref.shape[1]
    row = lax.broadcasted_iota(jnp.int32, (side, side), 0)
    column = lax.broadcasted_iota(jnp.int32, (side, side), 1)
    row_imag, column_imag = row >= count, column >= count
    row_gate = jnp.where(row_imag, row - count, row)
    place = jnp.where(column_imag, column - count, column)
    inner = sum(jnp.where(place >= gate * sections, 1, 0) for gate in range(1, gates))
    column_gate = (place - inner * sections) * gates + inner
    tap = column_gate - row_gate + taps // 2
    real = sum(jnp.where(tap == j, taps_ref[0, j], 0.0) for j in range(taps))
    imag = sum(jnp.where(tap == j, taps_ref[1, j], 0.0) for j in range(taps))
    straight, crossed = row_imag == column_imag, jnp.where(row_imag, imag, -imag)
    matrix = jnp.where(straight, real, crossed)
    if conjugate:
        matrix = jnp.where(row_imag, -matrix, matrix)
    return split(matrix)


def stacked(product, left, right):
    rows = left[0].shape[0]
    both = product(jnp.concatenate(left, axis=0), right[0])
    return both[:rows] + (both[rows:] + product(left[0], right[1]))


def beside(value, negate_first):
    count = value.shape[0] // 2
    real, imag = value[:count], value[count:]
    if negate_first:
        return jnp.concatenate(
            [jnp.concatenate([real, -imag], axis=1), jnp.concatenate([imag, real], axis=1)], axis=0
        )
    return jnp.concatenate(
        [jnp.concatenate([real, imag], axis=1), jnp.concatenate([-imag, real], axis=1)], axis=0
    )


def weights_kernel(mine, other, steer, range_taps, loading):
    sections, _, gates, own, _ = mine.shape
    count = sections * gates
    side = 2 * count
    channels = 2 * LANES
    beams = steer.shape[1] // 2
    stride = 2 * gates * own
    mine = mine.reshape(sections * stride, LANES)
    other = other.reshape(sections * stride, LANES)

    def body(mine_ref, other_ref, steer_ref, taps_ref, load_ref,
             bh_ref, bl_ref, th_ref, tl_ref, gain_ref,
             ah_ref, al_ref, rows_ref, sums_ref, squares_ref, u_ref, gram_ref):
        matrix = filter_matrix(taps_ref, gates, sections, True)
        for index in range(own):
            def load(ref):
                return jnp.concatenate(
                    [ref[pl.ds((part * gates + gate) * own + index, sections, stride=stride), :]
                     for part in (0, 1) for gate in range(gates)], axis=0)

            data = jnp.concatenate([load(mine_ref), load(other_ref)], axis=1)
            value = stacked(dot, matrix, split(data))
            squares_ref[index : index + 1, :] = jnp.sum(value * value, axis=0, keepdims=True)
            high, low = split(value)
            ah_ref[index] = high
            al_ref[index] = low
            bh_ref[index] = beside(high, False)
            bl_ref[index] = beside(low, False)
            here = slice(index * count, (index + 1) * count)
            for place, part in enumerate((high, low, high)):
                lanes = slice(place * 2 * channels, (place + 1) * 2 * channels)
                rows_ref[here, lanes] = jnp.concatenate([part[:count], part[count:]], axis=1)
        for index in range(own):
            high, low = ah_ref[index], al_ref[index]
            turn = lambda v: jnp.concatenate(
                [v, jnp.concatenate([v[count:], -v[:count]], axis=0)], axis=1
            )
            rh, rl = turn(high), turn(low)
            left = jnp.concatenate([high, high, low], axis=0)
            right = jnp.concatenate([rh, rl, rh], axis=0)
            cov = jnp.abs(dot_tn(left, right))
            sums_ref[index : index + 1, :] = jnp.sum(
                cov[:, :channels] + cov[:, channels:], axis=0, keepdims=True
            )
        bound = jnp.max(sums_ref[...], axis=1, keepdims=True) / count
        trace = jnp.sum(squares_ref[...], axis=1, keepdims=True) / count
        delta = load_ref[0] * trace / channels
        bound = bound + delta
        ratio = 1.0 - delta / bound
        first = 1.0 + ratio * (1.0 + ratio * (1.0 + ratio))
        second = 1.0 + ratio * (2.0 + 3.0 * ratio)
        third = 1.0 + 3.0 * ratio
        norm = 1.0 / (count * bound)
        u_ref[...] = dot(rows_ref[...], steer_ref[...])
        low_at = 2 * 2 * channels
        table = steer_ref[:channels, :].astype(F32) + steer_ref[low_at : low_at + channels, :].astype(F32)
        power = jnp.sum(table * table, axis=0, keepdims=True)
        power = power[:, :beams] + power[:, beams:]
        eye = (
            lax.broadcasted_iota(jnp.int32, (side, side), 0)
            == lax.broadcasted_iota(jnp.int32, (side, side), 1)
        )
        for index in range(own):
            at = slice(index, index + 1)
            halves = beside(ah_ref[index], True), beside(al_ref[index], True)
            gram_ref[index] = stacked(dot_nt, halves, halves) * norm[at]
        for index in range(own):
            at = slice(index, index + 1)
            gram = gram_ref[index]
            parts = split(gram)
            square = stacked(dot, parts, parts)
            quad = jnp.where(eye, second[at], 0.0) - third[at] * gram + square
            gram_ref[index] = quad * (norm[at] / first[at])
        for index in range(own):
            u = u_ref[index * count : (index + 1) * count, :]
            up = jnp.concatenate([u[:, :beams], u[:, beams:]], axis=0)
            value = stacked(dot, split(gram_ref[index]), split(up))
            high, low = split(value)
            th_ref[index] = beside(high, False)
            tl_ref[index] = beside(low, False)
            sums_ref[index : index + 1, :] = jnp.sum(up * value, axis=0, keepdims=True)
        gain = power - sums_ref[...]
        gain_ref[...] = 1.0 / (gain * gain)

    wide = jax.ShapeDtypeStruct((own, side, 2 * channels), BF16)
    turned = jax.ShapeDtypeStruct((own, side, 2 * beams), BF16)
    return pl.pallas_call(
        body,
        in_specs=[VMEM] * 3 + [SMEM] * 2,
        out_specs=[VMEM] * 5,
        out_shape=[wide, wide, turned, turned, jax.ShapeDtypeStruct((own, beams), F32)],
        scratch_shapes=[
            pltpu.VMEM((own, side, channels), BF16),
            pltpu.VMEM((own, side, channels), BF16),
            pltpu.VMEM((own * count, 6 * channels), BF16),
            pltpu.VMEM((own, channels), F32),
            pltpu.VMEM((own, channels), F32),
            pltpu.VMEM((own * count, 2 * beams), F32),
            pltpu.VMEM((own, side, side), F32),
        ],
        compiler_params=pltpu.CompilerParams(vmem_limit_bytes=LIMIT),
        name="weights",
    )(mine, other, steer, range_taps, loading)


def beams_kernel(blocks, weights, steer, range_taps):
    sections = len(blocks)
    _, _, gates, own, _ = blocks[0].shape
    size = 4 * gates * own
    pitch = size + PAD
    count = sections * gates
    side = 2 * count
    channels = 2 * LANES
    beams = steer.shape[1] // 2
    blocks = [block.reshape(size, LANES) for block in blocks]

    def body(*refs):
        block_refs = refs[:sections]
        (bh_ref, bl_ref, th_ref, tl_ref, gain_ref, steer_ref, taps_ref,
         power_ref, total_ref, held, rows_ref, v_ref, cross_ref) = refs[sections:]
        section = lax.axis_index("section")
        for step in range(sections):
            start = pl.multiple_of(jnp.bitwise_xor(section, step) * pitch, 8)
            held[pl.ds(start, size), :] = block_refs[step][...]
        matrix = filter_matrix(taps_ref, gates, sections, False)
        matrix = jnp.concatenate([matrix[0], matrix[1], matrix[0]], axis=1)
        wide = 2 * channels
        for index in range(own):
            def load(half, part):
                return jnp.concatenate(
                    [held[pl.ds(((half * 2 + part) * gates + gate) * own + index, sections, stride=pitch), :]
                     for gate in range(gates)], axis=0)

            data = jnp.concatenate([load(half, part) for part in (0, 1) for half in (0, 1)], axis=1)
            high, low = split(data)
            here = slice(index * count, (index + 1) * count)
            for place, part in enumerate((high, low, high)):
                rows_ref[here, place * wide : (place + 1) * wide] = part
        for index in range(own):
            here = slice(index * count, (index + 1) * count)
            parts = rows_ref[here, :wide], rows_ref[here, wide : 2 * wide]
            cross_ref[index] = stacked(dot_nt, parts, (bh_ref[index], bl_ref[index]))
        v_ref[...] = dot(rows_ref[...], steer_ref[...])
        for index in range(own):
            here = slice(index * count, (index + 1) * count)
            low_rank = stacked(dot, split(cross_ref[index]), (th_ref[index], tl_ref[index]))
            v_ref[here, :] = v_ref[here, :] - low_rank
        total = jnp.zeros((1, beams), F32)
        for index in range(own):
            v = v_ref[index * count : (index + 1) * count, :]
            up = jnp.concatenate([v[:, :beams], v[:, beams:]], axis=0)
            high, low = split(up)
            out = dot(matrix, jnp.concatenate([high, high, low], axis=0))
            power = (out[:count] * out[:count] + out[count:] * out[count:]) * gain_ref[index : index + 1, :]
            total = total + jnp.sum(power, axis=0, keepdims=True)
            power_ref[index] = power
        total_ref[...] = jnp.broadcast_to(total, total_ref.shape)

    return pl.pallas_call(
        body,
        in_specs=[VMEM] * (sections + 6) + [SMEM],
        out_specs=[VMEM] * 2,
        out_shape=[
            jax.ShapeDtypeStruct((own, count, beams), F32),
            jax.ShapeDtypeStruct((2 * sections, beams), F32),
        ],
        scratch_shapes=[
            pltpu.VMEM((sections * pitch, LANES), F32),
            pltpu.VMEM((own * count, 6 * channels), BF16),
            pltpu.VMEM((own * count, 2 * beams), F32),
            pltpu.VMEM((own, count, side), F32),
        ],
        compiler_params=pltpu.CompilerParams(vmem_limit_bytes=LIMIT),
        name="beams",
    )(*blocks, *weights, steer, range_taps)


def steering_tables(beam_index, channel_phase):
    channels = channel_phase.shape[0]
    own = channels // 2
    sub = lax.axis_index("sub")
    place = jnp.arange(channels, dtype=jnp.int32)
    place = jnp.where(place + sub * own >= channels, place + sub * own - channels, place + sub * own)
    turned = jnp.concatenate([channel_phase[own:], channel_phase[:own]])
    phase = jnp.where(sub == 0, channel_phase, turned)
    direction = -1.0 + (2.0 * beam_index.astype(F32) + 1.0) / LOOKS
    angle = math.pi * place.astype(F32)[:, None] * direction[None, :] + phase[:, None]
    cosine, sine = jnp.cos(angle), jnp.sin(angle)
    table = jnp.concatenate(
        [jnp.concatenate([cosine, -sine], 1), jnp.concatenate([sine, cosine], 1)], 0
    )
    high = lax.reduce_precision(table, 8, 7)
    low = lax.reduce_precision(table - high, 8, 7).astype(BF16)
    high = high.astype(BF16)
    return jnp.concatenate([high, high, low], 0)


def permuted(block, sections, step):
    return lax.ppermute(block, "section", [(place, place ^ step) for place in range(sections)])


def swapped(block):
    return lax.ppermute(block, "sub", [(0, 1), (1, 0)])


def hop_order(sections):
    near, far = list(range(1, sections // 2)), list(range(sections // 2, sections))
    return far[::-1] + near[::-1], near[::-1] + far[::-1]


def factored_steps(echoes, range_taps, pulse_taper, channel_phase, loading, beam_index):
    parts, pulses, gates, lanes = echoes.shape
    sections = lax.axis_size("section")
    order = hop_order(sections)[0]
    view = echoes.reshape(parts, pulses // HOP, HOP * gates, lanes)
    taper = pulse_taper.reshape(2, HOP)

    sent = doppler(view, taper, sections, 0, False)
    got = {0: sent[0]}
    for step in order:
        got[step] = permuted(sent[step], sections, step)
    mine, theirs = doppler(view, taper, sections, 1, True)
    other = swapped(theirs)
    sent = pair_up(mine, other)
    later = {0: sent[0]}
    for step in order:
        later[step] = permuted(sent[step], sections, step)

    steer = steering_tables(beam_index, channel_phase)
    keep, pass_on = gather_sub([got[step] for step in range(sections)])
    other = swapped(pass_on)
    weights = weights_kernel(keep, other, steer, range_taps, loading)
    power, total = beams_kernel(
        [later[step] for step in range(sections)], weights, steer, range_taps
    )
    totals = lax.all_to_all(total, ("section", "sub"), 0, 0, tiled=True)
    noise_level = jnp.sum(totals, axis=0) / (PULSES * gates * sections)
    return (power / (noise_level + epsilon))[None]


def apply_taps(pad_real, pad_imag, range_taps, gate_count):
    axis_gates = pad_real.ndim - 2
    shape_out = pad_real.shape[:axis_gates] + (gate_count,) + pad_real.shape[axis_gates + 1 :]
    out_real = jnp.zeros(shape_out, jnp.float32)
    out_imag = jnp.zeros(shape_out, jnp.float32)
    for offset in range(range_taps.shape[1]):
        part_real = lax.slice_in_dim(pad_real, offset, offset + gate_count, axis=axis_gates)
        part_imag = lax.slice_in_dim(pad_imag, offset, offset + gate_count, axis=axis_gates)
        out_real = out_real + range_taps[0, offset] * part_real - range_taps[1, offset] * part_imag
        out_imag = out_imag + range_taps[0, offset] * part_imag + range_taps[1, offset] * part_real
    return (out_real, out_imag)


def doppler_table(pulse_taper):
    pulse_count = pulse_taper.shape[0]
    pulse_index = jnp.arange(pulse_count, dtype=jnp.int32)
    product = pulse_index[:, None] * pulse_index[None, :] % pulse_count
    phase_angle = 2.0 * math.pi / pulse_count * product.astype(jnp.float32)
    cosine = jnp.cos(phase_angle) * pulse_taper[None, :]
    sine_part = jnp.sin(phase_angle) * pulse_taper[None, :]
    upper_rows = jnp.concatenate([cosine, sine_part], axis=1)
    lower_rows = jnp.concatenate([-sine_part, cosine], axis=1)
    return jnp.concatenate([upper_rows, lower_rows], axis=0)


def transform(doppler, segment):
    shape_in = segment.shape
    flattened = segment.reshape(shape_in[0] * shape_in[1], -1)
    result = jnp.dot(doppler, flattened, precision=precise, preferred_element_type=jnp.float32)
    return result.reshape(shape_in)


def batched(first, second):
    return jnp.einsum("dij,djk->dik", first, second, precision=precise)


def complex_product(left_real, left_imag, right_real, right_imag):
    out_real = batched(left_real, right_real) - batched(left_imag, right_imag)
    out_imag = batched(left_real, right_imag) + batched(left_imag, right_real)
    return (out_real, out_imag)


def gram_product(first, second):
    return jnp.einsum("dgi,dgj->dij", first, second, precision=precise)


def loaded_inverse(real_part, imag_part, loading):
    gate_count = real_part.shape[1]
    channels = real_part.shape[2]
    cov_real = (
        gram_product(real_part, real_part) + gram_product(imag_part, imag_part)
    ) / gate_count
    cov_imag = (
        gram_product(real_part, imag_part) - gram_product(imag_part, real_part)
    ) / gate_count
    identity = jnp.eye(channels, dtype=jnp.float32)
    trace_sum = jnp.sum(cov_real * identity[None], axis=(1, 2))
    cov_real = cov_real + (loading[0] * trace_sum / channels)[:, None, None] * identity[None]
    row_bound = jnp.max(jnp.sum(jnp.abs(cov_real) + jnp.abs(cov_imag), axis=2), axis=1)
    inv_real = identity[None] / row_bound[:, None, None]
    inv_imag = jnp.zeros_like(inv_real)
    for _ in range(ITERS):
        prod_real, prod_imag = complex_product(cov_real, cov_imag, inv_real, inv_imag)
        inv_real, inv_imag = complex_product(
            inv_real, inv_imag, 2.0 * identity[None] - prod_real, -prod_imag
        )
    return (inv_real, inv_imag)


def steering(beam_index, channel_phase):
    channels = channel_phase.shape[0]
    direction = -1.0 + (2.0 * beam_index.astype(jnp.float32) + 1.0) / LOOKS
    phase_angle = (
        math.pi * jnp.arange(channels, dtype=jnp.float32)[:, None] * direction[None, :]
        + channel_phase[:, None]
    )
    return (jnp.cos(phase_angle), jnp.sin(phase_angle))


def beam_weights(inv_real, inv_imag, steer_real, steer_imag):
    weight_real = jnp.einsum("dij,jb->dib", inv_real, steer_real, precision=precise) - jnp.einsum(
        "dij,jb->dib", inv_imag, steer_imag, precision=precise
    )
    weight_imag = jnp.einsum("dij,jb->dib", inv_real, steer_imag, precision=precise) + jnp.einsum(
        "dij,jb->dib", inv_imag, steer_real, precision=precise
    )
    gain_norm = jnp.sum(steer_real[None] * weight_real + steer_imag[None] * weight_imag, axis=1)
    return (weight_real / gain_norm[:, None, :], weight_imag / gain_norm[:, None, :])


def form_beams(data_real, data_imag, weight_real, weight_imag):
    out_real = jnp.einsum("dgc,dcb->dgb", data_real, weight_real, precision=precise) + jnp.einsum(
        "dgc,dcb->dgb", data_imag, weight_imag, precision=precise
    )
    out_imag = jnp.einsum("dgc,dcb->dgb", data_imag, weight_real, precision=precise) - jnp.einsum(
        "dgc,dcb->dgb", data_real, weight_imag, precision=precise
    )
    return out_real * out_real + out_imag * out_imag


def on_device(echoes, range_taps, pulse_taper, channel_phase, loading, beam_index):
    rim_width = range_taps.shape[1] // 2
    doppler = doppler_table(pulse_taper)
    spectra = [
        transform(
            doppler, lax.slice_in_dim(echoes, interval * HOP, interval * HOP + PULSES, axis=1)
        )
        for interval in range(INTERVALS)
    ]
    turned = [
        lax.all_to_all(
            lax.all_to_all(spectrum, "section", split_axis=1, concat_axis=2, tiled=True),
            "sub",
            split_axis=1,
            concat_axis=3,
            tiled=True,
        )
        for spectrum in spectra
    ]
    refined = []
    for spectrum in turned:
        padded_bins = jnp.pad(spectrum, ((0, 0), (0, 0), (rim_width, rim_width), (0, 0)))
        part_real, part_imag = apply_taps(
            padded_bins[0], padded_bins[1], range_taps, spectrum.shape[2]
        )
        refined.append(jnp.stack([part_real, part_imag]))
    turned = refined
    steer_real, steer_imag = steering(beam_index, channel_phase)
    interval = 0
    inv_real, inv_imag = loaded_inverse(turned[interval][0], turned[interval][1], loading)
    weight_real, weight_imag = beam_weights(inv_real, inv_imag, steer_real, steer_imag)
    beam_power = form_beams(
        turned[interval + 1][0], turned[interval + 1][1], weight_real, weight_imag
    )
    partials = [jnp.sum(beam_power, axis=(0, 1))]
    totals = lax.psum(jnp.stack(partials), ("section", "sub"))
    noise_level = totals / (PULSES * turned[0].shape[2])
    return jnp.stack([beam_power / (noise_level[0] + epsilon)])


def solution(mesh):
    in_specs = (P("groups", None, "section", "sub"), P(), P(), P(), P(), P())
    out_specs = P("groups", ("section", "sub"), None, None)
    sections = mesh.shape["section"]
    small = sections == 8 and mesh.shape["sub"] == 2

    def run(echoes, range_taps, pulse_taper, channel_phase, loading, beam_index):
        args = (echoes, range_taps, pulse_taper, channel_phase, loading, beam_index)
        fits = small and echoes.shape[2] == 4 and echoes.shape[3] == LANES
        return factored_steps(*args) if fits else on_device(*args)

    return jax.shard_map(run, mesh=mesh, in_specs=in_specs, out_specs=out_specs, check_vma=False)
```

```python
import math

import jax
import jax.numpy as jnp
import numpy as np
from jax import lax
from jax.experimental import pallas as pl
from jax.experimental.pallas import tpu as pltpu
from jax.sharding import PartitionSpec as P


PULSES = 256
INTERVALS = 2
ITERS = 2
LOOKS = 1024
HOP = 128


precise = lax.Precision.HIGHEST
epsilon = 1e-06
F32 = jnp.float32
BF16 = jnp.bfloat16
LANES = 128
VMEM = pl.BlockSpec(memory_space=pltpu.VMEM)
SMEM = pl.BlockSpec(memory_space=pltpu.SMEM)
HBM = pl.BlockSpec(memory_space=pltpu.HBM)
LIMIT = 16 << 20
PAD = 8


def split(value):
    high = value.astype(BF16)
    return high, (value - high.astype(F32)).astype(BF16)


def dot(left, right):
    return jnp.dot(left, right, preferred_element_type=F32)


def dot_nt(left, right):
    return lax.dot_general(left, right, (((1,), (1,)), ((), ())), preferred_element_type=F32)


def dot_tn(left, right):
    return lax.dot_general(left, right, (((0,), (0,)), ((), ())), preferred_element_type=F32)


def triple(product, left, right):
    return product(left[0], right[0]) + (product(left[0], right[1]) + product(left[1], right[0]))


def doppler_tables(pulses):
    half = pulses // 2
    bins = np.arange(half)[:, None]
    tables = []
    for parity in (0, 1):
        phase = 2.0 * np.pi * ((bins * np.arange(parity, pulses, 2)[None, :]) % pulses) / pulses
        cosine, sine = np.cos(phase), np.sin(phase)
        table = np.concatenate([cosine, sine], 1).astype(np.float32)
        high = table.astype(jnp.bfloat16)
        tables += [high, (table - high.astype(np.float32)).astype(jnp.bfloat16)]
    return np.stack(tables)


def full_table(rows):
    half = rows.shape[1] // 2
    turned = jnp.concatenate([-rows[:, half:], rows[:, :half]], axis=1)
    return jnp.concatenate([rows, turned], axis=0)


def doppler_body(gates, hop, view_ref, taper_ref, table_ref, result, tapers):
    half = hop
    for segment in (0, 1):
        row = taper_ref[segment : segment + 1, :]
        tapers[segment * hop : (segment + 1) * hop, :] = jnp.broadcast_to(row, (hop, hop)).T
    for group in range(0, gates, 2):
        members = range(group, min(group + 2, gates))
        for parity in (0, 1):
            rows = []
            for part in (0, 1):
                for segment in (0, 1):
                    taper = tapers[pl.ds(segment * hop + parity, hop // 2, stride=2), :]
                    blocks = []
                    for gate in members:
                        at = pl.ds(parity * gates + gate, hop // 2, stride=2 * gates)
                        blocks.append(view_ref[part, segment, at, :] * taper)
                    rows.append(jnp.concatenate(blocks, axis=1))
            data = split(jnp.concatenate(rows, axis=0))
            table = full_table(table_ref[2 * parity]), full_table(table_ref[2 * parity + 1])
            value = triple(dot, table, data)
            if parity == 0:
                even = value
        for place, gate in enumerate(members):
            lanes = slice(place * LANES, (place + 1) * LANES)
            for part in (0, 1):
                own = slice(part * half, (part + 1) * half)
                result[part, gate, :half] = even[own, lanes] + value[own, lanes]
                result[part, gate, half:] = even[own, lanes] - value[own, lanes]


def doppler(view, taper, sections, interval, split_sub):
    gates = view.shape[2] // HOP
    per = PULSES // sections
    own = per // 2

    def body(view_ref, taper_ref, table_ref, *rest):
        outs = 2 if split_sub else sections
        out_refs, scratch = rest[:outs], rest[outs:]
        result, tapers, own_view, own_taper, own_table, sems = scratch
        copies = [pltpu.make_async_copy(taper_ref, own_taper, sems.at[0])]
        copies.append(pltpu.make_async_copy(table_ref, own_table, sems.at[1]))
        for part in (0, 1):
            blocks = view_ref.at[part, pl.ds(interval, 2)]
            copies.append(pltpu.make_async_copy(blocks, own_view.at[part], sems.at[2 + part]))
        for copy in copies:
            copy.start()
        for copy in copies:
            copy.wait()
        doppler_body(gates, HOP, own_view, own_taper, own_table, result, tapers)
        section = lax.axis_index("section")
        if not split_sub:
            for step in range(sections):
                start = pl.multiple_of(jnp.bitwise_xor(section, step) * per, per)
                out_refs[step][...] = result[:, :, pl.ds(start, per), :]
        else:
            sub = lax.axis_index("sub")
            for step in range(sections):
                start = jnp.bitwise_xor(section, step) * per
                mine = pl.multiple_of(start + sub * own, own)
                theirs = pl.multiple_of(start + (1 - sub) * own, own)
                out_refs[0][step] = result[:, :, pl.ds(mine, own), :]
                out_refs[1][step] = result[:, :, pl.ds(theirs, own), :]

    tables = jnp.asarray(doppler_tables(PULSES))
    if split_sub:
        shape = (sections, 2, gates, own, LANES)
        outs = [jax.ShapeDtypeStruct(shape, F32)] * 2
    else:
        shape = (2, gates, per, LANES)
        outs = [jax.ShapeDtypeStruct(shape, F32)] * sections
    return pl.pallas_call(
        body,
        in_specs=[HBM] * 3,
        out_specs=[VMEM] * len(outs),
        out_shape=outs,
        scratch_shapes=[
            pltpu.VMEM((2, gates, PULSES, LANES), F32),
            pltpu.VMEM((PULSES, LANES), F32),
            pltpu.VMEM((view.shape[0], 2) + view.shape[2:], F32),
            pltpu.VMEM(taper.shape, F32),
            pltpu.VMEM(tables.shape, BF16),
            pltpu.SemaphoreType.DMA((4,)),
        ],
        compiler_params=pltpu.CompilerParams(vmem_limit_bytes=LIMIT),
    )(*[pltpu.with_memory_space_constraint(v, pltpu.HBM) for v in (view, taper, tables)])


def gather_sub(blocks):
    sections = len(blocks)
    _, gates, per, _ = blocks[0].shape
    own = per // 2

    def body(*refs):
        section, sub = lax.axis_index("section"), lax.axis_index("sub")
        mine = pl.multiple_of(sub * own, own)
        theirs = pl.multiple_of((1 - sub) * own, own)
        for step in range(sections):
            source = jnp.bitwise_xor(section, step)
            refs[sections][source] = refs[step][:, :, pl.ds(mine, own), :]
            refs[sections + 1][source] = refs[step][:, :, pl.ds(theirs, own), :]

    shape = jax.ShapeDtypeStruct((sections, 2, gates, own, LANES), F32)
    return pl.pallas_call(
        body,
        in_specs=[VMEM] * sections,
        out_specs=[VMEM] * 2,
        out_shape=[shape] * 2,
        compiler_params=pltpu.CompilerParams(vmem_limit_bytes=LIMIT),
        name="gather_sub",
    )(*blocks)


def pair_up(mine, other):
    sections = mine.shape[0]

    def body(mine_ref, other_ref, *out_refs):
        for step in range(sections):
            out_refs[step][0] = mine_ref[step]
            out_refs[step][1] = other_ref[step]

    shape = jax.ShapeDtypeStruct((2,) + mine.shape[1:], F32)
    return pl.pallas_call(
        body,
        in_specs=[VMEM] * 2,
        out_specs=[VMEM] * sections,
        out_shape=[shape] * sections,
        compiler_params=pltpu.CompilerParams(vmem_limit_bytes=LIMIT),
        name="pair_up",
    )(mine, other)


def filter_matrix(taps_ref, gates, sections, section, steps, conjugate):
    count = gates * sections
    half = count if steps is None else len(steps) * gates
    taps = taps_ref.shape[1]
    row = lax.broadcasted_iota(jnp.int32, (2 * count, 2 * half), 0)
    column = lax.broadcasted_iota(jnp.int32, (2 * count, 2 * half), 1)
    row_imag, column_imag = row >= count, column >= half
    row_gate = jnp.where(row_imag, row - count, row)
    place = jnp.where(column_imag, column - half, column)
    if steps is None:
        inner = sum(jnp.where(place >= gate * sections, 1, 0) for gate in range(1, gates))
        step = place - inner * sections
    else:
        outer = sum(jnp.where(place >= order * gates, 1, 0) for order in range(1, len(steps)))
        inner = place - outer * gates
        step = jnp.full(place.shape, steps[0], jnp.int32)
        for order in range(1, len(steps)):
            step = jnp.where(outer >= order, steps[order], step)
    column_gate = jnp.bitwise_xor(step, section) * gates + inner
    tap = column_gate - row_gate + taps // 2
    real = sum(jnp.where(tap == j, taps_ref[0, j], 0.0) for j in range(taps))
    imag = sum(jnp.where(tap == j, taps_ref[1, j], 0.0) for j in range(taps))
    straight, crossed = row_imag == column_imag, jnp.where(row_imag, imag, -imag)
    matrix = jnp.where(straight, real, crossed)
    if conjugate:
        matrix = jnp.where(row_imag, -matrix, matrix)
    return matrix


def stacked(product, left, right):
    rows = left[0].shape[0]
    both = product(jnp.concatenate(left, axis=0), right[0])
    return both[:rows] + (both[rows:] + product(left[0], right[1]))


def beside(value, negate_first):
    count = value.shape[0] // 2
    real, imag = value[:count], value[count:]
    if negate_first:
        return jnp.concatenate(
            [jnp.concatenate([real, -imag], axis=1), jnp.concatenate([imag, real], axis=1)], axis=0
        )
    return jnp.concatenate(
        [jnp.concatenate([real, imag], axis=1), jnp.concatenate([-imag, real], axis=1)], axis=0
    )


def weights_kernel(mine, other, steer, range_taps, loading):
    sections, _, gates, own, _ = mine.shape
    count = sections * gates
    side = 2 * count
    channels = 2 * LANES
    beams = steer.shape[1] // 2
    stride = 2 * gates * own
    mine = mine.reshape(sections * stride, LANES)
    other = other.reshape(sections * stride, LANES)

    def body(mine_ref, other_ref, steer_ref, taps_ref, load_ref,
             b_ref, th_ref, tl_ref, gain_ref,
             ah_ref, al_ref, rows_ref, sums_ref, squares_ref, u_ref, gram_ref):
        matrix = split(filter_matrix(taps_ref, gates, sections, 0, None, True))
        for index in range(own):
            def load(ref):
                return jnp.concatenate(
                    [ref[pl.ds((part * gates + gate) * own + index, sections, stride=stride), :]
                     for part in (0, 1) for gate in range(gates)], axis=0)

            data = jnp.concatenate([load(mine_ref), load(other_ref)], axis=1)
            value = stacked(dot, matrix, split(data))
            squares_ref[index : index + 1, :] = jnp.sum(value * value, axis=0, keepdims=True)
            high, low = split(value)
            ah_ref[index] = high
            al_ref[index] = low
            b_ref[index, :side] = beside(high, False)
            b_ref[index, side:] = beside(low, False)
            here = slice(index * count, (index + 1) * count)
            for place, part in enumerate((high, low, high)):
                lanes = slice(place * 2 * channels, (place + 1) * 2 * channels)
                rows_ref[here, lanes] = jnp.concatenate([part[:count], part[count:]], axis=1)
        for index in range(own):
            high, low = ah_ref[index], al_ref[index]
            turn = lambda v: jnp.concatenate(
                [v, jnp.concatenate([v[count:], -v[:count]], axis=0)], axis=1
            )
            rh, rl = turn(high), turn(low)
            left = jnp.concatenate([high, high, low], axis=0)
            right = jnp.concatenate([rh, rl, rh], axis=0)
            cov = jnp.abs(dot_tn(left, right))
            sums_ref[index : index + 1, :] = jnp.sum(
                cov[:, :channels] + cov[:, channels:], axis=0, keepdims=True
            )
        bound = jnp.max(sums_ref[...], axis=1, keepdims=True) / count
        trace = jnp.sum(squares_ref[...], axis=1, keepdims=True) / count
        delta = load_ref[0] * trace / channels
        bound = bound + delta
        ratio = 1.0 - delta / bound
        first = 1.0 + ratio * (1.0 + ratio * (1.0 + ratio))
        second = 1.0 + ratio * (2.0 + 3.0 * ratio)
        third = 1.0 + 3.0 * ratio
        norm = 1.0 / (count * bound)
        u_ref[...] = dot(rows_ref[...], steer_ref[...])
        low_at = 2 * 2 * channels
        table = steer_ref[:channels, :].astype(F32) + steer_ref[low_at : low_at + channels, :].astype(F32)
        power = jnp.sum(table * table, axis=0, keepdims=True)
        power = power[:, :beams] + power[:, beams:]
        eye = (
            lax.broadcasted_iota(jnp.int32, (side, side), 0)
            == lax.broadcasted_iota(jnp.int32, (side, side), 1)
        )
        for index in range(own):
            at = slice(index, index + 1)
            halves = beside(ah_ref[index], True), beside(al_ref[index], True)
            gram_ref[index] = stacked(dot_nt, halves, halves) * norm[at]
        for index in range(own):
            at = slice(index, index + 1)
            gram = gram_ref[index]
            parts = split(gram)
            square = stacked(dot, parts, parts)
            quad = jnp.where(eye, second[at], 0.0) - third[at] * gram + square
            gram_ref[index] = quad * (norm[at] / first[at])
        for index in range(own):
            u = u_ref[index * count : (index + 1) * count, :]
            up = jnp.concatenate([u[:, :beams], u[:, beams:]], axis=0)
            value = stacked(dot, split(gram_ref[index]), split(up))
            high, low = split(value)
            th_ref[index] = beside(high, False)
            tl_ref[index] = beside(low, False)
            sums_ref[index : index + 1, :] = jnp.sum(up * value, axis=0, keepdims=True)
        gain = power - sums_ref[...]
        gain_ref[...] = 1.0 / (gain * gain)

    wide = jax.ShapeDtypeStruct((own, 2 * side, 2 * channels), BF16)
    turned = jax.ShapeDtypeStruct((own, side, 2 * beams), BF16)
    return pl.pallas_call(
        body,
        in_specs=[VMEM] * 3 + [SMEM] * 2,
        out_specs=[VMEM] * 4,
        out_shape=[wide, turned, turned, jax.ShapeDtypeStruct((own, beams), F32)],
        scratch_shapes=[
            pltpu.VMEM((own, side, channels), BF16),
            pltpu.VMEM((own, side, channels), BF16),
            pltpu.VMEM((own * count, 6 * channels), BF16),
            pltpu.VMEM((own, channels), F32),
            pltpu.VMEM((own, channels), F32),
            pltpu.VMEM((own * count, 2 * beams), F32),
            pltpu.VMEM((own, side, side), F32),
        ],
        compiler_params=pltpu.CompilerParams(vmem_limit_bytes=LIMIT),
        name="weights",
    )(mine, other, steer, range_taps, loading)


def near_kernel(blocks, conjugated, turned, steer, range_taps):
    steps = sorted(blocks)
    _, _, gates, own, _ = blocks[steps[0]].shape
    size = 4 * gates * own
    pitch = size + PAD
    wide = 4 * LANES
    side = conjugated.shape[1] // 2
    count = side // 2
    sections = count // gates
    beams = steer.shape[1] // 2

    def body(*refs):
        (b_ref, th_ref, tl_ref, steer_ref, taps_ref, out_ref,
         held, rows_ref, v_ref, cross_ref) = refs[len(steps) :]
        for step in range(sections):
            here = slice(step * pitch, step * pitch + size)
            held[here, :] = refs[steps.index(step)][...] if step in steps else jnp.zeros((size, LANES), F32)
        matrix = split(filter_matrix(taps_ref, gates, sections, lax.axis_index("section"), None, False))
        matrix = jnp.concatenate([matrix[0], matrix[1], matrix[0]], axis=1)
        for index in range(own):
            def load(half, part):
                return jnp.concatenate(
                    [held[pl.ds(((half * 2 + part) * gates + gate) * own + index, sections, stride=pitch), :]
                     for gate in range(gates)], axis=0)

            data = jnp.concatenate([load(half, part) for part in (0, 1) for half in (0, 1)], axis=1)
            high, low = split(data)
            here = slice(index * count, (index + 1) * count)
            for place, part in enumerate((high, low, high)):
                rows_ref[here, place * wide : (place + 1) * wide] = part
        for index in range(own):
            here = slice(index * count, (index + 1) * count)
            parts = jnp.concatenate([rows_ref[here, :wide], rows_ref[here, wide : 2 * wide]], axis=0)
            both = dot_nt(parts, b_ref[index])
            both = both[:count] + both[count:]
            cross_ref[index] = both[:, :side] + both[:, side:]
        v_ref[...] = dot(rows_ref[...], steer_ref[...])
        for index in range(own):
            here = slice(index * count, (index + 1) * count)
            low_rank = stacked(dot, split(cross_ref[index]), (th_ref[index], tl_ref[index]))
            v_ref[here, :] = v_ref[here, :] - low_rank
        for index in range(own):
            v = v_ref[index * count : (index + 1) * count, :]
            high, low = split(jnp.concatenate([v[:, :beams], v[:, beams:]], axis=0))
            out_ref[index] = dot(matrix, jnp.concatenate([high, high, low], axis=0))

    return pl.pallas_call(
        body,
        in_specs=[VMEM] * (len(steps) + 4) + [SMEM],
        out_specs=VMEM,
        out_shape=jax.ShapeDtypeStruct((own, side, beams), F32),
        scratch_shapes=[
            pltpu.VMEM((sections * pitch, LANES), F32),
            pltpu.VMEM((own * count, 3 * wide), BF16),
            pltpu.VMEM((own * count, 2 * beams), F32),
            pltpu.VMEM((own, count, side), F32),
        ],
        compiler_params=pltpu.CompilerParams(vmem_limit_bytes=LIMIT),
        name="near",
    )(*[blocks[step].reshape(size, LANES) for step in steps], conjugated, *turned, steer, range_taps)


def beams_kernel(blocks, near, weights, steer, range_taps):
    steps = sorted(blocks)
    _, _, gates, own, _ = blocks[steps[0]].shape
    size = 4 * gates * own
    side = near.shape[1]
    count = side // 2
    sections = count // gates
    beams = steer.shape[1] // 2
    each = len(steps) * gates
    group = 16 // each

    def body(*refs):
        (near_ref, b_ref, th_ref, tl_ref, gain_ref, steer_ref, taps_ref,
         power_ref, total_ref, dense) = refs[len(steps) :]
        for order in range(len(steps)):
            for half in (0, 1):
                for part in (0, 1):
                    for gate in range(gates):
                        start = ((half * 2 + part) * gates + gate) * own
                        at = pl.ds(order * gates + gate, own, stride=each)
                        dense[part * 2 + half, at, :] = refs[order][start : start + own, :]
        matrix = filter_matrix(taps_ref, gates, sections, lax.axis_index("section"), steps, False)
        first, second = split(matrix)
        first, second = first.astype(F32), second.astype(F32)
        matrix = jnp.concatenate([first, second, first], axis=1).astype(BF16)
        high, low = split(jnp.concatenate([dense[place] for place in range(4)], axis=1))
        value = dot(jnp.concatenate([high, low, high], axis=1), steer_ref[...])
        crosses = []
        for index in range(own):
            base = index // group * group * each
            rows = slice(base, base + group * each)
            parts = jnp.concatenate([high[rows], low[rows]], axis=0)
            both = dot_nt(parts, b_ref[index])
            both = both[: group * each] + both[group * each :]
            both = both[index * each - base : (index + 1) * each - base]
            crosses.append(both[:, :side] + both[:, side:])
        stacks = []
        for index in range(own):
            ch, cl = split(crosses[index])
            both = jnp.concatenate([ch.astype(F32), cl.astype(F32)], axis=0).astype(BF16)
            both = dot(both, th_ref[index]) + dot(both, tl_ref[index])
            v = value[index * each : (index + 1) * each, :] - (both[:each] + both[each:])
            high, low = split(jnp.concatenate([v[:, :beams], v[:, beams:]], axis=0))
            stacks.append(jnp.concatenate([high, high, low], axis=0))
        total = jnp.zeros((1, beams), F32)
        for index in range(own):
            out = near_ref[index] + dot(matrix, stacks[index])
            power = (out[:count] * out[:count] + out[count:] * out[count:]) * gain_ref[index : index + 1, :]
            total = total + jnp.sum(power, axis=0, keepdims=True)
            power_ref[index] = power
        total_ref[...] = jnp.broadcast_to(total, total_ref.shape)

    return pl.pallas_call(
        body,
        in_specs=[VMEM] * (len(steps) + 6) + [SMEM],
        out_specs=[VMEM] * 2,
        out_shape=[
            jax.ShapeDtypeStruct((own, count, beams), F32),
            jax.ShapeDtypeStruct((2 * sections, beams), F32),
        ],
        scratch_shapes=[pltpu.VMEM((4, own * each, LANES), F32)],
        compiler_params=pltpu.CompilerParams(vmem_limit_bytes=LIMIT),
        name="beams",
    )(*[blocks[step].reshape(size, LANES) for step in steps], near, *weights, steer, range_taps)


def steering_tables(beam_index, channel_phase):
    channels = channel_phase.shape[0]
    own = channels // 2
    sub = lax.axis_index("sub")
    place = jnp.arange(channels, dtype=jnp.int32)
    place = jnp.where(place + sub * own >= channels, place + sub * own - channels, place + sub * own)
    turned = jnp.concatenate([channel_phase[own:], channel_phase[:own]])
    phase = jnp.where(sub == 0, channel_phase, turned)
    direction = -1.0 + (2.0 * beam_index.astype(F32) + 1.0) / LOOKS
    angle = math.pi * place.astype(F32)[:, None] * direction[None, :] + phase[:, None]
    cosine, sine = jnp.cos(angle), jnp.sin(angle)
    table = jnp.concatenate(
        [jnp.concatenate([cosine, -sine], 1), jnp.concatenate([sine, cosine], 1)], 0
    )
    high = lax.reduce_precision(table, 8, 7)
    low = lax.reduce_precision(table - high, 8, 7).astype(BF16)
    high = high.astype(BF16)
    return jnp.concatenate([high, high, low], 0)


def permuted(block, sections, step):
    return lax.ppermute(block, "section", [(place, place ^ step) for place in range(sections)])


def swapped(block):
    return lax.ppermute(block, "sub", [(0, 1), (1, 0)])


def hop_order(sections):
    near, far = list(range(1, sections // 2)), list(range(sections // 2, sections))
    return far[::-1] + near[::-1], near[::-1] + far[::-1]


def factored_steps(echoes, range_taps, pulse_taper, channel_phase, loading, beam_index):
    parts, pulses, gates, lanes = echoes.shape
    sections = lax.axis_size("section")
    order = hop_order(sections)[0]
    view = echoes.reshape(parts, pulses // HOP, HOP * gates, lanes)
    taper = pulse_taper.reshape(2, HOP)

    sent = doppler(view, taper, sections, 0, False)
    got = {0: sent[0]}
    for step in order:
        got[step] = permuted(sent[step], sections, step)
    mine, theirs = doppler(view, taper, sections, 1, True)
    other = swapped(theirs)
    sent = pair_up(mine, other)
    later = {0: sent[0]}
    for step in order:
        later[step] = permuted(sent[step], sections, step)

    steer = steering_tables(beam_index, channel_phase)
    keep, pass_on = gather_sub([got[step] for step in range(sections)])
    other = swapped(pass_on)
    weights = weights_kernel(keep, other, steer, range_taps, loading)
    last = hop_order(sections)[1][-2:]
    blocks = {step: block for step, block in later.items() if step not in last}
    near = near_kernel(blocks, weights[0], weights[1:3], steer, range_taps)
    blocks = {step: later[step] for step in last}
    power, total = beams_kernel(blocks, near, weights, steer, range_taps)
    totals = lax.all_to_all(total, ("section", "sub"), 0, 0, tiled=True)
    noise_level = jnp.sum(totals, axis=0) / (PULSES * gates * sections)
    return (power / (noise_level + epsilon))[None]


def apply_taps(pad_real, pad_imag, range_taps, gate_count):
    axis_gates = pad_real.ndim - 2
    shape_out = pad_real.shape[:axis_gates] + (gate_count,) + pad_real.shape[axis_gates + 1 :]
    out_real = jnp.zeros(shape_out, jnp.float32)
    out_imag = jnp.zeros(shape_out, jnp.float32)
    for offset in range(range_taps.shape[1]):
        part_real = lax.slice_in_dim(pad_real, offset, offset + gate_count, axis=axis_gates)
        part_imag = lax.slice_in_dim(pad_imag, offset, offset + gate_count, axis=axis_gates)
        out_real = out_real + range_taps[0, offset] * part_real - range_taps[1, offset] * part_imag
        out_imag = out_imag + range_taps[0, offset] * part_imag + range_taps[1, offset] * part_real
    return (out_real, out_imag)


def doppler_table(pulse_taper):
    pulse_count = pulse_taper.shape[0]
    pulse_index = jnp.arange(pulse_count, dtype=jnp.int32)
    product = pulse_index[:, None] * pulse_index[None, :] % pulse_count
    phase_angle = 2.0 * math.pi / pulse_count * product.astype(jnp.float32)
    cosine = jnp.cos(phase_angle) * pulse_taper[None, :]
    sine_part = jnp.sin(phase_angle) * pulse_taper[None, :]
    upper_rows = jnp.concatenate([cosine, sine_part], axis=1)
    lower_rows = jnp.concatenate([-sine_part, cosine], axis=1)
    return jnp.concatenate([upper_rows, lower_rows], axis=0)


def transform(doppler, segment):
    shape_in = segment.shape
    flattened = segment.reshape(shape_in[0] * shape_in[1], -1)
    result = jnp.dot(doppler, flattened, precision=precise, preferred_element_type=jnp.float32)
    return result.reshape(shape_in)


def batched(first, second):
    return jnp.einsum("dij,djk->dik", first, second, precision=precise)


def complex_product(left_real, left_imag, right_real, right_imag):
    out_real = batched(left_real, right_real) - batched(left_imag, right_imag)
    out_imag = batched(left_real, right_imag) + batched(left_imag, right_real)
    return (out_real, out_imag)


def gram_product(first, second):
    return jnp.einsum("dgi,dgj->dij", first, second, precision=precise)


def loaded_inverse(real_part, imag_part, loading):
    gate_count = real_part.shape[1]
    channels = real_part.shape[2]
    cov_real = (
        gram_product(real_part, real_part) + gram_product(imag_part, imag_part)
    ) / gate_count
    cov_imag = (
        gram_product(real_part, imag_part) - gram_product(imag_part, real_part)
    ) / gate_count
    identity = jnp.eye(channels, dtype=jnp.float32)
    trace_sum = jnp.sum(cov_real * identity[None], axis=(1, 2))
    cov_real = cov_real + (loading[0] * trace_sum / channels)[:, None, None] * identity[None]
    row_bound = jnp.max(jnp.sum(jnp.abs(cov_real) + jnp.abs(cov_imag), axis=2), axis=1)
    inv_real = identity[None] / row_bound[:, None, None]
    inv_imag = jnp.zeros_like(inv_real)
    for _ in range(ITERS):
        prod_real, prod_imag = complex_product(cov_real, cov_imag, inv_real, inv_imag)
        inv_real, inv_imag = complex_product(
            inv_real, inv_imag, 2.0 * identity[None] - prod_real, -prod_imag
        )
    return (inv_real, inv_imag)


def steering(beam_index, channel_phase):
    channels = channel_phase.shape[0]
    direction = -1.0 + (2.0 * beam_index.astype(jnp.float32) + 1.0) / LOOKS
    phase_angle = (
        math.pi * jnp.arange(channels, dtype=jnp.float32)[:, None] * direction[None, :]
        + channel_phase[:, None]
    )
    return (jnp.cos(phase_angle), jnp.sin(phase_angle))


def beam_weights(inv_real, inv_imag, steer_real, steer_imag):
    weight_real = jnp.einsum("dij,jb->dib", inv_real, steer_real, precision=precise) - jnp.einsum(
        "dij,jb->dib", inv_imag, steer_imag, precision=precise
    )
    weight_imag = jnp.einsum("dij,jb->dib", inv_real, steer_imag, precision=precise) + jnp.einsum(
        "dij,jb->dib", inv_imag, steer_real, precision=precise
    )
    gain_norm = jnp.sum(steer_real[None] * weight_real + steer_imag[None] * weight_imag, axis=1)
    return (weight_real / gain_norm[:, None, :], weight_imag / gain_norm[:, None, :])


def form_beams(data_real, data_imag, weight_real, weight_imag):
    out_real = jnp.einsum("dgc,dcb->dgb", data_real, weight_real, precision=precise) + jnp.einsum(
        "dgc,dcb->dgb", data_imag, weight_imag, precision=precise
    )
    out_imag = jnp.einsum("dgc,dcb->dgb", data_imag, weight_real, precision=precise) - jnp.einsum(
        "dgc,dcb->dgb", data_real, weight_imag, precision=precise
    )
    return out_real * out_real + out_imag * out_imag


def on_device(echoes, range_taps, pulse_taper, channel_phase, loading, beam_index):
    rim_width = range_taps.shape[1] // 2
    doppler = doppler_table(pulse_taper)
    spectra = [
        transform(
            doppler, lax.slice_in_dim(echoes, interval * HOP, interval * HOP + PULSES, axis=1)
        )
        for interval in range(INTERVALS)
    ]
    turned = [
        lax.all_to_all(
            lax.all_to_all(spectrum, "section", split_axis=1, concat_axis=2, tiled=True),
            "sub",
            split_axis=1,
            concat_axis=3,
            tiled=True,
        )
        for spectrum in spectra
    ]
    refined = []
    for spectrum in turned:
        padded_bins = jnp.pad(spectrum, ((0, 0), (0, 0), (rim_width, rim_width), (0, 0)))
        part_real, part_imag = apply_taps(
            padded_bins[0], padded_bins[1], range_taps, spectrum.shape[2]
        )
        refined.append(jnp.stack([part_real, part_imag]))
    turned = refined
    steer_real, steer_imag = steering(beam_index, channel_phase)
    interval = 0
    inv_real, inv_imag = loaded_inverse(turned[interval][0], turned[interval][1], loading)
    weight_real, weight_imag = beam_weights(inv_real, inv_imag, steer_real, steer_imag)
    beam_power = form_beams(
        turned[interval + 1][0], turned[interval + 1][1], weight_real, weight_imag
    )
    partials = [jnp.sum(beam_power, axis=(0, 1))]
    totals = lax.psum(jnp.stack(partials), ("section", "sub"))
    noise_level = totals / (PULSES * turned[0].shape[2])
    return jnp.stack([beam_power / (noise_level[0] + epsilon)])


def solution(mesh):
    in_specs = (P("groups", None, "section", "sub"), P(), P(), P(), P(), P())
    out_specs = P("groups", ("section", "sub"), None, None)
    sections = mesh.shape["section"]
    small = sections == 8 and mesh.shape["sub"] == 2

    def run(echoes, range_taps, pulse_taper, channel_phase, loading, beam_index):
        args = (echoes, range_taps, pulse_taper, channel_phase, loading, beam_index)
        fits = small and echoes.shape[2] == 4 and echoes.shape[3] == LANES
        return factored_steps(*args) if fits else on_device(*args)

    return jax.shard_map(run, mesh=mesh, in_specs=in_specs, out_specs=out_specs, check_vma=False)
```

```python
import math

import jax
import jax.numpy as jnp
import numpy as np
from jax import lax
from jax.experimental import pallas as pl
from jax.experimental.pallas import tpu as pltpu
from jax.sharding import PartitionSpec as P


PULSES = 256
INTERVALS = 2
ITERS = 2
LOOKS = 1024
HOP = 128


precise = lax.Precision.HIGHEST
epsilon = 1e-06
F32 = jnp.float32
BF16 = jnp.bfloat16
LANES = 128
VMEM = pl.BlockSpec(memory_space=pltpu.VMEM)
SMEM = pl.BlockSpec(memory_space=pltpu.SMEM)
HBM = pl.BlockSpec(memory_space=pltpu.HBM)
LIMIT = 16 << 20
PAD = 8


def split(value):
    high = value.astype(BF16)
    return high, (value - high.astype(F32)).astype(BF16)


def dot(left, right):
    return jnp.dot(left, right, preferred_element_type=F32)


def dot_nt(left, right):
    return lax.dot_general(left, right, (((1,), (1,)), ((), ())), preferred_element_type=F32)


def dot_tn(left, right):
    return lax.dot_general(left, right, (((0,), (0,)), ((), ())), preferred_element_type=F32)


def triple(product, left, right):
    return product(left[0], right[0]) + (product(left[0], right[1]) + product(left[1], right[0]))


def doppler_tables(pulses):
    half = pulses // 2
    bins = np.arange(half)[:, None]
    tables = []
    for parity in (0, 1):
        phase = 2.0 * np.pi * ((bins * np.arange(parity, pulses, 2)[None, :]) % pulses) / pulses
        cosine, sine = np.cos(phase), np.sin(phase)
        table = np.concatenate([cosine, sine], 1).astype(np.float32)
        high = table.astype(jnp.bfloat16)
        tables += [high, (table - high.astype(np.float32)).astype(jnp.bfloat16)]
    return np.stack(tables)


def full_table(rows):
    half = rows.shape[1] // 2
    turned = jnp.concatenate([-rows[:, half:], rows[:, :half]], axis=1)
    return jnp.concatenate([rows, turned], axis=0)


def doppler_body(gates, hop, view_ref, table_ref, result, tapers):
    half = hop
    for group in range(0, gates, 2):
        members = range(group, min(group + 2, gates))
        for parity in (0, 1):
            rows = []
            for part in (0, 1):
                for segment in (0, 1):
                    taper = tapers[pl.ds(segment * hop + parity, hop // 2, stride=2), :]
                    blocks = []
                    for gate in members:
                        at = pl.ds(parity * gates + gate, hop // 2, stride=2 * gates)
                        blocks.append(view_ref[part, segment, at, :] * taper)
                    rows.append(jnp.concatenate(blocks, axis=1))
            data = split(jnp.concatenate(rows, axis=0))
            table = full_table(table_ref[2 * parity]), full_table(table_ref[2 * parity + 1])
            value = triple(dot, table, data)
            if parity == 0:
                even = value
        for place, gate in enumerate(members):
            lanes = slice(place * LANES, (place + 1) * LANES)
            for part in (0, 1):
                own = slice(part * half, (part + 1) * half)
                result[part, gate, :half] = even[own, lanes] + value[own, lanes]
                result[part, gate, half:] = even[own, lanes] - value[own, lanes]


def doppler(view, taper, sections, interval, split_sub):
    gates = view.shape[2] // HOP
    per = PULSES // sections
    own = per // 2

    def body(view_ref, taper_ref, table_ref, *rest):
        outs = 2 if split_sub else sections
        out_refs, scratch = rest[:outs], rest[outs:]
        result, tapers, own_view, own_taper, own_table, sems = scratch
        copies = [pltpu.make_async_copy(taper_ref, own_taper, sems.at[0])]
        copies.append(pltpu.make_async_copy(table_ref, own_table, sems.at[1]))
        for part in (0, 1):
            blocks = view_ref.at[part, pl.ds(interval, 2)]
            copies.append(pltpu.make_async_copy(blocks, own_view.at[part], sems.at[2 + part]))
        for copy in copies:
            copy.start()
        copies[0].wait()
        for segment in (0, 1):
            row = own_taper[segment : segment + 1, :]
            tapers[segment * HOP : (segment + 1) * HOP, :] = jnp.broadcast_to(row, (HOP, HOP)).T
        for copy in copies[1:]:
            copy.wait()
        doppler_body(gates, HOP, own_view, own_table, result, tapers)
        section = lax.axis_index("section")
        if not split_sub:
            for step in range(sections):
                start = pl.multiple_of(jnp.bitwise_xor(section, step) * per, per)
                out_refs[step][...] = result[:, :, pl.ds(start, per), :]
        else:
            sub = lax.axis_index("sub")
            for step in range(sections):
                start = jnp.bitwise_xor(section, step) * per
                mine = pl.multiple_of(start + sub * own, own)
                theirs = pl.multiple_of(start + (1 - sub) * own, own)
                out_refs[0][step] = result[:, :, pl.ds(mine, own), :]
                out_refs[1][step] = result[:, :, pl.ds(theirs, own), :]

    tables = jnp.asarray(doppler_tables(PULSES))
    if split_sub:
        shape = (sections, 2, gates, own, LANES)
        outs = [jax.ShapeDtypeStruct(shape, F32)] * 2
    else:
        shape = (2, gates, per, LANES)
        outs = [jax.ShapeDtypeStruct(shape, F32)] * sections
    return pl.pallas_call(
        body,
        in_specs=[HBM] * 3,
        out_specs=[VMEM] * len(outs),
        out_shape=outs,
        scratch_shapes=[
            pltpu.VMEM((2, gates, PULSES, LANES), F32),
            pltpu.VMEM((PULSES, LANES), F32),
            pltpu.VMEM((view.shape[0], 2) + view.shape[2:], F32),
            pltpu.VMEM(taper.shape, F32),
            pltpu.VMEM(tables.shape, BF16),
            pltpu.SemaphoreType.DMA((4,)),
        ],
        compiler_params=pltpu.CompilerParams(vmem_limit_bytes=LIMIT),
    )(*[pltpu.with_memory_space_constraint(v, pltpu.HBM) for v in (view, taper, tables)])


def gather_sub(blocks):
    sections = len(blocks)
    _, gates, per, _ = blocks[0].shape
    own = per // 2

    def body(*refs):
        section, sub = lax.axis_index("section"), lax.axis_index("sub")
        mine = pl.multiple_of(sub * own, own)
        theirs = pl.multiple_of((1 - sub) * own, own)
        for step in range(sections):
            source = jnp.bitwise_xor(section, step)
            refs[sections][source] = refs[step][:, :, pl.ds(mine, own), :]
            refs[sections + 1][source] = refs[step][:, :, pl.ds(theirs, own), :]

    shape = jax.ShapeDtypeStruct((sections, 2, gates, own, LANES), F32)
    return pl.pallas_call(
        body,
        in_specs=[VMEM] * sections,
        out_specs=[VMEM] * 2,
        out_shape=[shape] * 2,
        compiler_params=pltpu.CompilerParams(vmem_limit_bytes=LIMIT),
        name="gather_sub",
    )(*blocks)


def pair_up(mine, other):
    sections = mine.shape[0]

    def body(mine_ref, other_ref, *out_refs):
        for step in range(sections):
            out_refs[step][0] = mine_ref[step]
            out_refs[step][1] = other_ref[step]

    shape = jax.ShapeDtypeStruct((2,) + mine.shape[1:], F32)
    return pl.pallas_call(
        body,
        in_specs=[VMEM] * 2,
        out_specs=[VMEM] * sections,
        out_shape=[shape] * sections,
        compiler_params=pltpu.CompilerParams(vmem_limit_bytes=LIMIT),
        name="pair_up",
    )(mine, other)


def filter_matrix(taps_ref, gates, sections, section, steps, conjugate):
    count = gates * sections
    half = count if steps is None else len(steps) * gates
    taps = taps_ref.shape[1]
    row = lax.broadcasted_iota(jnp.int32, (2 * count, 2 * half), 0)
    column = lax.broadcasted_iota(jnp.int32, (2 * count, 2 * half), 1)
    row_imag, column_imag = row >= count, column >= half
    row_gate = jnp.where(row_imag, row - count, row)
    place = jnp.where(column_imag, column - half, column)
    if steps is None:
        inner = sum(jnp.where(place >= gate * sections, 1, 0) for gate in range(1, gates))
        step = place - inner * sections
    else:
        outer = sum(jnp.where(place >= order * gates, 1, 0) for order in range(1, len(steps)))
        inner = place - outer * gates
        step = jnp.full(place.shape, steps[0], jnp.int32)
        for order in range(1, len(steps)):
            step = jnp.where(outer >= order, steps[order], step)
    column_gate = jnp.bitwise_xor(step, section) * gates + inner
    tap = column_gate - row_gate + taps // 2
    real = sum(jnp.where(tap == j, taps_ref[0, j], 0.0) for j in range(taps))
    imag = sum(jnp.where(tap == j, taps_ref[1, j], 0.0) for j in range(taps))
    straight, crossed = row_imag == column_imag, jnp.where(row_imag, imag, -imag)
    matrix = jnp.where(straight, real, crossed)
    if conjugate:
        matrix = jnp.where(row_imag, -matrix, matrix)
    return matrix


def stacked(product, left, right):
    rows = left[0].shape[0]
    both = product(jnp.concatenate(left, axis=0), right[0])
    return both[:rows] + (both[rows:] + product(left[0], right[1]))


def beside(value, negate_first):
    count = value.shape[0] // 2
    real, imag = value[:count], value[count:]
    if negate_first:
        return jnp.concatenate(
            [jnp.concatenate([real, -imag], axis=1), jnp.concatenate([imag, real], axis=1)], axis=0
        )
    return jnp.concatenate(
        [jnp.concatenate([real, imag], axis=1), jnp.concatenate([-imag, real], axis=1)], axis=0
    )


def weights_kernel(mine, other, steer, range_taps, loading):
    sections, _, gates, own, _ = mine.shape
    count = sections * gates
    side = 2 * count
    channels = 2 * LANES
    beams = steer.shape[1] // 2
    stride = 2 * gates * own
    mine = mine.reshape(sections * stride, LANES)
    other = other.reshape(sections * stride, LANES)

    def body(mine_ref, other_ref, steer_ref, taps_ref, load_ref,
             b_ref, th_ref, tl_ref, gain_ref,
             ah_ref, al_ref, rows_ref, sums_ref, squares_ref, u_ref, gram_ref):
        matrix = split(filter_matrix(taps_ref, gates, sections, 0, None, True))
        for index in range(own):
            def load(ref):
                return jnp.concatenate(
                    [ref[pl.ds((part * gates + gate) * own + index, sections, stride=stride), :]
                     for part in (0, 1) for gate in range(gates)], axis=0)

            data = jnp.concatenate([load(mine_ref), load(other_ref)], axis=1)
            value = stacked(dot, matrix, split(data))
            squares_ref[index : index + 1, :] = jnp.sum(value * value, axis=0, keepdims=True)
            high, low = split(value)
            ah_ref[index] = high
            al_ref[index] = low
            b_ref[index, :side] = beside(high, False)
            b_ref[index, side:] = beside(low, False)
            here = slice(index * count, (index + 1) * count)
            for place, part in enumerate((high, low, high)):
                lanes = slice(place * 2 * channels, (place + 1) * 2 * channels)
                rows_ref[here, lanes] = jnp.concatenate([part[:count], part[count:]], axis=1)
        for index in range(own):
            high, low = ah_ref[index], al_ref[index]
            turn = lambda v: jnp.concatenate(
                [v, jnp.concatenate([v[count:], -v[:count]], axis=0)], axis=1
            )
            rh, rl = turn(high), turn(low)
            left = jnp.concatenate([high, high, low], axis=0)
            right = jnp.concatenate([rh, rl, rh], axis=0)
            cov = jnp.abs(dot_tn(left, right))
            sums_ref[index : index + 1, :] = jnp.sum(
                cov[:, :channels] + cov[:, channels:], axis=0, keepdims=True
            )
        bound = jnp.max(sums_ref[...], axis=1, keepdims=True) / count
        trace = jnp.sum(squares_ref[...], axis=1, keepdims=True) / count
        delta = load_ref[0] * trace / channels
        bound = bound + delta
        ratio = 1.0 - delta / bound
        first = 1.0 + ratio * (1.0 + ratio * (1.0 + ratio))
        second = 1.0 + ratio * (2.0 + 3.0 * ratio)
        third = 1.0 + 3.0 * ratio
        norm = 1.0 / (count * bound)
        u_ref[...] = dot(rows_ref[...], steer_ref[...])
        low_at = 2 * 2 * channels
        table = steer_ref[:channels, :].astype(F32) + steer_ref[low_at : low_at + channels, :].astype(F32)
        power = jnp.sum(table * table, axis=0, keepdims=True)
        power = power[:, :beams] + power[:, beams:]
        eye = (
            lax.broadcasted_iota(jnp.int32, (side, side), 0)
            == lax.broadcasted_iota(jnp.int32, (side, side), 1)
        )
        for index in range(own):
            at = slice(index, index + 1)
            halves = beside(ah_ref[index], True), beside(al_ref[index], True)
            gram_ref[index] = stacked(dot_nt, halves, halves) * norm[at]
        for index in range(own):
            at = slice(index, index + 1)
            gram = gram_ref[index]
            parts = split(gram)
            square = stacked(dot, parts, parts)
            quad = jnp.where(eye, second[at], 0.0) - third[at] * gram + square
            gram_ref[index] = quad * (norm[at] / first[at])
        for index in range(own):
            u = u_ref[index * count : (index + 1) * count, :]
            up = jnp.concatenate([u[:, :beams], u[:, beams:]], axis=0)
            value = stacked(dot, split(gram_ref[index]), split(up))
            high, low = split(value)
            th_ref[index] = beside(high, False)
            tl_ref[index] = beside(low, False)
            sums_ref[index : index + 1, :] = jnp.sum(up * value, axis=0, keepdims=True)
        gain = power - sums_ref[...]
        gain_ref[...] = 1.0 / (gain * gain)

    wide = jax.ShapeDtypeStruct((own, 2 * side, 2 * channels), BF16)
    turned = jax.ShapeDtypeStruct((own, side, 2 * beams), BF16)
    return pl.pallas_call(
        body,
        in_specs=[VMEM] * 3 + [SMEM] * 2,
        out_specs=[VMEM] * 4,
        out_shape=[wide, turned, turned, jax.ShapeDtypeStruct((own, beams), F32)],
        scratch_shapes=[
            pltpu.VMEM((own, side, channels), BF16),
            pltpu.VMEM((own, side, channels), BF16),
            pltpu.VMEM((own * count, 6 * channels), BF16),
            pltpu.VMEM((own, channels), F32),
            pltpu.VMEM((own, channels), F32),
            pltpu.VMEM((own * count, 2 * beams), F32),
            pltpu.VMEM((own, side, side), F32),
        ],
        compiler_params=pltpu.CompilerParams(vmem_limit_bytes=LIMIT),
        name="weights",
    )(mine, other, steer, range_taps, loading)


def near_kernel(blocks, conjugated, turned, steer, range_taps):
    steps = sorted(blocks)
    _, _, gates, own, _ = blocks[steps[0]].shape
    size = 4 * gates * own
    pitch = size + PAD
    wide = 4 * LANES
    side = conjugated.shape[1] // 2
    count = side // 2
    sections = count // gates
    beams = steer.shape[1] // 2

    def body(*refs):
        (b_ref, th_ref, tl_ref, steer_ref, taps_ref, out_ref,
         held, rows_ref, v_ref, cross_ref) = refs[len(steps) :]
        for step in range(sections):
            here = slice(step * pitch, step * pitch + size)
            held[here, :] = refs[steps.index(step)][...] if step in steps else jnp.zeros((size, LANES), F32)
        matrix = split(filter_matrix(taps_ref, gates, sections, lax.axis_index("section"), None, False))
        matrix = jnp.concatenate([matrix[0], matrix[1], matrix[0]], axis=1)
        for index in range(own):
            def load(half, part):
                return jnp.concatenate(
                    [held[pl.ds(((half * 2 + part) * gates + gate) * own + index, sections, stride=pitch), :]
                     for gate in range(gates)], axis=0)

            data = jnp.concatenate([load(half, part) for part in (0, 1) for half in (0, 1)], axis=1)
            high, low = split(data)
            here = slice(index * count, (index + 1) * count)
            for place, part in enumerate((high, low, high)):
                rows_ref[here, place * wide : (place + 1) * wide] = part
        for index in range(own):
            here = slice(index * count, (index + 1) * count)
            parts = jnp.concatenate([rows_ref[here, :wide], rows_ref[here, wide : 2 * wide]], axis=0)
            both = dot_nt(parts, b_ref[index])
            both = both[:count] + both[count:]
            cross_ref[index] = both[:, :side] + both[:, side:]
        v_ref[...] = dot(rows_ref[...], steer_ref[...])
        for index in range(own):
            here = slice(index * count, (index + 1) * count)
            low_rank = stacked(dot, split(cross_ref[index]), (th_ref[index], tl_ref[index]))
            v_ref[here, :] = v_ref[here, :] - low_rank
        for index in range(own):
            v = v_ref[index * count : (index + 1) * count, :]
            high, low = split(jnp.concatenate([v[:, :beams], v[:, beams:]], axis=0))
            out_ref[index] = dot(matrix, jnp.concatenate([high, high, low], axis=0))

    return pl.pallas_call(
        body,
        in_specs=[VMEM] * (len(steps) + 4) + [SMEM],
        out_specs=VMEM,
        out_shape=jax.ShapeDtypeStruct((own, side, beams), F32),
        scratch_shapes=[
            pltpu.VMEM((sections * pitch, LANES), F32),
            pltpu.VMEM((own * count, 3 * wide), BF16),
            pltpu.VMEM((own * count, 2 * beams), F32),
            pltpu.VMEM((own, count, side), F32),
        ],
        compiler_params=pltpu.CompilerParams(vmem_limit_bytes=LIMIT),
        name="near",
    )(*[blocks[step].reshape(size, LANES) for step in steps], conjugated, *turned, steer, range_taps)


def beams_kernel(blocks, near, weights, steer, range_taps):
    steps = sorted(blocks)
    _, _, gates, own, _ = blocks[steps[0]].shape
    size = 4 * gates * own
    side = near.shape[1]
    count = side // 2
    sections = count // gates
    beams = steer.shape[1] // 2
    each = len(steps) * gates
    group = 16 // each

    def body(*refs):
        (near_ref, b_ref, th_ref, tl_ref, gain_ref, steer_ref, taps_ref,
         power_ref, total_ref, dense) = refs[len(steps) :]
        for order in range(len(steps)):
            for half in (0, 1):
                for part in (0, 1):
                    for gate in range(gates):
                        start = ((half * 2 + part) * gates + gate) * own
                        at = pl.ds(order * gates + gate, own, stride=each)
                        dense[part * 2 + half, at, :] = refs[order][start : start + own, :]
        matrix = filter_matrix(taps_ref, gates, sections, lax.axis_index("section"), steps, False)
        first, second = split(matrix)
        first, second = first.astype(F32), second.astype(F32)
        matrix = jnp.concatenate([first, second, first], axis=1).astype(BF16)
        high, low = split(jnp.concatenate([dense[place] for place in range(4)], axis=1))
        value = dot(jnp.concatenate([high, low, high], axis=1), steer_ref[...])
        crosses = []
        for index in range(own):
            base = index // group * group * each
            rows = slice(base, base + group * each)
            parts = jnp.concatenate([high[rows], low[rows]], axis=0)
            both = dot_nt(parts, b_ref[index])
            both = both[: group * each] + both[group * each :]
            both = both[index * each - base : (index + 1) * each - base]
            crosses.append(both[:, :side] + both[:, side:])
        stacks = []
        for index in range(own):
            ch, cl = split(crosses[index])
            both = jnp.concatenate([ch.astype(F32), cl.astype(F32)], axis=0).astype(BF16)
            both = dot(both, th_ref[index]) + dot(both, tl_ref[index])
            v = value[index * each : (index + 1) * each, :] - (both[:each] + both[each:])
            high, low = split(jnp.concatenate([v[:, :beams], v[:, beams:]], axis=0))
            stacks.append(jnp.concatenate([high, high, low], axis=0))
        total = jnp.zeros((1, beams), F32)
        for index in range(own):
            out = near_ref[index] + dot(matrix, stacks[index])
            power = (out[:count] * out[:count] + out[count:] * out[count:]) * gain_ref[index : index + 1, :]
            total = total + jnp.sum(power, axis=0, keepdims=True)
            power_ref[index] = power
        total_ref[...] = jnp.broadcast_to(total, total_ref.shape)

    return pl.pallas_call(
        body,
        in_specs=[VMEM] * (len(steps) + 6) + [SMEM],
        out_specs=[VMEM] * 2,
        out_shape=[
            jax.ShapeDtypeStruct((own, count, beams), F32),
            jax.ShapeDtypeStruct((2 * sections, beams), F32),
        ],
        scratch_shapes=[pltpu.VMEM((4, own * each, LANES), F32)],
        compiler_params=pltpu.CompilerParams(vmem_limit_bytes=LIMIT),
        name="beams",
    )(*[blocks[step].reshape(size, LANES) for step in steps], near, *weights, steer, range_taps)


def steering_tables(beam_index, channel_phase):
    channels = channel_phase.shape[0]
    own = channels // 2
    sub = lax.axis_index("sub")
    place = jnp.arange(channels, dtype=jnp.int32)
    place = jnp.where(place + sub * own >= channels, place + sub * own - channels, place + sub * own)
    turned = jnp.concatenate([channel_phase[own:], channel_phase[:own]])
    phase = jnp.where(sub == 0, channel_phase, turned)
    direction = -1.0 + (2.0 * beam_index.astype(F32) + 1.0) / LOOKS
    angle = math.pi * place.astype(F32)[:, None] * direction[None, :] + phase[:, None]
    cosine, sine = jnp.cos(angle), jnp.sin(angle)
    table = jnp.concatenate(
        [jnp.concatenate([cosine, -sine], 1), jnp.concatenate([sine, cosine], 1)], 0
    )
    high = lax.reduce_precision(table, 8, 7)
    low = lax.reduce_precision(table - high, 8, 7).astype(BF16)
    high = high.astype(BF16)
    return jnp.concatenate([high, high, low], 0)


def permuted(block, sections, step):
    return lax.ppermute(block, "section", [(place, place ^ step) for place in range(sections)])


def swapped(block):
    return lax.ppermute(block, "sub", [(0, 1), (1, 0)])


def hop_order(sections):
    near, far = list(range(1, sections // 2)), list(range(sections // 2, sections))
    half = len(far) // 2
    return far[::-1] + near[::-1], far[:half][::-1] + near[::-1] + far[half:][::-1]


def factored_steps(echoes, range_taps, pulse_taper, channel_phase, loading, beam_index):
    parts, pulses, gates, lanes = echoes.shape
    sections = lax.axis_size("section")
    order = hop_order(sections)[0]
    view = echoes.reshape(parts, pulses // HOP, HOP * gates, lanes)
    taper = pulse_taper.reshape(2, HOP)

    sent = doppler(view, taper, sections, 0, False)
    got = {0: sent[0]}
    for step in order:
        got[step] = permuted(sent[step], sections, step)
    mine, theirs = doppler(view, taper, sections, 1, True)
    other = swapped(theirs)
    sent = pair_up(mine, other)
    later = {0: sent[0]}
    for step in order:
        later[step] = permuted(sent[step], sections, step)

    steer = steering_tables(beam_index, channel_phase)
    keep, pass_on = gather_sub([got[step] for step in range(sections)])
    other = swapped(pass_on)
    weights = weights_kernel(keep, other, steer, range_taps, loading)
    last = hop_order(sections)[1][-2:]
    blocks = {step: block for step, block in later.items() if step not in last}
    near = near_kernel(blocks, weights[0], weights[1:3], steer, range_taps)
    blocks = {step: later[step] for step in last}
    power, total = beams_kernel(blocks, near, weights, steer, range_taps)
    totals = lax.all_to_all(total, ("section", "sub"), 0, 0, tiled=True)
    noise_level = jnp.sum(totals, axis=0) / (PULSES * gates * sections)
    return (power / (noise_level + epsilon))[None]


def apply_taps(pad_real, pad_imag, range_taps, gate_count):
    axis_gates = pad_real.ndim - 2
    shape_out = pad_real.shape[:axis_gates] + (gate_count,) + pad_real.shape[axis_gates + 1 :]
    out_real = jnp.zeros(shape_out, jnp.float32)
    out_imag = jnp.zeros(shape_out, jnp.float32)
    for offset in range(range_taps.shape[1]):
        part_real = lax.slice_in_dim(pad_real, offset, offset + gate_count, axis=axis_gates)
        part_imag = lax.slice_in_dim(pad_imag, offset, offset + gate_count, axis=axis_gates)
        out_real = out_real + range_taps[0, offset] * part_real - range_taps[1, offset] * part_imag
        out_imag = out_imag + range_taps[0, offset] * part_imag + range_taps[1, offset] * part_real
    return (out_real, out_imag)


def doppler_table(pulse_taper):
    pulse_count = pulse_taper.shape[0]
    pulse_index = jnp.arange(pulse_count, dtype=jnp.int32)
    product = pulse_index[:, None] * pulse_index[None, :] % pulse_count
    phase_angle = 2.0 * math.pi / pulse_count * product.astype(jnp.float32)
    cosine = jnp.cos(phase_angle) * pulse_taper[None, :]
    sine_part = jnp.sin(phase_angle) * pulse_taper[None, :]
    upper_rows = jnp.concatenate([cosine, sine_part], axis=1)
    lower_rows = jnp.concatenate([-sine_part, cosine], axis=1)
    return jnp.concatenate([upper_rows, lower_rows], axis=0)


def transform(doppler, segment):
    shape_in = segment.shape
    flattened = segment.reshape(shape_in[0] * shape_in[1], -1)
    result = jnp.dot(doppler, flattened, precision=precise, preferred_element_type=jnp.float32)
    return result.reshape(shape_in)


def batched(first, second):
    return jnp.einsum("dij,djk->dik", first, second, precision=precise)


def complex_product(left_real, left_imag, right_real, right_imag):
    out_real = batched(left_real, right_real) - batched(left_imag, right_imag)
    out_imag = batched(left_real, right_imag) + batched(left_imag, right_real)
    return (out_real, out_imag)


def gram_product(first, second):
    return jnp.einsum("dgi,dgj->dij", first, second, precision=precise)


def loaded_inverse(real_part, imag_part, loading):
    gate_count = real_part.shape[1]
    channels = real_part.shape[2]
    cov_real = (
        gram_product(real_part, real_part) + gram_product(imag_part, imag_part)
    ) / gate_count
    cov_imag = (
        gram_product(real_part, imag_part) - gram_product(imag_part, real_part)
    ) / gate_count
    identity = jnp.eye(channels, dtype=jnp.float32)
    trace_sum = jnp.sum(cov_real * identity[None], axis=(1, 2))
    cov_real = cov_real + (loading[0] * trace_sum / channels)[:, None, None] * identity[None]
    row_bound = jnp.max(jnp.sum(jnp.abs(cov_real) + jnp.abs(cov_imag), axis=2), axis=1)
    inv_real = identity[None] / row_bound[:, None, None]
    inv_imag = jnp.zeros_like(inv_real)
    for _ in range(ITERS):
        prod_real, prod_imag = complex_product(cov_real, cov_imag, inv_real, inv_imag)
        inv_real, inv_imag = complex_product(
            inv_real, inv_imag, 2.0 * identity[None] - prod_real, -prod_imag
        )
    return (inv_real, inv_imag)


def steering(beam_index, channel_phase):
    channels = channel_phase.shape[0]
    direction = -1.0 + (2.0 * beam_index.astype(jnp.float32) + 1.0) / LOOKS
    phase_angle = (
        math.pi * jnp.arange(channels, dtype=jnp.float32)[:, None] * direction[None, :]
        + channel_phase[:, None]
    )
    return (jnp.cos(phase_angle), jnp.sin(phase_angle))


def beam_weights(inv_real, inv_imag, steer_real, steer_imag):
    weight_real = jnp.einsum("dij,jb->dib", inv_real, steer_real, precision=precise) - jnp.einsum(
        "dij,jb->dib", inv_imag, steer_imag, precision=precise
    )
    weight_imag = jnp.einsum("dij,jb->dib", inv_real, steer_imag, precision=precise) + jnp.einsum(
        "dij,jb->dib", inv_imag, steer_real, precision=precise
    )
    gain_norm = jnp.sum(steer_real[None] * weight_real + steer_imag[None] * weight_imag, axis=1)
    return (weight_real / gain_norm[:, None, :], weight_imag / gain_norm[:, None, :])


def form_beams(data_real, data_imag, weight_real, weight_imag):
    out_real = jnp.einsum("dgc,dcb->dgb", data_real, weight_real, precision=precise) + jnp.einsum(
        "dgc,dcb->dgb", data_imag, weight_imag, precision=precise
    )
    out_imag = jnp.einsum("dgc,dcb->dgb", data_imag, weight_real, precision=precise) - jnp.einsum(
        "dgc,dcb->dgb", data_real, weight_imag, precision=precise
    )
    return out_real * out_real + out_imag * out_imag


def on_device(echoes, range_taps, pulse_taper, channel_phase, loading, beam_index):
    rim_width = range_taps.shape[1] // 2
    doppler = doppler_table(pulse_taper)
    spectra = [
        transform(
            doppler, lax.slice_in_dim(echoes, interval * HOP, interval * HOP + PULSES, axis=1)
        )
        for interval in range(INTERVALS)
    ]
    turned = [
        lax.all_to_all(
            lax.all_to_all(spectrum, "section", split_axis=1, concat_axis=2, tiled=True),
            "sub",
            split_axis=1,
            concat_axis=3,
            tiled=True,
        )
        for spectrum in spectra
    ]
    refined = []
    for spectrum in turned:
        padded_bins = jnp.pad(spectrum, ((0, 0), (0, 0), (rim_width, rim_width), (0, 0)))
        part_real, part_imag = apply_taps(
            padded_bins[0], padded_bins[1], range_taps, spectrum.shape[2]
        )
        refined.append(jnp.stack([part_real, part_imag]))
    turned = refined
    steer_real, steer_imag = steering(beam_index, channel_phase)
    interval = 0
    inv_real, inv_imag = loaded_inverse(turned[interval][0], turned[interval][1], loading)
    weight_real, weight_imag = beam_weights(inv_real, inv_imag, steer_real, steer_imag)
    beam_power = form_beams(
        turned[interval + 1][0], turned[interval + 1][1], weight_real, weight_imag
    )
    partials = [jnp.sum(beam_power, axis=(0, 1))]
    totals = lax.psum(jnp.stack(partials), ("section", "sub"))
    noise_level = totals / (PULSES * turned[0].shape[2])
    return jnp.stack([beam_power / (noise_level[0] + epsilon)])


def solution(mesh):
    in_specs = (P("groups", None, "section", "sub"), P(), P(), P(), P(), P())
    out_specs = P("groups", ("section", "sub"), None, None)
    sections = mesh.shape["section"]
    small = sections == 8 and mesh.shape["sub"] == 2

    def run(echoes, range_taps, pulse_taper, channel_phase, loading, beam_index):
        args = (echoes, range_taps, pulse_taper, channel_phase, loading, beam_index)
        fits = small and echoes.shape[2] == 4 and echoes.shape[3] == LANES
        return factored_steps(*args) if fits else on_device(*args)

    return jax.shard_map(run, mesh=mesh, in_specs=in_specs, out_specs=out_specs, check_vma=False)
```

```python
import math

import jax
import jax.numpy as jnp
import numpy as np
from jax import lax
from jax.experimental import pallas as pl
from jax.experimental.pallas import tpu as pltpu
from jax.sharding import PartitionSpec as P


PULSES = 256
INTERVALS = 2
ITERS = 2
LOOKS = 1024
HOP = 128


precise = lax.Precision.HIGHEST
epsilon = 1e-06
F32 = jnp.float32
BF16 = jnp.bfloat16
LANES = 128
VMEM = pl.BlockSpec(memory_space=pltpu.VMEM)
SMEM = pl.BlockSpec(memory_space=pltpu.SMEM)
HBM = pl.BlockSpec(memory_space=pltpu.HBM)
LIMIT = 16 << 20
PAD = 8


def split(value):
    high = value.astype(BF16)
    return high, (value - high.astype(F32)).astype(BF16)


def dot(left, right):
    return jnp.dot(left, right, preferred_element_type=F32)


def dot_nt(left, right):
    return lax.dot_general(left, right, (((1,), (1,)), ((), ())), preferred_element_type=F32)


def dot_tn(left, right):
    return lax.dot_general(left, right, (((0,), (0,)), ((), ())), preferred_element_type=F32)


def triple(product, left, right):
    return product(left[0], right[0]) + (product(left[0], right[1]) + product(left[1], right[0]))


def doppler_tables(pulses):
    half = pulses // 2
    bins = np.arange(half)[:, None]
    tables = []
    for parity in (0, 1):
        phase = 2.0 * np.pi * ((bins * np.arange(parity, pulses, 2)[None, :]) % pulses) / pulses
        cosine, sine = np.cos(phase), np.sin(phase)
        table = np.concatenate([cosine, sine], 1).astype(np.float32)
        high = table.astype(jnp.bfloat16)
        tables += [high, (table - high.astype(np.float32)).astype(jnp.bfloat16)]
    return np.stack(tables)


def full_table(rows):
    half = rows.shape[1] // 2
    turned = jnp.concatenate([-rows[:, half:], rows[:, :half]], axis=1)
    return jnp.concatenate([rows, turned], axis=0)


def doppler_body(gates, hop, view_ref, table_ref, result, tapers):
    half = hop
    for group in range(0, gates, 2):
        members = range(group, min(group + 2, gates))
        for parity in (0, 1):
            rows = []
            for part in (0, 1):
                for segment in (0, 1):
                    taper = tapers[pl.ds(segment * hop + parity, hop // 2, stride=2), :]
                    blocks = []
                    for gate in members:
                        at = pl.ds(parity * gates + gate, hop // 2, stride=2 * gates)
                        blocks.append(view_ref[part, segment, at, :] * taper)
                    rows.append(jnp.concatenate(blocks, axis=1))
            data = split(jnp.concatenate(rows, axis=0))
            table = full_table(table_ref[2 * parity]), full_table(table_ref[2 * parity + 1])
            value = triple(dot, table, data)
            if parity == 0:
                even = value
        for place, gate in enumerate(members):
            lanes = slice(place * LANES, (place + 1) * LANES)
            for part in (0, 1):
                own = slice(part * half, (part + 1) * half)
                result[part, gate, :half] = even[own, lanes] + value[own, lanes]
                result[part, gate, half:] = even[own, lanes] - value[own, lanes]


def doppler(view, taper, sections, interval, split_sub):
    gates = view.shape[2] // HOP
    per = PULSES // sections
    own = per // 2

    def body(view_ref, taper_ref, table_ref, *rest):
        outs = 2 if split_sub else sections
        out_refs, scratch = rest[:outs], rest[outs:]
        result, tapers, own_view, own_taper, own_table, sems = scratch
        copies = [pltpu.make_async_copy(taper_ref, own_taper, sems.at[0])]
        copies.append(pltpu.make_async_copy(table_ref, own_table, sems.at[1]))
        for part in (0, 1):
            blocks = view_ref.at[part, pl.ds(interval, 2)]
            copies.append(pltpu.make_async_copy(blocks, own_view.at[part], sems.at[2 + part]))
        for copy in copies:
            copy.start()
        copies[0].wait()
        for segment in (0, 1):
            row = own_taper[segment : segment + 1, :]
            tapers[segment * HOP : (segment + 1) * HOP, :] = jnp.broadcast_to(row, (HOP, HOP)).T
        for copy in copies[1:]:
            copy.wait()
        doppler_body(gates, HOP, own_view, own_table, result, tapers)
        section = lax.axis_index("section")
        if not split_sub:
            for step in range(sections):
                start = pl.multiple_of(jnp.bitwise_xor(section, step) * per, per)
                out_refs[step][...] = result[:, :, pl.ds(start, per), :]
        else:
            sub = lax.axis_index("sub")
            for step in range(sections):
                start = jnp.bitwise_xor(section, step) * per
                mine = pl.multiple_of(start + sub * own, own)
                theirs = pl.multiple_of(start + (1 - sub) * own, own)
                out_refs[0][step] = result[:, :, pl.ds(mine, own), :]
                out_refs[1][step] = result[:, :, pl.ds(theirs, own), :]

    tables = jnp.asarray(doppler_tables(PULSES))
    if split_sub:
        shape = (sections, 2, gates, own, LANES)
        outs = [jax.ShapeDtypeStruct(shape, F32)] * 2
    else:
        shape = (2, gates, per, LANES)
        outs = [jax.ShapeDtypeStruct(shape, F32)] * sections
    return pl.pallas_call(
        body,
        in_specs=[HBM] * 3,
        out_specs=[VMEM] * len(outs),
        out_shape=outs,
        scratch_shapes=[
            pltpu.VMEM((2, gates, PULSES, LANES), F32),
            pltpu.VMEM((PULSES, LANES), F32),
            pltpu.VMEM((view.shape[0], 2) + view.shape[2:], F32),
            pltpu.VMEM(taper.shape, F32),
            pltpu.VMEM(tables.shape, BF16),
            pltpu.SemaphoreType.DMA((4,)),
        ],
        compiler_params=pltpu.CompilerParams(vmem_limit_bytes=LIMIT),
    )(*[pltpu.with_memory_space_constraint(v, pltpu.HBM) for v in (view, taper, tables)])


def gather_sub(blocks):
    sections = len(blocks)
    _, gates, per, _ = blocks[0].shape
    own = per // 2

    def body(*refs):
        section, sub = lax.axis_index("section"), lax.axis_index("sub")
        mine = pl.multiple_of(sub * own, own)
        theirs = pl.multiple_of((1 - sub) * own, own)
        for step in range(sections):
            source = jnp.bitwise_xor(section, step)
            refs[sections][source] = refs[step][:, :, pl.ds(mine, own), :]
            refs[sections + 1][source] = refs[step][:, :, pl.ds(theirs, own), :]

    shape = jax.ShapeDtypeStruct((sections, 2, gates, own, LANES), F32)
    return pl.pallas_call(
        body,
        in_specs=[VMEM] * sections,
        out_specs=[VMEM] * 2,
        out_shape=[shape] * 2,
        compiler_params=pltpu.CompilerParams(vmem_limit_bytes=LIMIT),
        name="gather_sub",
    )(*blocks)


def pair_up(mine, other):
    sections = mine.shape[0]

    def body(mine_ref, other_ref, *out_refs):
        for step in range(sections):
            out_refs[step][0] = mine_ref[step]
            out_refs[step][1] = other_ref[step]

    shape = jax.ShapeDtypeStruct((2,) + mine.shape[1:], F32)
    return pl.pallas_call(
        body,
        in_specs=[VMEM] * 2,
        out_specs=[VMEM] * sections,
        out_shape=[shape] * sections,
        compiler_params=pltpu.CompilerParams(vmem_limit_bytes=LIMIT),
        name="pair_up",
    )(mine, other)


def filter_matrix(taps_ref, gates, sections, section, steps, conjugate):
    count = gates * sections
    half = count if steps is None else len(steps) * gates
    taps = taps_ref.shape[1]
    row = lax.broadcasted_iota(jnp.int32, (2 * count, 2 * half), 0)
    column = lax.broadcasted_iota(jnp.int32, (2 * count, 2 * half), 1)
    row_imag, column_imag = row >= count, column >= half
    row_gate = jnp.where(row_imag, row - count, row)
    place = jnp.where(column_imag, column - half, column)
    if steps is None:
        inner = sum(jnp.where(place >= gate * sections, 1, 0) for gate in range(1, gates))
        step = place - inner * sections
    else:
        outer = sum(jnp.where(place >= order * gates, 1, 0) for order in range(1, len(steps)))
        inner = place - outer * gates
        step = jnp.full(place.shape, steps[0], jnp.int32)
        for order in range(1, len(steps)):
            step = jnp.where(outer >= order, steps[order], step)
    column_gate = jnp.bitwise_xor(step, section) * gates + inner
    tap = column_gate - row_gate + taps // 2
    real = sum(jnp.where(tap == j, taps_ref[0, j], 0.0) for j in range(taps))
    imag = sum(jnp.where(tap == j, taps_ref[1, j], 0.0) for j in range(taps))
    straight, crossed = row_imag == column_imag, jnp.where(row_imag, imag, -imag)
    matrix = jnp.where(straight, real, crossed)
    if conjugate:
        matrix = jnp.where(row_imag, -matrix, matrix)
    return matrix


def stacked(product, left, right):
    rows = left[0].shape[0]
    both = product(jnp.concatenate(left, axis=0), right[0])
    return both[:rows] + (both[rows:] + product(left[0], right[1]))


def beside(value, negate_first):
    count = value.shape[0] // 2
    real, imag = value[:count], value[count:]
    if negate_first:
        return jnp.concatenate(
            [jnp.concatenate([real, -imag], axis=1), jnp.concatenate([imag, real], axis=1)], axis=0
        )
    return jnp.concatenate(
        [jnp.concatenate([real, imag], axis=1), jnp.concatenate([-imag, real], axis=1)], axis=0
    )


def weights_kernel(mine, other, steer, range_taps, loading):
    sections, _, gates, own, _ = mine.shape
    count = sections * gates
    side = 2 * count
    channels = 2 * LANES
    beams = steer.shape[1] // 2
    stride = 2 * gates * own
    mine = mine.reshape(sections * stride, LANES)
    other = other.reshape(sections * stride, LANES)

    def body(mine_ref, other_ref, steer_ref, taps_ref, load_ref,
             b_ref, th_ref, tl_ref, gain_ref,
             ah_ref, al_ref, rows_ref, sums_ref, squares_ref, u_ref, gram_ref):
        matrix = split(filter_matrix(taps_ref, gates, sections, 0, None, True))
        for index in range(own):
            def load(ref):
                return jnp.concatenate(
                    [ref[pl.ds((part * gates + gate) * own + index, sections, stride=stride), :]
                     for part in (0, 1) for gate in range(gates)], axis=0)

            data = jnp.concatenate([load(mine_ref), load(other_ref)], axis=1)
            value = stacked(dot, matrix, split(data))
            squares_ref[index : index + 1, :] = jnp.sum(value * value, axis=0, keepdims=True)
            high, low = split(value)
            ah_ref[index] = high
            al_ref[index] = low
            b_ref[index, :side] = beside(high, False)
            b_ref[index, side:] = beside(low, False)
            here = slice(index * count, (index + 1) * count)
            for place, part in enumerate((high, low, high)):
                lanes = slice(place * 2 * channels, (place + 1) * 2 * channels)
                rows_ref[here, lanes] = jnp.concatenate([part[:count], part[count:]], axis=1)
        for index in range(own):
            high, low = ah_ref[index], al_ref[index]
            turn = lambda v: jnp.concatenate(
                [v, jnp.concatenate([v[count:], -v[:count]], axis=0)], axis=1
            )
            rh, rl = turn(high), turn(low)
            left = jnp.concatenate([high, high, low], axis=0)
            right = jnp.concatenate([rh, rl, rh], axis=0)
            cov = jnp.abs(dot_tn(left, right))
            sums_ref[index : index + 1, :] = jnp.sum(
                cov[:, :channels] + cov[:, channels:], axis=0, keepdims=True
            )
        bound = jnp.max(sums_ref[...], axis=1, keepdims=True) / count
        trace = jnp.sum(squares_ref[...], axis=1, keepdims=True) / count
        delta = load_ref[0] * trace / channels
        bound = bound + delta
        ratio = 1.0 - delta / bound
        first = 1.0 + ratio * (1.0 + ratio * (1.0 + ratio))
        second = 1.0 + ratio * (2.0 + 3.0 * ratio)
        third = 1.0 + 3.0 * ratio
        norm = 1.0 / (count * bound)
        u_ref[...] = dot(rows_ref[...], steer_ref[...])
        low_at = 2 * 2 * channels
        table = steer_ref[:channels, :].astype(F32) + steer_ref[low_at : low_at + channels, :].astype(F32)
        power = jnp.sum(table * table, axis=0, keepdims=True)
        power = power[:, :beams] + power[:, beams:]
        eye = (
            lax.broadcasted_iota(jnp.int32, (side, side), 0)
            == lax.broadcasted_iota(jnp.int32, (side, side), 1)
        )
        for index in range(own):
            at = slice(index, index + 1)
            halves = beside(ah_ref[index], True), beside(al_ref[index], True)
            gram_ref[index] = stacked(dot_nt, halves, halves) * norm[at]
        for index in range(own):
            at = slice(index, index + 1)
            gram = gram_ref[index]
            parts = split(gram)
            square = stacked(dot, parts, parts)
            quad = jnp.where(eye, second[at], 0.0) - third[at] * gram + square
            gram_ref[index] = quad * (norm[at] / first[at])
        for index in range(own):
            u = u_ref[index * count : (index + 1) * count, :]
            up = jnp.concatenate([u[:, :beams], u[:, beams:]], axis=0)
            value = stacked(dot, split(gram_ref[index]), split(up))
            high, low = split(value)
            th_ref[index] = beside(high, False)
            tl_ref[index] = beside(low, False)
            sums_ref[index : index + 1, :] = jnp.sum(up * value, axis=0, keepdims=True)
        gain = power - sums_ref[...]
        gain_ref[...] = 1.0 / (gain * gain)

    wide = jax.ShapeDtypeStruct((own, 2 * side, 2 * channels), BF16)
    turned = jax.ShapeDtypeStruct((own, side, 2 * beams), BF16)
    return pl.pallas_call(
        body,
        in_specs=[VMEM] * 3 + [SMEM] * 2,
        out_specs=[VMEM] * 4,
        out_shape=[wide, turned, turned, jax.ShapeDtypeStruct((own, beams), F32)],
        scratch_shapes=[
            pltpu.VMEM((own, side, channels), BF16),
            pltpu.VMEM((own, side, channels), BF16),
            pltpu.VMEM((own * count, 6 * channels), BF16),
            pltpu.VMEM((own, channels), F32),
            pltpu.VMEM((own, channels), F32),
            pltpu.VMEM((own * count, 2 * beams), F32),
            pltpu.VMEM((own, side, side), F32),
        ],
        compiler_params=pltpu.CompilerParams(vmem_limit_bytes=LIMIT),
        name="weights",
    )(mine, other, steer, range_taps, loading)


def near_kernel(blocks, conjugated, turned, steer, range_taps):
    steps = sorted(blocks)
    _, _, gates, own, _ = blocks[steps[0]].shape
    size = 4 * gates * own
    pitch = size + PAD
    wide = 4 * LANES
    side = conjugated.shape[1] // 2
    count = side // 2
    sections = count // gates
    beams = steer.shape[1] // 2

    def body(*refs):
        (b_ref, th_ref, tl_ref, steer_ref, taps_ref, out_ref,
         held, rows_ref, v_ref, cross_ref) = refs[len(steps) :]
        for step in range(sections):
            here = slice(step * pitch, step * pitch + size)
            held[here, :] = refs[steps.index(step)][...] if step in steps else jnp.zeros((size, LANES), F32)
        matrix = split(filter_matrix(taps_ref, gates, sections, lax.axis_index("section"), None, False))
        matrix = jnp.concatenate([matrix[0], matrix[1], matrix[0]], axis=1)
        for index in range(own):
            def load(half, part):
                return jnp.concatenate(
                    [held[pl.ds(((half * 2 + part) * gates + gate) * own + index, sections, stride=pitch), :]
                     for gate in range(gates)], axis=0)

            data = jnp.concatenate([load(half, part) for part in (0, 1) for half in (0, 1)], axis=1)
            high, low = split(data)
            here = slice(index * count, (index + 1) * count)
            for place, part in enumerate((high, low, high)):
                rows_ref[here, place * wide : (place + 1) * wide] = part
        for index in range(own):
            here = slice(index * count, (index + 1) * count)
            parts = jnp.concatenate([rows_ref[here, :wide], rows_ref[here, wide : 2 * wide]], axis=0)
            both = dot_nt(parts, b_ref[index])
            both = both[:count] + both[count:]
            cross_ref[index] = both[:, :side] + both[:, side:]
        v_ref[...] = dot(rows_ref[...], steer_ref[...])
        for index in range(own):
            here = slice(index * count, (index + 1) * count)
            low_rank = stacked(dot, split(cross_ref[index]), (th_ref[index], tl_ref[index]))
            v_ref[here, :] = v_ref[here, :] - low_rank
        for index in range(own):
            v = v_ref[index * count : (index + 1) * count, :]
            high, low = split(jnp.concatenate([v[:, :beams], v[:, beams:]], axis=0))
            out_ref[index] = dot(matrix, jnp.concatenate([high, high, low], axis=0))

    return pl.pallas_call(
        body,
        in_specs=[VMEM] * (len(steps) + 4) + [SMEM],
        out_specs=VMEM,
        out_shape=jax.ShapeDtypeStruct((own, side, beams), F32),
        scratch_shapes=[
            pltpu.VMEM((sections * pitch, LANES), F32),
            pltpu.VMEM((own * count, 3 * wide), BF16),
            pltpu.VMEM((own * count, 2 * beams), F32),
            pltpu.VMEM((own, count, side), F32),
        ],
        compiler_params=pltpu.CompilerParams(vmem_limit_bytes=LIMIT),
        name="near",
    )(*[blocks[step].reshape(size, LANES) for step in steps], conjugated, *turned, steer, range_taps)


def beams_kernel(blocks, near, weights, steer, range_taps):
    steps = sorted(blocks)
    _, _, gates, own, _ = blocks[steps[0]].shape
    size = 4 * gates * own
    side = near.shape[1]
    count = side // 2
    sections = count // gates
    beams = steer.shape[1] // 2
    each = len(steps) * gates
    group = 16 // each

    def body(*refs):
        (near_ref, b_ref, th_ref, tl_ref, gain_ref, steer_ref, taps_ref,
         power_ref, total_ref, dense) = refs[len(steps) :]
        for order in range(len(steps)):
            for half in (0, 1):
                for part in (0, 1):
                    for gate in range(gates):
                        start = ((half * 2 + part) * gates + gate) * own
                        at = pl.ds(order * gates + gate, own, stride=each)
                        dense[part * 2 + half, at, :] = refs[order][start : start + own, :]
        matrix = filter_matrix(taps_ref, gates, sections, lax.axis_index("section"), steps, False)
        first, second = split(matrix)
        first, second = first.astype(F32), second.astype(F32)
        matrix = jnp.concatenate([first, second, first], axis=1).astype(BF16)
        high, low = split(jnp.concatenate([dense[place] for place in range(4)], axis=1))
        value = dot(jnp.concatenate([high, low, high], axis=1), steer_ref[...])
        crosses = []
        for index in range(own):
            base = index // group * group * each
            rows = slice(base, base + group * each)
            parts = jnp.concatenate([high[rows], low[rows]], axis=0)
            both = dot_nt(parts, b_ref[index])
            both = both[: group * each] + both[group * each :]
            both = both[index * each - base : (index + 1) * each - base]
            crosses.append(both[:, :side] + both[:, side:])
        stacks = []
        for index in range(own):
            ch, cl = split(crosses[index])
            both = jnp.concatenate([ch.astype(F32), cl.astype(F32)], axis=0).astype(BF16)
            both = dot(both, th_ref[index]) + dot(both, tl_ref[index])
            v = value[index * each : (index + 1) * each, :] - (both[:each] + both[each:])
            high, low = split(jnp.concatenate([v[:, :beams], v[:, beams:]], axis=0))
            stacks.append(jnp.concatenate([high, high, low], axis=0))
        total = jnp.zeros((1, beams), F32)
        for index in range(own):
            out = near_ref[index] + dot(matrix, stacks[index])
            power = (out[:count] * out[:count] + out[count:] * out[count:]) * gain_ref[index : index + 1, :]
            total = total + jnp.sum(power, axis=0, keepdims=True)
            power_ref[index] = power
        total_ref[...] = jnp.broadcast_to(total, total_ref.shape)

    return pl.pallas_call(
        body,
        in_specs=[VMEM] * (len(steps) + 6) + [SMEM],
        out_specs=[VMEM] * 2,
        out_shape=[
            jax.ShapeDtypeStruct((own, count, beams), F32),
            jax.ShapeDtypeStruct((2 * sections, beams), F32),
        ],
        scratch_shapes=[pltpu.VMEM((4, own * each, LANES), F32)],
        compiler_params=pltpu.CompilerParams(vmem_limit_bytes=LIMIT),
        name="beams",
    )(*[blocks[step].reshape(size, LANES) for step in steps], near, *weights, steer, range_taps)


def scaled(power, totals, samples):
    own, chunks = power.shape[0], 4
    each = own // chunks

    def body(power_ref, totals_ref, out_ref, held, sems):
        noise_level = jnp.sum(totals_ref[...], axis=0, keepdims=True) / samples
        factor = 1.0 / (noise_level + epsilon)
        copies = []
        for chunk in range(chunks):
            here = pl.ds(chunk * each, each)
            held[here] = power_ref[here] * factor[None]
            copies.append(pltpu.make_async_copy(held.at[here], out_ref.at[here], sems.at[chunk]))
            copies[-1].start()
        for copy in copies:
            copy.wait()

    return pl.pallas_call(
        body,
        in_specs=[VMEM] * 2,
        out_specs=HBM,
        out_shape=jax.ShapeDtypeStruct(power.shape, F32),
        scratch_shapes=[pltpu.VMEM(power.shape, F32), pltpu.SemaphoreType.DMA((chunks,))],
        compiler_params=pltpu.CompilerParams(vmem_limit_bytes=LIMIT),
        name="scaled",
    )(power, totals)


def steering_tables(beam_index, channel_phase):
    channels = channel_phase.shape[0]
    own = channels // 2
    sub = lax.axis_index("sub")
    place = jnp.arange(channels, dtype=jnp.int32)
    place = jnp.where(place + sub * own >= channels, place + sub * own - channels, place + sub * own)
    turned = jnp.concatenate([channel_phase[own:], channel_phase[:own]])
    phase = jnp.where(sub == 0, channel_phase, turned)
    direction = -1.0 + (2.0 * beam_index.astype(F32) + 1.0) / LOOKS
    angle = math.pi * place.astype(F32)[:, None] * direction[None, :] + phase[:, None]
    cosine, sine = jnp.cos(angle), jnp.sin(angle)
    table = jnp.concatenate(
        [jnp.concatenate([cosine, -sine], 1), jnp.concatenate([sine, cosine], 1)], 0
    )
    high = lax.reduce_precision(table, 8, 7)
    low = lax.reduce_precision(table - high, 8, 7).astype(BF16)
    high = high.astype(BF16)
    return jnp.concatenate([high, high, low], 0)


def permuted(block, sections, step):
    return lax.ppermute(block, "section", [(place, place ^ step) for place in range(sections)])


def swapped(block):
    return lax.ppermute(block, "sub", [(0, 1), (1, 0)])


def hop_order(sections):
    near, far = list(range(1, sections // 2)), list(range(sections // 2, sections))
    half = len(far) // 2
    return far[::-1] + near[::-1], far[:half][::-1] + near[::-1] + far[half:][::-1]


def factored_steps(echoes, range_taps, pulse_taper, channel_phase, loading, beam_index):
    parts, pulses, gates, lanes = echoes.shape
    sections = lax.axis_size("section")
    order = hop_order(sections)[0]
    view = echoes.reshape(parts, pulses // HOP, HOP * gates, lanes)
    taper = pulse_taper.reshape(2, HOP)

    sent = doppler(view, taper, sections, 0, False)
    got = {0: sent[0]}
    for step in order:
        got[step] = permuted(sent[step], sections, step)
    mine, theirs = doppler(view, taper, sections, 1, True)
    other = swapped(theirs)
    sent = pair_up(mine, other)
    later = {0: sent[0]}
    for step in order:
        later[step] = permuted(sent[step], sections, step)

    steer = steering_tables(beam_index, channel_phase)
    keep, pass_on = gather_sub([got[step] for step in range(sections)])
    other = swapped(pass_on)
    weights = weights_kernel(keep, other, steer, range_taps, loading)
    last = hop_order(sections)[1][-2:]
    blocks = {step: block for step, block in later.items() if step not in last}
    near = near_kernel(blocks, weights[0], weights[1:3], steer, range_taps)
    blocks = {step: later[step] for step in last}
    power, total = beams_kernel(blocks, near, weights, steer, range_taps)
    totals = lax.all_to_all(total, ("section", "sub"), 0, 0, tiled=True)
    return scaled(power, totals, PULSES * gates * sections)[None]


def apply_taps(pad_real, pad_imag, range_taps, gate_count):
    axis_gates = pad_real.ndim - 2
    shape_out = pad_real.shape[:axis_gates] + (gate_count,) + pad_real.shape[axis_gates + 1 :]
    out_real = jnp.zeros(shape_out, jnp.float32)
    out_imag = jnp.zeros(shape_out, jnp.float32)
    for offset in range(range_taps.shape[1]):
        part_real = lax.slice_in_dim(pad_real, offset, offset + gate_count, axis=axis_gates)
        part_imag = lax.slice_in_dim(pad_imag, offset, offset + gate_count, axis=axis_gates)
        out_real = out_real + range_taps[0, offset] * part_real - range_taps[1, offset] * part_imag
        out_imag = out_imag + range_taps[0, offset] * part_imag + range_taps[1, offset] * part_real
    return (out_real, out_imag)


def doppler_table(pulse_taper):
    pulse_count = pulse_taper.shape[0]
    pulse_index = jnp.arange(pulse_count, dtype=jnp.int32)
    product = pulse_index[:, None] * pulse_index[None, :] % pulse_count
    phase_angle = 2.0 * math.pi / pulse_count * product.astype(jnp.float32)
    cosine = jnp.cos(phase_angle) * pulse_taper[None, :]
    sine_part = jnp.sin(phase_angle) * pulse_taper[None, :]
    upper_rows = jnp.concatenate([cosine, sine_part], axis=1)
    lower_rows = jnp.concatenate([-sine_part, cosine], axis=1)
    return jnp.concatenate([upper_rows, lower_rows], axis=0)


def transform(doppler, segment):
    shape_in = segment.shape
    flattened = segment.reshape(shape_in[0] * shape_in[1], -1)
    result = jnp.dot(doppler, flattened, precision=precise, preferred_element_type=jnp.float32)
    return result.reshape(shape_in)


def batched(first, second):
    return jnp.einsum("dij,djk->dik", first, second, precision=precise)


def complex_product(left_real, left_imag, right_real, right_imag):
    out_real = batched(left_real, right_real) - batched(left_imag, right_imag)
    out_imag = batched(left_real, right_imag) + batched(left_imag, right_real)
    return (out_real, out_imag)


def gram_product(first, second):
    return jnp.einsum("dgi,dgj->dij", first, second, precision=precise)


def loaded_inverse(real_part, imag_part, loading):
    gate_count = real_part.shape[1]
    channels = real_part.shape[2]
    cov_real = (
        gram_product(real_part, real_part) + gram_product(imag_part, imag_part)
    ) / gate_count
    cov_imag = (
        gram_product(real_part, imag_part) - gram_product(imag_part, real_part)
    ) / gate_count
    identity = jnp.eye(channels, dtype=jnp.float32)
    trace_sum = jnp.sum(cov_real * identity[None], axis=(1, 2))
    cov_real = cov_real + (loading[0] * trace_sum / channels)[:, None, None] * identity[None]
    row_bound = jnp.max(jnp.sum(jnp.abs(cov_real) + jnp.abs(cov_imag), axis=2), axis=1)
    inv_real = identity[None] / row_bound[:, None, None]
    inv_imag = jnp.zeros_like(inv_real)
    for _ in range(ITERS):
        prod_real, prod_imag = complex_product(cov_real, cov_imag, inv_real, inv_imag)
        inv_real, inv_imag = complex_product(
            inv_real, inv_imag, 2.0 * identity[None] - prod_real, -prod_imag
        )
    return (inv_real, inv_imag)


def steering(beam_index, channel_phase):
    channels = channel_phase.shape[0]
    direction = -1.0 + (2.0 * beam_index.astype(jnp.float32) + 1.0) / LOOKS
    phase_angle = (
        math.pi * jnp.arange(channels, dtype=jnp.float32)[:, None] * direction[None, :]
        + channel_phase[:, None]
    )
    return (jnp.cos(phase_angle), jnp.sin(phase_angle))


def beam_weights(inv_real, inv_imag, steer_real, steer_imag):
    weight_real = jnp.einsum("dij,jb->dib", inv_real, steer_real, precision=precise) - jnp.einsum(
        "dij,jb->dib", inv_imag, steer_imag, precision=precise
    )
    weight_imag = jnp.einsum("dij,jb->dib", inv_real, steer_imag, precision=precise) + jnp.einsum(
        "dij,jb->dib", inv_imag, steer_real, precision=precise
    )
    gain_norm = jnp.sum(steer_real[None] * weight_real + steer_imag[None] * weight_imag, axis=1)
    return (weight_real / gain_norm[:, None, :], weight_imag / gain_norm[:, None, :])


def form_beams(data_real, data_imag, weight_real, weight_imag):
    out_real = jnp.einsum("dgc,dcb->dgb", data_real, weight_real, precision=precise) + jnp.einsum(
        "dgc,dcb->dgb", data_imag, weight_imag, precision=precise
    )
    out_imag = jnp.einsum("dgc,dcb->dgb", data_imag, weight_real, precision=precise) - jnp.einsum(
        "dgc,dcb->dgb", data_real, weight_imag, precision=precise
    )
    return out_real * out_real + out_imag * out_imag


def on_device(echoes, range_taps, pulse_taper, channel_phase, loading, beam_index):
    rim_width = range_taps.shape[1] // 2
    doppler = doppler_table(pulse_taper)
    spectra = [
        transform(
            doppler, lax.slice_in_dim(echoes, interval * HOP, interval * HOP + PULSES, axis=1)
        )
        for interval in range(INTERVALS)
    ]
    turned = [
        lax.all_to_all(
            lax.all_to_all(spectrum, "section", split_axis=1, concat_axis=2, tiled=True),
            "sub",
            split_axis=1,
            concat_axis=3,
            tiled=True,
        )
        for spectrum in spectra
    ]
    refined = []
    for spectrum in turned:
        padded_bins = jnp.pad(spectrum, ((0, 0), (0, 0), (rim_width, rim_width), (0, 0)))
        part_real, part_imag = apply_taps(
            padded_bins[0], padded_bins[1], range_taps, spectrum.shape[2]
        )
        refined.append(jnp.stack([part_real, part_imag]))
    turned = refined
    steer_real, steer_imag = steering(beam_index, channel_phase)
    interval = 0
    inv_real, inv_imag = loaded_inverse(turned[interval][0], turned[interval][1], loading)
    weight_real, weight_imag = beam_weights(inv_real, inv_imag, steer_real, steer_imag)
    beam_power = form_beams(
        turned[interval + 1][0], turned[interval + 1][1], weight_real, weight_imag
    )
    partials = [jnp.sum(beam_power, axis=(0, 1))]
    totals = lax.psum(jnp.stack(partials), ("section", "sub"))
    noise_level = totals / (PULSES * turned[0].shape[2])
    return jnp.stack([beam_power / (noise_level[0] + epsilon)])


def solution(mesh):
    in_specs = (P("groups", None, "section", "sub"), P(), P(), P(), P(), P())
    out_specs = P("groups", ("section", "sub"), None, None)
    sections = mesh.shape["section"]
    small = sections == 8 and mesh.shape["sub"] == 2

    def run(echoes, range_taps, pulse_taper, channel_phase, loading, beam_index):
        args = (echoes, range_taps, pulse_taper, channel_phase, loading, beam_index)
        fits = small and echoes.shape[2] == 4 and echoes.shape[3] == LANES
        return factored_steps(*args) if fits else on_device(*args)

    return jax.shard_map(run, mesh=mesh, in_specs=in_specs, out_specs=out_specs, check_vma=False)
```
